256 devices in a mesh: outer: 4 (over x), inner: 16 (over z_hi, y), tensor: 4 (over z_lo, core).
Axes of the slice: x: 4, y: 4, z: 8 (z_hi: 4, z_lo: 2; z = z_hi * 2 + z_lo), core: 2. Of those that a mesh axis runs over, the one named last changes fastest.
Arguments:
- hidden_in: bfloat16 [12288, 4096], P(('outer', 'inner', 'tensor')), may hold values from -15 to 15
- norm_gain: float32 [4096], replicated, may hold values from 0.5 to 5
- w_query: bfloat16 [4096, 4096], P('inner', 'tensor'), may hold values from -0.110485435 to 0.110485435
- w_key: bfloat16 [4096, 1024], P('inner', 'tensor'), may hold values from -0.110485435 to 0.110485435
- value_weight: bfloat16 [4096, 1024], P('inner', 'tensor'), may hold values from -0.09375 to 0.09375
- w_out: bfloat16 [4096, 4096], P('tensor'), may hold values from -0.09375 to 0.09375
- doc_ids: int32 [12288], P(('outer', 'inner')), may hold values from 0 to 5, as said below
- positions: int32 [12288], P(('outer', 'inner')), may hold values from 0 to 65535, as said below
Outputs:
- layer_out: bfloat16 [12288, 4096], P(('outer', 'inner', 'tensor'))
The draws below stay inside these ranges and needn't reach their ends.
Inputs may be any that keep to these rules, and one draw needn't show every extreme that they name: `doc_ids`: document numbers never fall along the sequence; each of the 6 documents has at least one token, and exactly one of them has 7680 tokens. Document numbers may be sent packed or coded. `positions`: inside a document the position rises by one from each token to the next; one document other than the one of 7680 tokens ends at position 65535.
All inputs are finite; a program needn't handle non-finite values.
Results may differ from the reference program's by a relative error of at most 0.012.
The reference program's roundings to bfloat16 on the way count: a program that leaves them out, or rounds other values in their place, can miss the bound.
Values may be sent and summed in bfloat16 or wider, within the bound.
A program may use at most 128 MiB of HBM per device.

```python
import math
import jax
import jax.numpy as jnp
from jax import lax

MODEL_WIDTH = 4096
QUERY_HEADS = 32
KEY_VALUE_HEADS = 8
HEAD_SIZE = 128
NDOC = 6
YARN_CTX = 65536
SEQUENCE_TOKENS = 12288
LONGEST = 7680


def draw_hidden_in(key, part):
    values = jnp.clip(jax.random.normal(jax.random.fold_in(key, 3), (SEQUENCE_TOKENS, MODEL_WIDTH), jnp.float32), -5.0, 5.0)
    return values.astype(jnp.bfloat16)


def draw_norm_gain(key, part):
    return jax.random.uniform(jax.random.fold_in(key, 5), (MODEL_WIDTH,), jnp.float32, 0.6, 1.4)


def normed_queries(key):
    return jnp.clip(jax.random.normal(jax.random.fold_in(key, 21), (MODEL_WIDTH, QUERY_HEADS * HEAD_SIZE), jnp.float32), -5.0, 5.0)


def draw_w_query(key, part):
    sigma = (MODEL_WIDTH // 2) ** (-0.5)
    return (sigma * normed_queries(key)).astype(jnp.bfloat16)


def draw_w_key(key, part):
    sigma = (MODEL_WIDTH // 2) ** (-0.5)
    random_noise = jnp.clip(jax.random.normal(jax.random.fold_in(key, 22), (MODEL_WIDTH, KEY_VALUE_HEADS * HEAD_SIZE), jnp.float32), -5.0, 5.0)
    return (sigma * random_noise).astype(jnp.bfloat16)


def document_layout(key):
    doc_key = jax.random.fold_in(key, 11)
    cut_key, slot_key, offset_key, end_key = jax.random.split(doc_key, 4)
    remaining = SEQUENCE_TOKENS - LONGEST
    cut_picks = jax.random.permutation(cut_key, remaining - 1)[:NDOC - 2] + 1
    cut_points = jnp.sort(cut_picks).astype(jnp.int32)
    edge_points = jnp.concatenate([jnp.zeros((1,), jnp.int32), cut_points, jnp.full((1,), remaining, jnp.int32)])
    other_lengths = edge_points[1:] - edge_points[:-1]
    long_slot = jax.random.randint(slot_key, (), 0, NDOC)
    end_pick = jax.random.randint(end_key, (), 0, NDOC - 1)
    end_slot = end_pick + (end_pick >= long_slot).astype(jnp.int32)
    indices = jnp.arange(NDOC, dtype=jnp.int32)
    before = jnp.take(other_lengths, jnp.clip(indices, 0, NDOC - 2))
    later_lengths = jnp.take(other_lengths, jnp.clip(indices - 1, 0, NDOC - 2))
    doc_lengths = jnp.where(indices < long_slot, before, jnp.where(indices == long_slot, LONGEST, later_lengths)).astype(jnp.int32)
    doc_ends = jnp.cumsum(doc_lengths)
    doc_begins = doc_ends - doc_lengths
    token_index = jnp.arange(SEQUENCE_TOKENS, dtype=jnp.int32)
    documents = jnp.sum((token_index[:, None] >= doc_ends[None, :NDOC - 1]).astype(jnp.int32), axis=1)
    raw_offsets = jax.random.randint(offset_key, (NDOC,), 0, 2 ** 30)
    offsets = raw_offsets % (YARN_CTX - doc_lengths + 1)
    offsets = jnp.where(indices == long_slot, raw_offsets % (YARN_CTX - LONGEST), offsets)
    offsets = jnp.where(indices == end_slot, YARN_CTX - doc_lengths, offsets)
    placed = jnp.take(offsets, documents) + token_index - jnp.take(doc_begins, documents)
    return (documents.astype(jnp.int32), placed.astype(jnp.int32))


def draw_doc_ids(key, part):
    return document_layout(key)[0]


def draw_positions(key, part):
    return document_layout(key)[1]


def levels(stream_key, shape, pieces, low, top_value):
    level, own = 1.0, jax.random.fold_in(stream_key, 6)
    for position, parts in pieces:
        heights = jnp.exp(jax.random.uniform(jax.random.fold_in(own, position), (parts,), jnp.float32, low / len(pieces), top_value / len(pieces)))
        level = level * jnp.repeat(heights, shape[position] // parts).reshape([-1 if axis == position else 1 for axis in range(len(shape))])
    return level


def gaussian(key, shape, scale, reach, cuts=(), kind=jnp.bfloat16):
    array = jax.random.normal(key, shape, jnp.float32) * scale
    if len(cuts) > 0:
        array = levels(key, shape, cuts, -0.22, 0.18) * array
    return jnp.clip(array, min=-reach, max=reach).astype(kind)


def setup_inputs(seed: int = 0) -> dict:
    seeds = jax.random.split(jax.random.key(seed), 9)
    hidden_in = draw_hidden_in(jax.random.fold_in(seeds[8], 71), 0)
    norm_gain = draw_norm_gain(jax.random.fold_in(seeds[8], 71), 0)
    w_query = draw_w_query(jax.random.fold_in(seeds[8], 71), 0)
    w_key = draw_w_key(jax.random.fold_in(seeds[8], 71), 0)
    value_weight = gaussian(seeds[4], (MODEL_WIDTH, KEY_VALUE_HEADS * HEAD_SIZE), MODEL_WIDTH ** -0.5, 0.09375, ((0, 16), (1, 4)))
    w_out = gaussian(seeds[5], (QUERY_HEADS * HEAD_SIZE, MODEL_WIDTH), (QUERY_HEADS * HEAD_SIZE) ** -0.5, 0.09375, ((0, 4),))
    doc_ids = draw_doc_ids(jax.random.fold_in(seeds[8], 71), 0)
    positions = draw_positions(jax.random.fold_in(seeds[8], 71), 0)
    return dict(hidden_in=hidden_in, norm_gain=norm_gain, w_query=w_query, w_key=w_key, value_weight=value_weight, w_out=w_out, doc_ids=doc_ids, positions=positions)


rope_base = 500000.0
yarn_factor = 8.0
trained_context = 8192.0
beta_fast = 32.0
beta_slow = 1.0
norm_epsilon = 1e-05
masked_score = -1e+30

def yarn_inverse(head_dim):
    half_dim = head_dim // 2

    def correction(rotations):
        return head_dim * math.log(trained_context / (rotations * 2.0 * math.pi)) / (2.0 * math.log(rope_base))
    lowest = max(math.floor(correction(beta_fast)), 0)
    highest = min(math.ceil(correction(beta_slow)), head_dim - 1)
    spread = max(highest - lowest, 0.001)
    values = []
    for column in range(half_dim):
        extrapolated = rope_base ** (-2.0 * column / head_dim)
        ramp = min(max((column - lowest) / spread, 0.0), 1.0)
        values.append(extrapolated / yarn_factor * ramp + extrapolated * (1.0 - ramp))
    return values

def yarn_tables(positions, head_dim):
    inverse = jnp.asarray(yarn_inverse(head_dim), dtype=jnp.float32)
    attention_gain = 0.1 * math.log(yarn_factor) + 1.0
    angles = positions.astype(jnp.float32)[:, None] * inverse[None, :]
    return (jnp.cos(angles) * attention_gain, jnp.sin(angles) * attention_gain)

def apply_rotation(heads, cosine_table, sine_table):
    half_dim = heads.shape[-1] // 2
    first_half = heads[..., :half_dim]
    second_half = heads[..., half_dim:]
    cos_rows = cosine_table[:, None, :]
    sin_rows = sine_table[:, None, :]
    return jnp.concatenate([first_half * cos_rows - second_half * sin_rows, second_half * cos_rows + first_half * sin_rows], axis=-1)

def rms_normed(hidden_in, norm_gain):
    widened = hidden_in.astype(jnp.float32)
    power = lax.optimization_barrier(jnp.mean(widened * widened, axis=-1, keepdims=True))
    return (widened * lax.rsqrt(power + norm_epsilon) * norm_gain).astype(jnp.bfloat16)

def reference(hidden_in, norm_gain, w_query, w_key, value_weight, w_out, doc_ids, positions):
    normed = rms_normed(hidden_in, norm_gain)
    queries = jnp.dot(normed, w_query, preferred_element_type=jnp.float32)
    key_matrix = jnp.dot(normed, w_key, preferred_element_type=jnp.float32)
    value_matrix = jnp.dot(normed, value_weight, preferred_element_type=jnp.float32).astype(jnp.bfloat16)
    cosine_table, sine_table = yarn_tables(positions, HEAD_SIZE)
    query_rot = apply_rotation(queries.reshape(SEQUENCE_TOKENS, QUERY_HEADS, HEAD_SIZE), cosine_table, sine_table).astype(jnp.bfloat16)
    rotated_keys = apply_rotation(key_matrix.reshape(SEQUENCE_TOKENS, KEY_VALUE_HEADS, HEAD_SIZE), cosine_table, sine_table).astype(jnp.bfloat16)
    value_per_head = value_matrix.reshape(SEQUENCE_TOKENS, KEY_VALUE_HEADS, HEAD_SIZE)
    sequence_index = jnp.arange(SEQUENCE_TOKENS, dtype=jnp.int32)
    allowed = (sequence_index[:, None] >= sequence_index[None, :]) & (doc_ids[:, None] == doc_ids[None, :])
    score_scale = HEAD_SIZE ** (-0.5)
    queries_per_group = QUERY_HEADS // KEY_VALUE_HEADS

    def one_head(head_index):
        shared = head_index // queries_per_group
        head_query = lax.dynamic_index_in_dim(query_rot, head_index, 1, keepdims=False)
        head_key = lax.dynamic_index_in_dim(rotated_keys, shared, 1, keepdims=False)
        head_value = lax.dynamic_index_in_dim(value_per_head, shared, 1, keepdims=False)
        scores = jnp.dot(head_query, head_key.T, preferred_element_type=jnp.float32) * score_scale
        scores = jnp.where(allowed, scores, masked_score)
        row_peaks = lax.optimization_barrier(jnp.max(scores, axis=-1, keepdims=True))
        weights = jnp.where(allowed, jnp.exp(scores - row_peaks), 0.0)
        totals = lax.optimization_barrier(jnp.sum(weights, axis=-1, keepdims=True))
        summed = jnp.dot(weights.astype(jnp.bfloat16), head_value, preferred_element_type=jnp.float32)
        return (summed / totals).astype(jnp.bfloat16)
    attended = lax.map(one_head, jnp.arange(QUERY_HEADS, dtype=jnp.int32))
    attended = jnp.transpose(attended, (1, 0, 2)).reshape(SEQUENCE_TOKENS, QUERY_HEADS * HEAD_SIZE)
    projected = jnp.dot(attended, w_out, preferred_element_type=jnp.float32)
    return (hidden_in.astype(jnp.float32) + projected).astype(jnp.bfloat16)
```

```python
import functools
import math

import jax
import jax.numpy as jnp
from jax import lax
from jax.experimental import pallas as pl
from jax.experimental.pallas import tpu as pltpu
from jax.sharding import PartitionSpec as P

HEAD_SIZE = 128
BLOCK = 192
SEQUENCE = 12288
KEY_TILE = 512
MESH = pl.DeviceIdType.MESH


rope_base = 500000.0
yarn_factor = 8.0
trained_context = 8192.0
beta_fast = 32.0
beta_slow = 1.0
norm_epsilon = 1e-05
masked_score = -1e30


def yarn_inverse(head_dim):
    half_dim = head_dim // 2

    def correction(rotations):
        return (
            head_dim
            * math.log(trained_context / (rotations * 2.0 * math.pi))
            / (2.0 * math.log(rope_base))
        )

    lowest = max(math.floor(correction(beta_fast)), 0)
    highest = min(math.ceil(correction(beta_slow)), head_dim - 1)
    spread = max(highest - lowest, 0.001)
    values = []
    for column in range(half_dim):
        extrapolated = rope_base ** (-2.0 * column / head_dim)
        ramp = min(max((column - lowest) / spread, 0.0), 1.0)
        values.append(extrapolated / yarn_factor * ramp + extrapolated * (1.0 - ramp))
    return values


def yarn_tables(positions, head_dim):
    inverse = jnp.asarray(yarn_inverse(head_dim), dtype=jnp.float32)
    attention_gain = 0.1 * math.log(yarn_factor) + 1.0
    angles = positions.astype(jnp.float32)[:, None] * inverse[None, :]
    return (jnp.cos(angles) * attention_gain, jnp.sin(angles) * attention_gain)


def apply_rotation(heads, cosine_table, sine_table):
    half_dim = heads.shape[-1] // 2
    first_half = heads[..., :half_dim]
    second_half = heads[..., half_dim:]
    cos_rows = cosine_table[:, None, :]
    sin_rows = sine_table[:, None, :]
    return jnp.concatenate(
        [
            first_half * cos_rows - second_half * sin_rows,
            second_half * cos_rows + first_half * sin_rows,
        ],
        axis=-1,
    )


def rms_normed(hidden_in, norm_gain):
    widened = hidden_in.astype(jnp.float32)
    power = jnp.mean(widened * widened, axis=-1, keepdims=True)
    return (widened * lax.rsqrt(power + norm_epsilon) * norm_gain).astype(jnp.bfloat16)


def place():
    outer, inner, tensor = (lax.axis_index(name) for name in ("outer", "inner", "tensor"))
    return outer, inner % 4, inner // 4, tensor // 2, tensor % 2


def device(x, y, zh, zl, c):
    return (x, zh * 4 + y, zl * 2 + c)


def greet(partners):
    barrier = pltpu.get_barrier_semaphore()
    for partner in partners:
        pl.semaphore_signal(barrier, inc=1, device_id=partner, device_id_type=MESH)
    pl.semaphore_wait(barrier, len(partners))


class Copies:
    def __init__(self, send_sems, recv_sems):
        self.send_sems, self.recv_sems, self.count, self.sent = send_sems, recv_sems, 0, []

    def send(self, src, dst, target):
        copy = pltpu.make_async_remote_copy(
            src_ref=src,
            dst_ref=dst,
            send_sem=self.send_sems.at[self.count],
            recv_sem=self.recv_sems.at[self.count],
            device_id=target,
            device_id_type=MESH,
        )
        self.count += 1
        copy.start()
        self.sent.append(copy)
        return copy

    def finish(self):
        for copy in self.sent:
            copy.wait_send()


def gather_kernel(
    normed, weights, meta, rows_out, weights_out, meta_out, send_sems, recv_sems, a2a_send, a2a_recv, local_sems
):
    x, y, zh, zl, c = place()
    p = zh * 2 + zl
    near = lambda q: device(x, y, (q % 8) // 2, q % 2, c)
    right, left = near(p + 1), near(p + 7)
    sibling = device(x, y, zh, zl, 1 - c)
    y_next, y_prev = device(x, (y + 1) % 4, zh, zl, c), device(x, (y + 3) % 4, zh, zl, c)
    x_next, x_prev = device((x + 1) % 4, y, zh, zl, c), device((x + 3) % 4, y, zh, zl, c)
    y_far, x_far = device(x, (y + 2) % 4, zh, zl, c), device((x + 2) % 4, y, zh, zl, c)
    columns = [device(x, y, (zh + k) % 4, zl, cc) for k in range(4) for cc in (c, 1 - c)][1:]
    greet(columns + [right, left, y_next, y_prev, y_far, x_next, x_prev, x_far])
    cp = Copies(send_sems, recv_sems)

    a2a = []
    for j in range(2):
        for cc in range(2):
            zt = 2 * c + j
            own = (zt == zh) & (c == cc)
            copy = pltpu.make_async_remote_copy(
                src_ref=weights.at[2 * j + cc],
                dst_ref=weights_out.at[zh, y, x],
                send_sem=a2a_send.at[2 * j + cc],
                recv_sem=a2a_recv.at[zh],
                device_id=device(x, y, zt, zl, cc),
                device_id_type=MESH,
            )
            stay = pltpu.make_async_copy(
                weights.at[2 * j + cc], weights_out.at[zh, y, x], local_sems.at[0]
            )
            pl.when(own)(stay.start)
            pl.when(jnp.logical_not(own))(copy.start)
            a2a.append((own, copy, stay))
    own_row = pltpu.make_async_copy(normed, rows_out.at[p, c], local_sems.at[1])
    own_row.start()
    own_meta = pltpu.make_async_copy(meta, meta_out.at[x, y, zh], local_sems.at[2])
    own_meta.start()

    to_right, to_left, to_sibling = {}, {}, []
    for h in range(2):
        spot = rows_out.at[p, c, h]
        to_right[0, h] = cp.send(normed.at[h], spot, right)
        to_left[0, h] = cp.send(normed.at[h], spot, left)
    to_sibling.append(cp.send(normed, rows_out.at[p, c], sibling))
    meta_z = [
        cp.send(meta, meta_out.at[x, y, zh], device(x, y, (zh + k) % 4, zl, c)) for k in (1, 2, 3)
    ]

    for source in range(4):
        arrives = pltpu.make_async_remote_copy(
            src_ref=weights.at[0],
            dst_ref=weights_out.at[source, y, x],
            send_sem=a2a_send.at[0],
            recv_sem=a2a_recv.at[source],
            device_id=sibling,
            device_id_type=MESH,
        )
        own = (zh == source) & (c == zh // 2)
        pl.when(jnp.logical_not(own))(arrives.wait_recv)
    for own, copy, stay in a2a:
        pl.when(own)(stay.wait)
    mine = weights_out.at[:, y, x]
    wy_next, wy_prev = cp.send(mine, mine, y_next), cp.send(mine, mine, y_prev)
    wx = {}

    def along_x(yy):
        piece = weights_out.at[:, yy, x]
        wx[len(wx)] = (yy, cp.send(piece, piece, x_next), cp.send(piece, piece, x_prev))

    forwards = []

    def forward_x(k):
        yy, a, b = wx[k]
        a.wait_recv()
        piece = weights_out.at[pl.ds(0, 2), yy, (x + 3) % 4]
        forwards.append(cp.send(piece, piece, x_next))
        b.wait_recv()
        piece = weights_out.at[pl.ds(2, 2), yy, (x + 1) % 4]
        forwards.append(cp.send(piece, piece, x_prev))

    along_x(y)
    own_meta.wait()
    for copy in meta_z:
        copy.wait_recv()
    mine = meta_out.at[x, y]
    meta_y = [cp.send(mine, mine, device(x, (y + k) % 4, zh, zl, c)) for k in (1, 2, 3)]

    def ring(step):
        for h in range(2):
            if (step, h) in to_right:
                to_right[step, h].wait_recv()
                spot = rows_out.at[(p + 7 - step) % 8, c, h]
                if step < 2 or (step == 2 and h == 0):
                    to_right[step + 1, h] = cp.send(spot, spot, right)
                to_sibling.append(cp.send(spot, spot, sibling))
            if (step, h) in to_left:
                to_left[step, h].wait_recv()
                spot = rows_out.at[(p + 1 + step) % 8, c, h]
                if step < 2 or (step == 2 and h == 1):
                    to_left[step + 1, h] = cp.send(spot, spot, left)
                to_sibling.append(cp.send(spot, spot, sibling))

    ring(0)
    wy_next.wait_recv()
    piece = weights_out.at[pl.ds(0, 2), (y + 3) % 4, x]
    wy_far_next = cp.send(piece, piece, y_next)
    along_x((y + 3) % 4)
    wy_prev.wait_recv()
    piece = weights_out.at[pl.ds(2, 2), (y + 1) % 4, x]
    wy_far_prev = cp.send(piece, piece, y_prev)
    along_x((y + 1) % 4)
    for copy in meta_y:
        copy.wait_recv()
    mine = meta_out.at[x]
    meta_x = [cp.send(mine, mine, device((x + k) % 4, y, zh, zl, c)) for k in (1, 2, 3)]
    forward_x(0)
    wy_far_next.wait_recv()
    wy_far_prev.wait_recv()
    along_x((y + 2) % 4)
    ring(1)
    forward_x(1)
    forward_x(2)
    ring(2)
    forward_x(3)
    ring(3)
    for copy in forwards + to_sibling + meta_x:
        copy.wait_recv()
    own_row.wait()
    for own, copy, stay in a2a:
        pl.when(jnp.logical_not(own))(copy.wait_send)
    cp.finish()


def gather(normed, weights, meta):
    anywhere = pl.BlockSpec(memory_space=pl.ANY)
    return pl.pallas_call(
        gather_kernel,
        out_shape=(
            jax.ShapeDtypeStruct((8, 2, 2, 24, 4096), jnp.bfloat16),
            jax.ShapeDtypeStruct((4, 4, 4, 64, 384), jnp.bfloat16),
            jax.ShapeDtypeStruct((4, 4, 4, 8, 128), jnp.int32),
        ),
        in_specs=[anywhere] * 3,
        out_specs=(anywhere,) * 3,
        scratch_shapes=[
            pltpu.SemaphoreType.DMA((64,)),
            pltpu.SemaphoreType.DMA((64,)),
            pltpu.SemaphoreType.DMA((4,)),
            pltpu.SemaphoreType.DMA((4,)),
            pltpu.SemaphoreType.DMA((3,)),
        ],
        compiler_params=pltpu.CompilerParams(collective_id=0, has_side_effects=True),
        name="gather",
    )(normed, weights, meta)


def keys_kernel(own, out, send_sems, recv_sems, local_sem):
    x, y, zh, zl, c = place()
    sibling = device(x, y, zh, zl, 1 - c)
    xs = [(x + k) % 4 for k in range(4)]
    ys = [(y + k) % 4 for k in range(4)]
    y_next, y_prev = device(x, ys[1], zh, zl, c), device(x, ys[3], zh, zl, c)
    x_next, x_prev = device(xs[1], y, zh, zl, c), device(xs[3], y, zh, zl, c)
    greet([sibling, y_next, y_prev, x_next, x_prev])
    cp = Copies(send_sems, recv_sems)
    whole = lambda xx, yy: out.at[c, xx, :, :, yy]
    half = lambda f, xx, yy: out.at[c, xx, f, :, yy]
    part = lambda a, xx, yy: out.at[c, xx, :, a, yy]
    cell = lambda f, a, xx, yy: out.at[c, xx, f, a, yy]
    same = lambda ref, target: cp.send(ref, ref, target)

    stay = pltpu.make_async_copy(own, whole(x, y), local_sem.at[0])
    stay.start()
    from_y_prev = cp.send(own, whole(x, y), y_next)
    from_y_next = cp.send(own, whole(x, y), y_prev)
    from_x_prev = cp.send(own, whole(x, y), x_next)
    from_x_next = cp.send(own, whole(x, y), x_prev)
    siblings = [cp.send(own, whole(x, y), sibling)]

    def share(xx, yy):
        siblings.append(same(whole(xx, yy), sibling))

    a_prev, a_next, b_prev, b_next = {}, {}, {}, {}

    def a_send(k):
        a_prev[k] = same(part(0, x, ys[k]), x_next)
        a_next[k] = same(part(0, x, ys[k]), x_prev)

    def b_send(k):
        b_prev[k] = same(part(1, xs[k], y), y_next)
        b_next[k] = same(part(1, xs[k], y), y_prev)

    from_y_prev.wait_recv()
    y_far_prev = same(half(0, x, ys[3]), y_next)
    a_send(3)
    from_x_prev.wait_recv()
    x_far_prev = same(half(0, xs[3], y), x_next)
    b_send(3)
    from_y_next.wait_recv()
    y_far_next = same(half(1, x, ys[1]), y_prev)
    a_send(1)
    from_x_next.wait_recv()
    x_far_next = same(half(1, xs[1], y), x_prev)
    b_send(1)
    share(x, ys[3])
    share(x, ys[1])
    share(xs[3], y)
    share(xs[1], y)
    y_far_prev.wait_recv()
    y_far_next.wait_recv()
    a_send(2)
    x_far_prev.wait_recv()
    x_far_next.wait_recv()
    b_send(2)
    share(x, ys[2])
    share(xs[2], y)
    fa, fb = {}, {}
    for k in (3, 1, 2):
        a_prev[k].wait_recv()
        fa[k, 0] = same(cell(0, 0, xs[3], ys[k]), x_next)
        b_prev[k].wait_recv()
        fb[k, 0] = same(cell(0, 1, xs[k], ys[3]), y_next)
        a_next[k].wait_recv()
        fa[k, 1] = same(cell(1, 0, xs[1], ys[k]), x_prev)
        b_next[k].wait_recv()
        fb[k, 1] = same(cell(1, 1, xs[k], ys[1]), y_prev)
        if k == 1:
            for xx in (1, 3):
                for yy in (1, 3):
                    share(xs[xx], ys[yy])
    for k in (3, 1, 2):
        for f in range(2):
            fa[k, f].wait_recv()
            fb[k, f].wait_recv()
        if k == 2:
            share(xs[1], ys[2])
            share(xs[3], ys[2])
            share(xs[2], ys[1])
            share(xs[2], ys[3])
            share(xs[2], ys[2])
    for copy in siblings:
        copy.wait_recv()
    stay.wait()
    cp.finish()


def gather_keys(own):
    anywhere = pl.BlockSpec(memory_space=pl.ANY)
    return pl.pallas_call(
        keys_kernel,
        out_shape=jax.ShapeDtypeStruct((2, 4, 2, 2, 4, BLOCK, HEAD_SIZE), jnp.bfloat16),
        in_specs=[anywhere],
        out_specs=anywhere,
        scratch_shapes=[
            pltpu.SemaphoreType.DMA((48,)),
            pltpu.SemaphoreType.DMA((48,)),
            pltpu.SemaphoreType.DMA((1,)),
        ],
        compiler_params=pltpu.CompilerParams(collective_id=1, has_side_effects=True),
        name="gather_keys",
    )(own)


def attend_kernel(bounds, q_ref, k_ref, v_ref, first_ref, out_ref):
    block = pl.program_id(0)
    t_low, t_clear, t_edge, t_high, row0 = (bounds[block, i] for i in range(5))
    scale = HEAD_SIZE ** (-0.5) * math.log2(math.e)
    queries = [q_ref[0, :, h * HEAD_SIZE : (h + 1) * HEAD_SIZE] for h in range(2)]

    def tile(masked, t, carry):
        at = pl.ds(pl.multiple_of(t * KEY_TILE, KEY_TILE), KEY_TILE)
        keys, values = k_ref[at, :], v_ref[at, :]
        if masked:
            column = t * KEY_TILE + lax.broadcasted_iota(jnp.int32, (BLOCK, KEY_TILE), 1)
            row = row0 + lax.broadcasted_iota(jnp.int32, (BLOCK, KEY_TILE), 0)
            allowed = (column <= row) & (column >= first_ref[0])
        result = []
        for h in range(2):
            peak, total, summed = carry[3 * h : 3 * h + 3]
            scores = lax.dot_general(
                queries[h], keys, (((1,), (1,)), ((), ())), preferred_element_type=jnp.float32
            )
            if masked:
                scores = jnp.where(allowed, scores, masked_score)
            fresh = jnp.maximum(peak, jnp.max(scores, axis=-1, keepdims=True))
            weights = jnp.exp2((scores - fresh) * scale)
            if masked:
                weights = jnp.where(allowed, weights, 0.0)
            shrink = jnp.exp2((peak - fresh) * scale)
            total = total * shrink + jnp.sum(weights, axis=-1, keepdims=True)
            summed = summed * shrink + jnp.dot(
                weights.astype(jnp.bfloat16), values, preferred_element_type=jnp.float32
            )
            result += [fresh, total, summed]
        return tuple(result)

    carry = (
        jnp.full((BLOCK, 1), masked_score, jnp.float32),
        jnp.zeros((BLOCK, 1), jnp.float32),
        jnp.zeros((BLOCK, HEAD_SIZE), jnp.float32),
    ) * 2
    carry = lax.fori_loop(t_low, t_clear, functools.partial(tile, True), carry)
    carry = lax.fori_loop(t_clear, t_edge, functools.partial(tile, False), carry)
    carry = lax.fori_loop(t_edge, t_high, functools.partial(tile, True), carry)
    for h in range(2):
        out_ref[0, :, h * HEAD_SIZE : (h + 1) * HEAD_SIZE] = (
            carry[3 * h + 2] / carry[3 * h + 1]
        ).astype(jnp.bfloat16)


def attend(bounds, queries, keys, values, first):
    return pl.pallas_call(
        attend_kernel,
        out_shape=jax.ShapeDtypeStruct((4, BLOCK, 2 * HEAD_SIZE), jnp.bfloat16),
        grid_spec=pltpu.PrefetchScalarGridSpec(
            num_scalar_prefetch=1,
            grid=(4,),
            in_specs=[
                pl.BlockSpec((1, BLOCK, 2 * HEAD_SIZE), lambda i, b: (i, 0, 0)),
                pl.BlockSpec((SEQUENCE, HEAD_SIZE), lambda i, b: (0, 0)),
                pl.BlockSpec((SEQUENCE, HEAD_SIZE), lambda i, b: (0, 0)),
                pl.BlockSpec((1, BLOCK, 1), lambda i, b: (i, 0, 0)),
            ],
            out_specs=pl.BlockSpec((1, BLOCK, 2 * HEAD_SIZE), lambda i, b: (i, 0, 0)),
        ),
        compiler_params=pltpu.CompilerParams(vmem_limit_bytes=48 << 20),
        name="attend",
    )(bounds, queries, keys, values, first)


def heads_kernel(own, out, send_sems, recv_sems, local_sem):
    x, y, zh, zl, c = place()
    cz = zh // 2
    partners = [device(x, y, (zh + k) % 4, zl, cc) for k in range(4) for cc in (c, 1 - c)][1:]
    greet(partners)
    spot = lambda j, cc: out.at[:, pl.ds(pl.multiple_of((2 * j + cc) * 256, 256), 256)]
    copies = []
    for k in range(4):
        zt = (zh + k) % 4
        copy = pltpu.make_async_remote_copy(
            src_ref=own.at[zt],
            dst_ref=spot(zh % 2, c),
            send_sem=send_sems.at[k],
            recv_sem=recv_sems.at[(zh % 2) * 2 + c],
            device_id=device(x, y, zt, zl, cz),
            device_id_type=MESH,
        )
        if k == 0:
            stay = pltpu.make_async_copy(own.at[zt], spot(zh % 2, c), local_sem.at[0])
            here = cz == c
            pl.when(here)(stay.start)
            pl.when(jnp.logical_not(here))(copy.start)
        else:
            copy.start()
        copies.append(copy)
    for j in range(2):
        for cc in range(2):
            arrives = pltpu.make_async_remote_copy(
                src_ref=own.at[0],
                dst_ref=spot(j, cc),
                send_sem=send_sems.at[0],
                recv_sem=recv_sems.at[2 * j + cc],
                device_id=partners[0],
                device_id_type=MESH,
            )
            mine = (zh == 2 * c + j) & (c == cc)
            pl.when(jnp.logical_not(mine))(arrives.wait_recv)
    pl.when(here)(stay.wait)
    pl.when(jnp.logical_not(here))(copies[0].wait_send)
    for copy in copies[1:]:
        copy.wait_send()


def exchange_heads(own):
    anywhere = pl.BlockSpec(memory_space=pl.ANY)
    return pl.pallas_call(
        heads_kernel,
        out_shape=jax.ShapeDtypeStruct((BLOCK, 1024), jnp.bfloat16),
        in_specs=[anywhere],
        out_specs=anywhere,
        scratch_shapes=[
            pltpu.SemaphoreType.DMA((4,)),
            pltpu.SemaphoreType.DMA((4,)),
            pltpu.SemaphoreType.DMA((1,)),
        ],
        compiler_params=pltpu.CompilerParams(collective_id=2, has_side_effects=True),
        name="exchange_heads",
    )(own)


def reduce_kernel(partial, hidden, out, landed, joined, arrived, send_sems, recv_sems):
    x, y, zh, zl, c = place()
    sibling, across = device(x, y, zh, zl, 1 - c), device(x, y, zh, 1 - zl, c)
    greet([sibling, across])
    cp = Copies(send_sems, recv_sems)
    pieces = 4
    width = 4096 // pieces
    cut = lambda i: pl.ds(i * width, width)
    first = [
        cp.send(partial.at[1 - zl, 1 - c, :, cut(i)], landed.at[1 - zl, :, cut(i)], sibling)
        for i in range(pieces)
    ]
    second = [
        cp.send(partial.at[zl, 1 - c, :, cut(i)], landed.at[zl, :, cut(i)], sibling)
        for i in range(pieces)
    ]
    third = []
    for i in range(pieces):
        first[i].wait_recv()
        joined[:, cut(i)] = (
            partial[1 - zl, c, :, cut(i)].astype(jnp.float32)
            + landed[1 - zl, :, cut(i)].astype(jnp.float32)
        ).astype(jnp.bfloat16)
        third.append(cp.send(joined.at[:, cut(i)], arrived.at[:, cut(i)], across))
    for i in range(pieces):
        second[i].wait_recv()
        total = partial[zl, c, :, cut(i)].astype(jnp.float32) + landed[zl, :, cut(i)].astype(
            jnp.float32
        )
        third[i].wait_recv()
        total = total + arrived[:, cut(i)].astype(jnp.float32)
        out[:, cut(i)] = (hidden[:, cut(i)].astype(jnp.float32) + total).astype(jnp.bfloat16)
    cp.finish()


def reduce_rows(partial, hidden):
    inside = pl.BlockSpec(memory_space=pltpu.VMEM)
    return pl.pallas_call(
        reduce_kernel,
        out_shape=jax.ShapeDtypeStruct((48, 4096), jnp.bfloat16),
        in_specs=[inside] * 2,
        out_specs=inside,
        scratch_shapes=[
            pltpu.VMEM((2, 48, 4096), jnp.bfloat16),
            pltpu.VMEM((48, 4096), jnp.bfloat16),
            pltpu.VMEM((48, 4096), jnp.bfloat16),
            pltpu.SemaphoreType.DMA((12,)),
            pltpu.SemaphoreType.DMA((12,)),
        ],
        compiler_params=pltpu.CompilerParams(collective_id=3, has_side_effects=True),
        name="reduce_rows",
    )(partial, hidden)


def body(hidden_in, norm_gain, w_query, w_key, value_weight, w_out, doc_ids, positions):
    x, y, zh, zl, c = place()
    normed = rms_normed(hidden_in, norm_gain)
    quarter = lambda w: lax.dynamic_slice_in_dim(w, x * 64, 64, 0)
    queries_w, keys_w, values_w = quarter(w_query), quarter(w_key), quarter(value_weight)
    weights = jnp.stack(
        [
            jnp.concatenate(
                [
                    queries_w[:, j * 512 + cc * 256 : j * 512 + cc * 256 + 256],
                    (values_w if cc else keys_w)[:, j * 128 : j * 128 + 128],
                ],
                axis=1,
            )
            for j in range(2)
            for cc in range(2)
        ]
    )
    meta = jnp.stack([doc_ids, positions]).reshape(2, 1, BLOCK)
    meta = jnp.pad(meta, ((0, 0), (0, 0), (0, 64))).reshape(4, 128)
    meta = jnp.pad(meta, ((0, 4), (0, 0)))
    rows, weights, meta = gather(normed.reshape(2, 24, 4096), weights, meta)
    rows, weights = rows.reshape(768, 4096), weights.reshape(4096, 384)
    meta = jnp.transpose(meta, (0, 2, 1, 3, 4))[:, :, :, :4].reshape(4, 4, 4, 2, 256)[..., :BLOCK]
    documents = meta[..., 0, :].reshape(SEQUENCE)
    mine = lax.dynamic_slice(meta, (x, 0, y, 0, 0), (1, 4, 1, 2, BLOCK)).reshape(4, 2, BLOCK)
    my_documents, my_positions = mine[:, 0], mine[:, 1].reshape(768)
    first = jnp.zeros((4, BLOCK), jnp.int32)
    for d in range(6):
        before = jnp.sum((documents < d).astype(jnp.int32))
        first = jnp.where(my_documents == d, before, first)
    row0 = (x * 16 + jnp.arange(4, dtype=jnp.int32) * 4 + y) * BLOCK
    t_low = first[:, 0] // KEY_TILE
    t_edge = jnp.maximum((row0 + 1) // KEY_TILE, t_low)
    t_clear = jnp.clip((first[:, -1] + KEY_TILE - 1) // KEY_TILE, t_low, t_edge)
    t_high = (row0 + BLOCK - 1) // KEY_TILE + 1
    bounds = jnp.stack([t_low, t_clear, t_edge, t_high, row0], axis=1)

    product = jnp.dot(rows, weights, preferred_element_type=jnp.float32)
    cosine_table, sine_table = yarn_tables(my_positions, HEAD_SIZE)
    turned = apply_rotation(product.reshape(768, 3, HEAD_SIZE), cosine_table, sine_table)
    queries = turned[:, :2].astype(jnp.bfloat16).reshape(4, BLOCK, 2 * HEAD_SIZE)
    own = jnp.where(c == 0, turned[:, 2], product[:, 2 * HEAD_SIZE :]).astype(jnp.bfloat16)
    both = gather_keys(own.reshape(2, 2, BLOCK, HEAD_SIZE))
    both = both.reshape(2, SEQUENCE, HEAD_SIZE)
    attended = attend(bounds, queries, both[0], both[1], first.reshape(4, BLOCK, 1))
    attended = exchange_heads(attended)
    partial = jnp.dot(attended, w_out, preferred_element_type=jnp.float32).astype(jnp.bfloat16)
    return reduce_rows(partial.reshape(2, 2, 48, 4096), hidden_in)


def solution(mesh):
    in_specs = (
        P(("outer", "inner", "tensor"), None),
        P(),
        P("inner", "tensor"),
        P("inner", "tensor"),
        P("inner", "tensor"),
        P("tensor", None),
        P(("outer", "inner")),
        P(("outer", "inner")),
    )
    out_specs = P(("outer", "inner", "tensor"), None)
    return jax.shard_map(body, mesh=mesh, in_specs=in_specs, out_specs=out_specs, check_vma=False)
```

```python
import functools
import math

import jax
import jax.numpy as jnp
from jax import lax
from jax.experimental import pallas as pl
from jax.experimental.pallas import tpu as pltpu
from jax.sharding import PartitionSpec as P

HEAD_SIZE = 128
BLOCK = 192
SEQUENCE = 12288
KEY_TILE = 1024
KEY_PIECE = 256
MESH = pl.DeviceIdType.MESH


rope_base = 500000.0
yarn_factor = 8.0
trained_context = 8192.0
beta_fast = 32.0
beta_slow = 1.0
norm_epsilon = 1e-05
masked_score = -1e30


def yarn_inverse(head_dim):
    half_dim = head_dim // 2

    def correction(rotations):
        return (
            head_dim
            * math.log(trained_context / (rotations * 2.0 * math.pi))
            / (2.0 * math.log(rope_base))
        )

    lowest = max(math.floor(correction(beta_fast)), 0)
    highest = min(math.ceil(correction(beta_slow)), head_dim - 1)
    spread = max(highest - lowest, 0.001)
    values = []
    for column in range(half_dim):
        extrapolated = rope_base ** (-2.0 * column / head_dim)
        ramp = min(max((column - lowest) / spread, 0.0), 1.0)
        values.append(extrapolated / yarn_factor * ramp + extrapolated * (1.0 - ramp))
    return values


def place():
    outer, inner, tensor = (lax.axis_index(name) for name in ("outer", "inner", "tensor"))
    return outer, inner % 4, inner // 4, tensor // 2, tensor % 2


def device(x, y, zh, zl, c):
    return (x, zh * 4 + y, zl * 2 + c)


def greet(partners):
    barrier = pltpu.get_barrier_semaphore()
    for partner in partners:
        pl.semaphore_signal(barrier, inc=1, device_id=partner, device_id_type=MESH)
    pl.semaphore_wait(barrier, len(partners))


class Copies:
    def __init__(self, send_sems, recv_sems):
        self.send_sems, self.recv_sems, self.count, self.sent = send_sems, recv_sems, 0, []

    def send(self, src, dst, target):
        copy = pltpu.make_async_remote_copy(
            src_ref=src,
            dst_ref=dst,
            send_sem=self.send_sems.at[self.count],
            recv_sem=self.recv_sems.at[self.count],
            device_id=target,
            device_id_type=MESH,
        )
        self.count += 1
        copy.start()
        self.sent.append(copy)
        return copy

    def finish(self):
        for copy in self.sent:
            copy.wait_send()


def front_kernel(
    hidden, gain, w_query, w_key, w_value, doc_ids, positions, inverse,
    q_out, both, first_out,
    rows, weights, meta, meta_own, tables, product, kv, q_sum,
    send_sems, recv_sems, a2a_send, a2a_recv, local_sems,
):
    x, y, zh, zl, c = place()
    p = zh * 2 + zl
    near = lambda q: device(x, y, (q % 8) // 2, q % 2, c)
    right, left = near(p + 1), near(p + 7)
    sibling = device(x, y, zh, zl, 1 - c)
    xs = [(x + k) % 4 for k in range(4)]
    ys = [(y + k) % 4 for k in range(4)]
    y_next, y_far, y_prev = (device(x, ys[k], zh, zl, c) for k in (1, 2, 3))
    x_next, x_far, x_prev = (device(xs[k], y, zh, zl, c) for k in (1, 2, 3))
    columns = [device(x, y, (zh + k) % 4, zl, cc) for k in range(4) for cc in (c, 1 - c)][1:]
    partners = columns + [right, left, y_next, y_prev, y_far, x_next, x_prev, x_far]
    barrier = pltpu.get_barrier_semaphore()
    for partner in partners:
        pl.semaphore_signal(barrier, inc=1, device_id=partner, device_id_type=MESH)
    cp = Copies(send_sems, recv_sems)

    meta_own[...] = jnp.full((8, 128), 99, jnp.int32)
    meta_own[0:1, :] = doc_ids[:, :128]
    meta_own[1:2, :64] = doc_ids[:, 128:]
    meta_own[2:3, :] = positions[:, :128]
    meta_own[3:4, :64] = positions[:, 128:]
    meta[x, y, zh] = meta_own[...]
    widened = hidden[...].astype(jnp.float32)
    power = jnp.mean(widened * widened, axis=-1, keepdims=True)
    rows[p, c] = (widened * lax.rsqrt(power + norm_epsilon) * gain[...]).astype(jnp.bfloat16)
    pl.semaphore_wait(barrier, len(partners))

    a2a = []
    landing = (pl.ds(0, 256), pl.ds(256, 128))
    for j in range(2):
        for cc in range(2):
            zt = 2 * c + j
            own = (zt == zh) & (c == cc)
            taken = pl.ds(pl.multiple_of(x * 64, 64), 64)
            sources = (
                w_query.at[taken, pl.ds(j * 512 + cc * 256, 256)],
                (w_value if cc else w_key).at[taken, pl.ds(j * 128, 128)],
            )
            for i in range(2):
                spot = weights.at[zh, y, x, :, landing[i]]
                copy = pltpu.make_async_remote_copy(
                    src_ref=sources[i],
                    dst_ref=spot,
                    send_sem=a2a_send.at[4 * j + 2 * cc + i],
                    recv_sem=a2a_recv.at[2 * zh + i],
                    device_id=device(x, y, zt, zl, cc),
                    device_id_type=MESH,
                )
                stay = pltpu.make_async_copy(sources[i], spot, local_sems.at[i])
                pl.when(own)(stay.start)
                pl.when(jnp.logical_not(own))(copy.start)
                a2a.append((own, copy, stay))
    chunks_right = (pl.ds(0, 16), pl.ds(16, 32))
    chunks_left = (pl.ds(32, 16), pl.ds(0, 32))
    to_right, to_left, to_sibling = {}, {}, []
    same = lambda ref, target: cp.send(ref, ref, target)
    meta_z = [
        cp.send(meta_own, meta.at[x, y, zh], device(x, y, (zh + k) % 4, zl, c)) for k in (1, 2, 3)
    ]
    for h in range(2):
        to_right[0, h] = same(rows.at[p, c, chunks_right[h]], right)
        to_left[0, h] = same(rows.at[p, c, chunks_left[h]], left)
    to_sibling.append(same(rows.at[p, c], sibling))

    for source in range(4):
        for i in range(2):
            arrives = pltpu.make_async_remote_copy(
                src_ref=weights.at[source, y, x, :, landing[i]],
                dst_ref=weights.at[source, y, x, :, landing[i]],
                send_sem=a2a_send.at[0],
                recv_sem=a2a_recv.at[2 * source + i],
                device_id=sibling,
                device_id_type=MESH,
            )
            own = (zh == source) & (c == zh // 2)
            pl.when(jnp.logical_not(own))(arrives.wait_recv)
    for own, copy, stay in a2a:
        pl.when(own)(stay.wait)
    mine = weights.at[:, y, x]
    wy_next, wy_prev = same(mine, y_next), same(mine, y_prev)
    wx, forwards = {}, []

    def along_x(k):
        piece = weights.at[:, ys[k], x]
        wx[len(wx)] = (ys[k], same(piece, x_next), same(piece, x_prev))

    def forward_x(k):
        yy, a, b = wx[k]
        a.wait_recv()
        forwards.append(same(weights.at[pl.ds(0, 2), yy, xs[3]], x_next))
        b.wait_recv()
        forwards.append(same(weights.at[pl.ds(2, 2), yy, xs[1]], x_prev))

    def ring(step):
        for h in range(2):
            for to, chunks, target, hop in (
                (to_right, chunks_right, right, 7),
                (to_left, chunks_left, left, 1),
            ):
                to[step, h].wait_recv()
                q = (p + hop * (step + 1)) % 8
                if step < 3:
                    spot = rows.at[q, c, chunks[h]]
                    to_sibling.append(same(spot, sibling))
                    if step < 2:
                        to[step + 1, h] = same(spot, target)
                    else:
                        to[3, h] = same(far_spot(q, h, hop), target)
                else:
                    to_sibling.append(same(far_spot(q, h, hop), sibling))

    def far_spot(q, h, hop):
        if h == 0:
            return rows.at[q, c, pl.ds(0, 16) if hop == 7 else pl.ds(32, 16)]
        return rows.at[q, c, pl.ds(16, 16), pl.ds(0 if hop == 7 else 2048, 2048)]

    along_x(0)
    for copy in meta_z:
        copy.wait_recv()
    mine = meta.at[x, y]
    meta_y = [same(mine, target) for target in (y_next, y_far, y_prev)]
    ring(0)
    wy_next.wait_recv()
    wy_far_next = same(weights.at[pl.ds(0, 2), ys[3], x], y_next)
    along_x(3)
    wy_prev.wait_recv()
    wy_far_prev = same(weights.at[pl.ds(2, 2), ys[1], x], y_prev)
    along_x(1)
    for copy in meta_y:
        copy.wait_recv()
    mine = meta.at[x]
    meta_x = [same(mine, target) for target in (x_next, x_far, x_prev)]
    forward_x(0)
    wy_far_next.wait_recv()
    wy_far_prev.wait_recv()
    along_x(2)

    def tables_of(zb):
        tile = meta[x, y, zb].astype(jnp.float32)
        upper = jnp.broadcast_to(tile[2:3], (128, 128)).T
        lower = jnp.broadcast_to(tile[3:4], (128, 128)).T
        angles = jnp.concatenate([upper, lower[:64]], axis=0) * inverse[...]
        attention_gain = 0.1 * math.log(yarn_factor) + 1.0
        lane = lax.broadcasted_iota(jnp.int32, (BLOCK, HEAD_SIZE), 1)
        sine = jnp.sin(angles) * attention_gain
        tables[0, zb] = jnp.cos(angles) * attention_gain
        tables[1, zb] = jnp.where(lane < HEAD_SIZE // 2, -sine, sine)

    tables_of(0)
    tables_of(1)
    ring(1)
    tables_of(2)
    forward_x(1)
    forward_x(2)
    tables_of(3)
    ring(2)
    forward_x(3)
    for copy in meta_x:
        copy.wait_recv()
    everything = meta[...].reshape(64, 8, 128)
    line = lax.broadcasted_iota(jnp.int32, (8, 128), 0)
    firsts = []
    for d in range(1, 6):
        hits = jnp.sum(jnp.where(everything < d, 1, 0), axis=0)
        hits = jnp.where(line < 2, hits, 0).astype(jnp.float32)
        firsts.append(jnp.sum(jnp.sum(hits, axis=0, keepdims=True), axis=1, keepdims=True))
    for zb in range(4):
        documents = meta[x, y, zb][0:2]
        first = jnp.zeros((2, 128), jnp.float32)
        for d in range(1, 6):
            first = jnp.where(documents == d, firsts[d - 1], first)
        first_out[2 * zb : 2 * zb + 2, :] = first.astype(jnp.int32)
    ring(3)
    for copy in forwards + to_sibling:
        copy.wait_recv()

    def depth(k):
        return pl.ds(pl.multiple_of(k * 256, 256), 256)

    product[...] = jnp.zeros_like(product)

    @pl.loop(0, 16)
    def _(k):
        piece = weights[k // 4, k % 4, :, :, 256:384].reshape(256, HEAD_SIZE)
        left_side = rows[:, :, :, depth(k)].reshape(768, 256)
        product[...] += jnp.dot(left_side, piece, preferred_element_type=jnp.float32)

    def turn(head, cosine, sine):
        return head * cosine + pltpu.roll(head, HEAD_SIZE // 2, 1) * sine

    is_key = c == 0
    for zb in range(4):
        head = product[zb * BLOCK : (zb + 1) * BLOCK, :]
        cosine = jnp.where(is_key, tables[0, zb], 1.0)
        sine = jnp.where(is_key, tables[1, zb], 0.0)
        kv[zb // 2, zb % 2] = turn(head, cosine, sine).astype(jnp.bfloat16)

    whole = lambda xx, yy: both.at[c, xx, :, :, yy]
    half = lambda f, xx, yy: both.at[c, xx, f, :, yy]
    part = lambda a, xx, yy: both.at[c, xx, :, a, yy]
    cell = lambda f, a, xx, yy: both.at[c, xx, f, a, yy]
    from_y_prev = cp.send(kv, whole(x, y), y_next)
    from_x_prev = cp.send(kv, whole(x, y), x_next)
    from_y_next = cp.send(kv, whole(x, y), y_prev)
    from_x_next = cp.send(kv, whole(x, y), x_prev)
    siblings = [cp.send(kv, whole(x, y), sibling)]
    stay = pltpu.make_async_copy(kv, whole(x, y), local_sems.at[2])
    stay.start()

    def queries_of(zb):
        q_sum[...] = jnp.zeros_like(q_sum)

        @pl.loop(0, 16)
        def _(k):
            piece = weights[k // 4, k % 4, :, :, 0:256].reshape(256, 256)
            left_side = rows[2 * zb : 2 * zb + 2, :, :, depth(k)].reshape(BLOCK, 256)
            q_sum[...] += jnp.dot(left_side, piece, preferred_element_type=jnp.float32)

        for h in range(2):
            at = pl.ds(h * HEAD_SIZE, HEAD_SIZE)
            q_out[zb, :, at] = turn(q_sum[:, at], tables[0, zb], tables[1, zb]).astype(jnp.bfloat16)

    def share(xx, yy):
        siblings.append(same(whole(xx, yy), sibling))

    a_prev, a_next, b_prev, b_next = {}, {}, {}, {}

    def a_send(k):
        a_prev[k] = same(part(0, x, ys[k]), x_next)
        a_next[k] = same(part(0, x, ys[k]), x_prev)

    def b_send(k):
        b_prev[k] = same(part(1, xs[k], y), y_next)
        b_next[k] = same(part(1, xs[k], y), y_prev)

    queries_of(0)
    queries_of(1)
    from_y_prev.wait_recv()
    y_far_prev = same(half(0, x, ys[3]), y_next)
    a_send(3)
    from_x_prev.wait_recv()
    x_far_prev = same(half(0, xs[3], y), x_next)
    b_send(3)
    from_y_next.wait_recv()
    y_far_next = same(half(1, x, ys[1]), y_prev)
    a_send(1)
    from_x_next.wait_recv()
    x_far_next = same(half(1, xs[1], y), x_prev)
    b_send(1)
    for xx, yy in ((0, 3), (0, 1), (3, 0), (1, 0)):
        share(xs[xx], ys[yy])
    queries_of(2)
    y_far_prev.wait_recv()
    y_far_next.wait_recv()
    a_send(2)
    x_far_prev.wait_recv()
    x_far_next.wait_recv()
    b_send(2)
    share(x, ys[2])
    share(xs[2], y)
    fa, fb = {}, {}
    for k in (3, 1, 2):
        a_prev[k].wait_recv()
        fa[k, 0] = same(cell(0, 0, xs[3], ys[k]), x_next)
        b_prev[k].wait_recv()
        fb[k, 0] = same(cell(0, 1, xs[k], ys[3]), y_next)
        a_next[k].wait_recv()
        fa[k, 1] = same(cell(1, 0, xs[1], ys[k]), x_prev)
        b_next[k].wait_recv()
        fb[k, 1] = same(cell(1, 1, xs[k], ys[1]), y_prev)
        if k == 1:
            for xx in (1, 3):
                for yy in (1, 3):
                    share(xs[xx], ys[yy])
            queries_of(3)
    for k in (3, 1, 2):
        for f in range(2):
            fa[k, f].wait_recv()
            fb[k, f].wait_recv()
    for xx, yy in ((1, 2), (3, 2), (2, 1), (2, 3), (2, 2)):
        share(xs[xx], ys[yy])
    for copy in siblings:
        copy.wait_recv()
    stay.wait()
    for own, copy, _ in a2a:
        pl.when(jnp.logical_not(own))(copy.wait_send)
    cp.finish()


def front(hidden, gain, w_query, w_key, w_value, doc_ids, positions, inverse):
    anywhere = pl.BlockSpec(memory_space=pl.ANY)
    inside = pl.BlockSpec(memory_space=pltpu.VMEM)
    return pl.pallas_call(
        front_kernel,
        out_shape=(
            jax.ShapeDtypeStruct((4, BLOCK, 2 * HEAD_SIZE), jnp.bfloat16),
            jax.ShapeDtypeStruct((2, 4, 2, 2, 4, BLOCK, HEAD_SIZE), jnp.bfloat16),
            jax.ShapeDtypeStruct((8, 128), jnp.int32),
        ),
        in_specs=[inside, inside, anywhere, anywhere, anywhere, inside, inside, inside],
        out_specs=(inside, anywhere, inside),
        scratch_shapes=[
            pltpu.VMEM((8, 2, 48, 4096), jnp.bfloat16),
            pltpu.VMEM((4, 4, 4, 64, 384), jnp.bfloat16),
            pltpu.VMEM((4, 4, 4, 8, 128), jnp.int32),
            pltpu.VMEM((8, 128), jnp.int32),
            pltpu.VMEM((2, 4, BLOCK, HEAD_SIZE), jnp.float32),
            pltpu.VMEM((768, HEAD_SIZE), jnp.float32),
            pltpu.VMEM((2, 2, BLOCK, HEAD_SIZE), jnp.bfloat16),
            pltpu.VMEM((BLOCK, 2 * HEAD_SIZE), jnp.float32),
            pltpu.SemaphoreType.DMA((120,)),
            pltpu.SemaphoreType.DMA((120,)),
            pltpu.SemaphoreType.DMA((8,)),
            pltpu.SemaphoreType.DMA((8,)),
            pltpu.SemaphoreType.DMA((3,)),
        ],
        compiler_params=pltpu.CompilerParams(
            collective_id=0, has_side_effects=True, vmem_limit_bytes=32 << 20
        ),
        name="front",
    )(hidden, gain, w_query, w_key, w_value, doc_ids, positions, inverse)


def attend_kernel(bounds, q_ref, k_ref, v_ref, first_ref, out_ref, even, odd, summed):
    block = pl.program_id(0)
    t_low, t_clear, t_edge, t_high, row0 = (bounds[block, i] for i in range(5))
    scale = HEAD_SIZE ** (-0.5) * math.log2(math.e)
    width = 2 * BLOCK
    queries = jnp.concatenate([q_ref[0, :, :HEAD_SIZE], q_ref[0, :, HEAD_SIZE:]], axis=0)
    summed[...] = jnp.zeros_like(summed)

    half = KEY_TILE // 2

    def produce(store, begin, masked):
        peak = None
        for u in range(half // KEY_PIECE):
            first_key = begin + u * KEY_PIECE
            keys = k_ref[pl.ds(pl.multiple_of(first_key, KEY_PIECE), KEY_PIECE), :]
            piece = lax.dot_general(
                keys, queries, (((1,), (1,)), ((), ())), preferred_element_type=jnp.float32
            )
            if masked:
                key = first_key + lax.broadcasted_iota(jnp.int32, (KEY_PIECE, width), 0)
                lane = lax.broadcasted_iota(jnp.int32, (1, width), 1)
                query = row0 + jnp.where(lane < BLOCK, lane, lane - BLOCK)
                allowed = (key <= query) & (key >= first_ref[0])
                piece = jnp.where(allowed, piece, masked_score)
            store[u * KEY_PIECE : (u + 1) * KEY_PIECE, :] = piece
            top = jnp.max(piece.reshape(KEY_PIECE // 8, 8, width), axis=0)
            peak = top if peak is None else jnp.maximum(peak, top)
        return peak

    def consume(store, begin, peak, total, fresh):
        latest = jnp.maximum(peak, jnp.max(fresh, axis=0, keepdims=True))
        shrink = jnp.exp2((peak - latest) * scale)
        total = total * shrink
        offset = latest * scale
        gained = None
        for u in range(half // KEY_PIECE):
            weights = jnp.exp2(store[u * KEY_PIECE : (u + 1) * KEY_PIECE, :] * scale - offset)
            total = total + jnp.sum(weights.reshape(KEY_PIECE // 8, 8, width), axis=0)
            values = v_ref[pl.ds(pl.multiple_of(begin + u * KEY_PIECE, KEY_PIECE), KEY_PIECE), :]
            term = lax.dot_general(
                values, weights.astype(jnp.bfloat16), (((0,), (0,)), ((), ())),
                preferred_element_type=jnp.float32,
            )
            gained = term if gained is None else gained + term
        summed[...] = summed[...] * shrink + gained
        return latest, total

    def step(masked, t, carry):
        peak, total, fresh = carry
        begin = t * KEY_TILE
        following = produce(even, begin, masked)
        peak, total = consume(odd, begin - half, peak, total, fresh)
        fresh = produce(odd, begin + half, masked)
        peak, total = consume(even, begin, peak, total, following)
        return peak, total, fresh

    begin = t_low * KEY_TILE
    peak, total = jnp.full((1, width), masked_score, jnp.float32), jnp.zeros((8, width), jnp.float32)
    following = produce(even, begin, True)
    fresh = produce(odd, begin + half, True)
    peak, total = consume(even, begin, peak, total, following)
    carry = (peak, total, fresh)
    start = t_low + 1
    carry = lax.fori_loop(start, t_clear, functools.partial(step, True), carry)
    carry = lax.fori_loop(jnp.maximum(t_clear, start), t_edge, functools.partial(step, False), carry)
    carry = lax.fori_loop(jnp.maximum(t_edge, start), t_high, functools.partial(step, True), carry)
    peak, total = consume(odd, t_high * KEY_TILE - half, *carry)
    total = jnp.sum(total, axis=0, keepdims=True)
    result = (summed[...] / total).T
    out_ref[0, :, :HEAD_SIZE] = result[:BLOCK].astype(jnp.bfloat16)
    out_ref[0, :, HEAD_SIZE:] = result[BLOCK:].astype(jnp.bfloat16)


def attend(bounds, queries, both, first):
    return pl.pallas_call(
        attend_kernel,
        out_shape=jax.ShapeDtypeStruct((4, BLOCK, 2 * HEAD_SIZE), jnp.bfloat16),
        grid_spec=pltpu.PrefetchScalarGridSpec(
            num_scalar_prefetch=1,
            grid=(4,),
            in_specs=[
                pl.BlockSpec((1, BLOCK, 2 * HEAD_SIZE), lambda i, b: (i, 0, 0)),
                pl.BlockSpec((None, SEQUENCE, HEAD_SIZE), lambda i, b: (0, 0, 0)),
                pl.BlockSpec((None, SEQUENCE, HEAD_SIZE), lambda i, b: (1, 0, 0)),
                pl.BlockSpec((1, 1, 2 * BLOCK), lambda i, b: (i, 0, 0)),
            ],
            out_specs=pl.BlockSpec((1, BLOCK, 2 * HEAD_SIZE), lambda i, b: (i, 0, 0)),
            scratch_shapes=[
                pltpu.VMEM((KEY_TILE // 2, 2 * BLOCK), jnp.float32),
                pltpu.VMEM((KEY_TILE // 2, 2 * BLOCK), jnp.float32),
                pltpu.VMEM((HEAD_SIZE, 2 * BLOCK), jnp.float32),
            ],
        ),
        compiler_params=pltpu.CompilerParams(vmem_limit_bytes=48 << 20),
        name="attend",
    )(bounds, queries, both, both, first)


def back_kernel(
    own, w_out, hidden, out,
    attended, weights, mine, given, landed, joined, arrived,
    send_sems, recv_sems, local_sems, step_send, step_recv,
):
    x, y, zh, zl, c = place()
    cz = zh // 2
    sibling, across = device(x, y, zh, zl, 1 - c), device(x, y, zh, 1 - zl, c)
    partners = [device(x, y, (zh + k) % 4, zl, cc) for k in range(4) for cc in (c, 1 - c)][1:]
    partners.append(across)
    pieces = 4
    width = 4096 // pieces
    cut = lambda i: pl.ds(i * width, width)
    fetch = [
        pltpu.make_async_copy(w_out.at[:, cut(i)], weights.at[:, cut(i)], local_sems.at[1 + i])
        for i in range(pieces)
    ]
    for copy in fetch:
        copy.start()
    greet(partners)
    spot = lambda j, cc: attended.at[:, pl.ds(pl.multiple_of((2 * j + cc) * 256, 256), 256)]
    copies = []
    here = cz == c
    for k in (2, 1, 3, 0):
        zt = (zh + k) % 4
        copy = pltpu.make_async_remote_copy(
            src_ref=own.at[zt],
            dst_ref=spot(zh % 2, c),
            send_sem=send_sems.at[k],
            recv_sem=recv_sems.at[(zh % 2) * 2 + c],
            device_id=device(x, y, zt, zl, cz),
            device_id_type=MESH,
        )
        if k == 0:
            stay = pltpu.make_async_copy(own.at[zt], spot(zh % 2, c), local_sems.at[0])
            pl.when(here)(stay.start)
            pl.when(jnp.logical_not(here))(copy.start)
        else:
            copy.start()
        copies.append(copy)
    for j in range(2):
        for cc in range(2):
            arrives = pltpu.make_async_remote_copy(
                src_ref=own.at[0],
                dst_ref=spot(j, cc),
                send_sem=send_sems.at[0],
                recv_sem=recv_sems.at[2 * j + cc],
                device_id=sibling,
                device_id_type=MESH,
            )
            local = (zh == 2 * c + j) & (c == cc)
            pl.when(jnp.logical_not(local))(arrives.wait_recv)
    pl.when(here)(stay.wait)

    cp = Copies(step_send, step_recv)
    to_sibling, to_across = [], []

    def pass_on(i):
        to_sibling[i].wait_recv()
        joined[i] = (mine[i, 1 - zl] + landed[i, 1 - zl].astype(jnp.float32)).astype(jnp.bfloat16)
        to_across.append(cp.send(joined.at[i], arrived.at[i], across))

    for i in range(pieces):
        fetch[i].wait()
        term = jnp.dot(attended[...], weights[:, cut(i)], preferred_element_type=jnp.float32)
        term = term.reshape(2, 2, 48, width)
        mine[i] = jnp.where(c == 0, term[:, 0], term[:, 1])
        given[i] = jnp.where(c == 0, term[:, 1], term[:, 0]).astype(jnp.bfloat16)
        to_sibling.append(cp.send(given.at[i], landed.at[i], sibling))
        if i > 0:
            pass_on(i - 1)
    pass_on(pieces - 1)
    for i in range(pieces):
        total = mine[i, zl] + landed[i, zl].astype(jnp.float32)
        to_across[i].wait_recv()
        total = total + arrived[i].astype(jnp.float32)
        out[:, cut(i)] = (hidden[:, cut(i)].astype(jnp.float32) + total).astype(jnp.bfloat16)
    pl.when(jnp.logical_not(here))(copies[-1].wait_send)
    for copy in copies[:-1]:
        copy.wait_send()
    cp.finish()


def back(own, w_out, hidden):
    anywhere = pl.BlockSpec(memory_space=pl.ANY)
    inside = pl.BlockSpec(memory_space=pltpu.VMEM)
    return pl.pallas_call(
        back_kernel,
        out_shape=jax.ShapeDtypeStruct((48, 4096), jnp.bfloat16),
        in_specs=[anywhere, anywhere, inside],
        out_specs=inside,
        scratch_shapes=[
            pltpu.VMEM((BLOCK, 1024), jnp.bfloat16),
            pltpu.VMEM((1024, 4096), jnp.bfloat16),
            pltpu.VMEM((4, 2, 48, 1024), jnp.float32),
            pltpu.VMEM((4, 2, 48, 1024), jnp.bfloat16),
            pltpu.VMEM((4, 2, 48, 1024), jnp.bfloat16),
            pltpu.VMEM((4, 48, 1024), jnp.bfloat16),
            pltpu.VMEM((4, 48, 1024), jnp.bfloat16),
            pltpu.SemaphoreType.DMA((4,)),
            pltpu.SemaphoreType.DMA((4,)),
            pltpu.SemaphoreType.DMA((5,)),
            pltpu.SemaphoreType.DMA((8,)),
            pltpu.SemaphoreType.DMA((8,)),
        ],
        compiler_params=pltpu.CompilerParams(
            collective_id=1, has_side_effects=True, vmem_limit_bytes=32 << 20
        ),
        name="back",
    )(own, w_out, hidden)


def body(hidden_in, norm_gain, w_query, w_key, value_weight, w_out, doc_ids, positions):
    x, y, zh, zl, c = place()
    inverse = yarn_inverse(HEAD_SIZE)
    queries, both, first = front(
        hidden_in,
        norm_gain.reshape(1, 4096),
        w_query,
        w_key,
        value_weight,
        doc_ids.reshape(1, BLOCK),
        positions.reshape(1, BLOCK),
        jnp.asarray([inverse + inverse], dtype=jnp.float32),
    )
    first = first.reshape(4, 256)[:, :BLOCK]
    row0 = (x * 16 + jnp.arange(4, dtype=jnp.int32) * 4 + y) * BLOCK
    t_low = first[:, 0] // KEY_TILE
    t_edge = jnp.maximum((row0 + 1) // KEY_TILE, t_low)
    t_clear = jnp.clip((first[:, -1] + KEY_TILE - 1) // KEY_TILE, t_low, t_edge)
    t_high = (row0 + BLOCK - 1) // KEY_TILE + 1
    bounds = jnp.stack([t_low, t_clear, t_edge, t_high, row0], axis=1)
    lanes = jnp.concatenate([first, first], axis=1).reshape(4, 1, 2 * BLOCK)
    attended = attend(bounds, queries, both.reshape(2, SEQUENCE, HEAD_SIZE), lanes)
    return back(attended, w_out, hidden_in)


def solution(mesh):
    in_specs = (
        P(("outer", "inner", "tensor"), None),
        P(),
        P("inner", "tensor"),
        P("inner", "tensor"),
        P("inner", "tensor"),
        P("tensor", None),
        P(("outer", "inner")),
        P(("outer", "inner")),
    )
    out_specs = P(("outer", "inner", "tensor"), None)
    return jax.shard_map(body, mesh=mesh, in_specs=in_specs, out_specs=out_specs, check_vma=False)
```

```python
import functools
import math

import jax
import jax.numpy as jnp
from jax import lax
from jax.experimental import pallas as pl
from jax.experimental.pallas import tpu as pltpu
from jax.sharding import PartitionSpec as P

HEAD_SIZE = 128
BLOCK = 192
SEQUENCE = 12288
KEY_TILE = 1024
KEY_PIECE = 256
MESH = pl.DeviceIdType.MESH


rope_base = 500000.0
yarn_factor = 8.0
trained_context = 8192.0
beta_fast = 32.0
beta_slow = 1.0
norm_epsilon = 1e-05
masked_score = -1e30


def yarn_inverse(head_dim):
    half_dim = head_dim // 2

    def correction(rotations):
        return (
            head_dim
            * math.log(trained_context / (rotations * 2.0 * math.pi))
            / (2.0 * math.log(rope_base))
        )

    lowest = max(math.floor(correction(beta_fast)), 0)
    highest = min(math.ceil(correction(beta_slow)), head_dim - 1)
    spread = max(highest - lowest, 0.001)
    values = []
    for column in range(half_dim):
        extrapolated = rope_base ** (-2.0 * column / head_dim)
        ramp = min(max((column - lowest) / spread, 0.0), 1.0)
        values.append(extrapolated / yarn_factor * ramp + extrapolated * (1.0 - ramp))
    return values


def place():
    outer, inner, tensor = (lax.axis_index(name) for name in ("outer", "inner", "tensor"))
    return outer, inner % 4, inner // 4, tensor // 2, tensor % 2


def device(x, y, zh, zl, c):
    return (x, zh * 4 + y, zl * 2 + c)


def greet(partners):
    barrier = pltpu.get_barrier_semaphore()
    for partner in partners:
        pl.semaphore_signal(barrier, inc=1, device_id=partner, device_id_type=MESH)
    pl.semaphore_wait(barrier, len(partners))


class Copies:
    def __init__(self, send_sems, recv_sems):
        self.send_sems, self.recv_sems, self.count, self.sent = send_sems, recv_sems, 0, []

    def send(self, src, dst, target):
        copy = pltpu.make_async_remote_copy(
            src_ref=src,
            dst_ref=dst,
            send_sem=self.send_sems.at[self.count],
            recv_sem=self.recv_sems.at[self.count],
            device_id=target,
            device_id_type=MESH,
        )
        self.count += 1
        copy.start()
        self.sent.append(copy)
        return copy

    def finish(self):
        for copy in self.sent:
            copy.wait_send()


def front_kernel(
    hidden_in, gain_in, w_query, w_key, w_value, doc_ids_in, positions_in, inverse_in,
    q_out, both, first_out,
    hidden, gain, doc_ids, positions, inverse, rows, weights, meta, meta_own, tables, product, kv, q_sum,
    send_sems, recv_sems, a2a_send, a2a_recv, local_sems,
):
    x, y, zh, zl, c = place()
    p = zh * 2 + zl
    near = lambda q: device(x, y, (q % 8) // 2, q % 2, c)
    right, left = near(p + 1), near(p + 7)
    sibling = device(x, y, zh, zl, 1 - c)
    xs = [(x + k) % 4 for k in range(4)]
    ys = [(y + k) % 4 for k in range(4)]
    y_next, y_far, y_prev = (device(x, ys[k], zh, zl, c) for k in (1, 2, 3))
    x_next, x_far, x_prev = (device(xs[k], y, zh, zl, c) for k in (1, 2, 3))
    columns = [device(x, y, (zh + k) % 4, zl, cc) for k in range(4) for cc in (c, 1 - c)][1:]
    partners = columns + [right, left, y_next, y_prev, y_far, x_next, x_prev, x_far]
    barrier = pltpu.get_barrier_semaphore()
    for partner in partners:
        pl.semaphore_signal(barrier, inc=1, device_id=partner, device_id_type=MESH)
    cp = Copies(send_sems, recv_sems)
    fetches = [
        pltpu.make_async_copy(source, target, local_sems.at[i])
        for i, (source, target) in enumerate(
            (
                (doc_ids_in, doc_ids),
                (positions_in, positions),
                (hidden_in, hidden),
                (gain_in, gain),
                (inverse_in, inverse),
            )
        )
    ]
    for copy in fetches:
        copy.start()
    fetches[0].wait()
    fetches[1].wait()

    meta_own[...] = jnp.full((8, 128), 99, jnp.int32)
    meta_own[0:1, :] = doc_ids[:, :128]
    meta_own[1:2, :64] = doc_ids[:, 128:]
    meta_own[2:3, :] = positions[:, :128]
    meta_own[3:4, :64] = positions[:, 128:]
    meta[x, y, zh] = meta_own[...]
    for copy in fetches[2:]:
        copy.wait()
    widened = hidden[...].astype(jnp.float32)
    power = jnp.mean(widened * widened, axis=-1, keepdims=True)
    rows[p, c] = (widened * lax.rsqrt(power + norm_epsilon) * gain[...]).astype(jnp.bfloat16)
    pl.semaphore_wait(barrier, len(partners))

    a2a = []
    landing = (pl.ds(0, 256), pl.ds(256, 128))
    for j in range(2):
        for cc in range(2):
            zt = 2 * c + j
            own = (zt == zh) & (c == cc)
            taken = pl.ds(pl.multiple_of(x * 64, 64), 64)
            sources = (
                w_query.at[taken, pl.ds(j * 512 + cc * 256, 256)],
                (w_value if cc else w_key).at[taken, pl.ds(j * 128, 128)],
            )
            for i in range(2):
                spot = weights.at[zh, y, x, :, landing[i]]
                copy = pltpu.make_async_remote_copy(
                    src_ref=sources[i],
                    dst_ref=spot,
                    send_sem=a2a_send.at[4 * j + 2 * cc + i],
                    recv_sem=a2a_recv.at[2 * zh + i],
                    device_id=device(x, y, zt, zl, cc),
                    device_id_type=MESH,
                )
                stay = pltpu.make_async_copy(sources[i], spot, local_sems.at[i])
                pl.when(own)(stay.start)
                pl.when(jnp.logical_not(own))(copy.start)
                a2a.append((own, copy, stay))
    chunks_right = (pl.ds(0, 16), pl.ds(16, 32))
    chunks_left = (pl.ds(32, 16), pl.ds(0, 32))
    to_right, to_left, to_sibling = {}, {}, []
    same = lambda ref, target: cp.send(ref, ref, target)
    meta_z = [
        cp.send(meta_own, meta.at[x, y, zh], device(x, y, (zh + k) % 4, zl, c)) for k in (1, 2, 3)
    ]
    for h in range(2):
        to_right[0, h] = same(rows.at[p, c, chunks_right[h]], right)
        to_left[0, h] = same(rows.at[p, c, chunks_left[h]], left)
    to_sibling.append(same(rows.at[p, c], sibling))

    for source in range(4):
        for i in range(2):
            arrives = pltpu.make_async_remote_copy(
                src_ref=weights.at[source, y, x, :, landing[i]],
                dst_ref=weights.at[source, y, x, :, landing[i]],
                send_sem=a2a_send.at[0],
                recv_sem=a2a_recv.at[2 * source + i],
                device_id=sibling,
                device_id_type=MESH,
            )
            own = (zh == source) & (c == zh // 2)
            pl.when(jnp.logical_not(own))(arrives.wait_recv)
    for own, copy, stay in a2a:
        pl.when(own)(stay.wait)
    mine = weights.at[:, y, x]
    wy_next, wy_prev = same(mine, y_next), same(mine, y_prev)
    wx, forwards = {}, []

    def along_x(k):
        piece = weights.at[:, ys[k], x]
        wx[len(wx)] = (ys[k], same(piece, x_next), same(piece, x_prev))

    def forward_x(k):
        yy, a, b = wx[k]
        a.wait_recv()
        forwards.append(same(weights.at[pl.ds(0, 2), yy, xs[3]], x_next))
        b.wait_recv()
        forwards.append(same(weights.at[pl.ds(2, 2), yy, xs[1]], x_prev))

    def ring(step):
        for h in range(2):
            for to, chunks, target, hop in (
                (to_right, chunks_right, right, 7),
                (to_left, chunks_left, left, 1),
            ):
                to[step, h].wait_recv()
                q = (p + hop * (step + 1)) % 8
                if step < 3:
                    spot = rows.at[q, c, chunks[h]]
                    to_sibling.append(same(spot, sibling))
                    if step < 2:
                        to[step + 1, h] = same(spot, target)
                    else:
                        to[3, h] = same(far_spot(q, h, hop), target)
                else:
                    to_sibling.append(same(far_spot(q, h, hop), sibling))

    def far_spot(q, h, hop):
        if h == 0:
            return rows.at[q, c, pl.ds(0, 16) if hop == 7 else pl.ds(32, 16)]
        return rows.at[q, c, pl.ds(16, 16), pl.ds(0 if hop == 7 else 2048, 2048)]

    along_x(0)
    for copy in meta_z:
        copy.wait_recv()
    mine = meta.at[x, y]
    meta_y = [same(mine, target) for target in (y_next, y_far, y_prev)]
    ring(0)
    wy_next.wait_recv()
    wy_far_next = same(weights.at[pl.ds(0, 2), ys[3], x], y_next)
    along_x(3)
    wy_prev.wait_recv()
    wy_far_prev = same(weights.at[pl.ds(2, 2), ys[1], x], y_prev)
    along_x(1)
    for copy in meta_y:
        copy.wait_recv()
    mine = meta.at[x]
    meta_x = [same(mine, target) for target in (x_next, x_far, x_prev)]
    forward_x(0)
    wy_far_next.wait_recv()
    wy_far_prev.wait_recv()
    along_x(2)

    def tables_of(zb):
        tile = meta[x, y, zb].astype(jnp.float32)
        upper = jnp.broadcast_to(tile[2:3], (128, 128)).T
        lower = jnp.broadcast_to(tile[3:4], (128, 128)).T
        angles = jnp.concatenate([upper, lower[:64]], axis=0) * inverse[...]
        attention_gain = 0.1 * math.log(yarn_factor) + 1.0
        lane = lax.broadcasted_iota(jnp.int32, (BLOCK, HEAD_SIZE), 1)
        sine = jnp.sin(angles) * attention_gain
        tables[0, zb] = jnp.cos(angles) * attention_gain
        tables[1, zb] = jnp.where(lane < HEAD_SIZE // 2, -sine, sine)

    tables_of(0)
    tables_of(1)
    ring(1)
    tables_of(2)
    forward_x(1)
    forward_x(2)
    tables_of(3)
    ring(2)
    forward_x(3)
    for copy in meta_x:
        copy.wait_recv()
    everything = meta[...].reshape(64, 8, 128)
    line = lax.broadcasted_iota(jnp.int32, (8, 128), 0)
    firsts = []
    for d in range(1, 6):
        hits = jnp.sum(jnp.where(everything < d, 1, 0), axis=0)
        hits = jnp.where(line < 2, hits, 0).astype(jnp.float32)
        firsts.append(jnp.sum(jnp.sum(hits, axis=0, keepdims=True), axis=1, keepdims=True))
    for zb in range(4):
        documents = meta[x, y, zb][0:2]
        first = jnp.zeros((2, 128), jnp.float32)
        for d in range(1, 6):
            first = jnp.where(documents == d, firsts[d - 1], first)
        first_out[2 * zb : 2 * zb + 2, :] = first.astype(jnp.int32)
    ring(3)
    for copy in forwards + to_sibling:
        copy.wait_recv()

    def depth(k):
        return pl.ds(pl.multiple_of(k * 256, 256), 256)

    product[...] = jnp.zeros_like(product)

    @pl.loop(0, 16)
    def _(k):
        piece = weights[k // 4, k % 4, :, :, 256:384].reshape(256, HEAD_SIZE)
        left_side = rows[:, :, :, depth(k)].reshape(768, 256)
        product[...] += jnp.dot(left_side, piece, preferred_element_type=jnp.float32)

    def turn(head, cosine, sine):
        return head * cosine + pltpu.roll(head, HEAD_SIZE // 2, 1) * sine

    is_key = c == 0
    for zb in range(4):
        head = product[zb * BLOCK : (zb + 1) * BLOCK, :]
        cosine = jnp.where(is_key, tables[0, zb], 1.0)
        sine = jnp.where(is_key, tables[1, zb], 0.0)
        kv[zb // 2, zb % 2] = turn(head, cosine, sine).astype(jnp.bfloat16)

    whole = lambda xx, yy: both.at[c, xx, :, :, yy]
    half = lambda f, xx, yy: both.at[c, xx, f, :, yy]
    part = lambda a, xx, yy: both.at[c, xx, :, a, yy]
    cell = lambda f, a, xx, yy: both.at[c, xx, f, a, yy]
    from_y_prev = cp.send(kv, whole(x, y), y_next)
    from_x_prev = cp.send(kv, whole(x, y), x_next)
    from_y_next = cp.send(kv, whole(x, y), y_prev)
    from_x_next = cp.send(kv, whole(x, y), x_prev)
    siblings = [cp.send(kv, whole(x, y), sibling)]
    stay = pltpu.make_async_copy(kv, whole(x, y), local_sems.at[2])
    stay.start()

    def queries_of(zb):
        q_sum[...] = jnp.zeros_like(q_sum)

        @pl.loop(0, 16)
        def _(k):
            piece = weights[k // 4, k % 4, :, :, 0:256].reshape(256, 256)
            left_side = rows[2 * zb : 2 * zb + 2, :, :, depth(k)].reshape(BLOCK, 256)
            q_sum[...] += jnp.dot(left_side, piece, preferred_element_type=jnp.float32)

        for h in range(2):
            at = pl.ds(h * HEAD_SIZE, HEAD_SIZE)
            q_out[zb, :, at] = turn(q_sum[:, at], tables[0, zb], tables[1, zb]).astype(jnp.bfloat16)

    def share(xx, yy):
        siblings.append(same(whole(xx, yy), sibling))

    a_prev, a_next, b_prev, b_next = {}, {}, {}, {}

    def a_send(k):
        a_prev[k] = same(part(0, x, ys[k]), x_next)
        a_next[k] = same(part(0, x, ys[k]), x_prev)

    def b_send(k):
        b_prev[k] = same(part(1, xs[k], y), y_next)
        b_next[k] = same(part(1, xs[k], y), y_prev)

    queries_of(0)
    queries_of(1)
    from_y_prev.wait_recv()
    y_far_prev = same(half(0, x, ys[3]), y_next)
    a_send(3)
    from_x_prev.wait_recv()
    x_far_prev = same(half(0, xs[3], y), x_next)
    b_send(3)
    from_y_next.wait_recv()
    y_far_next = same(half(1, x, ys[1]), y_prev)
    a_send(1)
    from_x_next.wait_recv()
    x_far_next = same(half(1, xs[1], y), x_prev)
    b_send(1)
    for xx, yy in ((0, 3), (0, 1), (3, 0), (1, 0)):
        share(xs[xx], ys[yy])
    queries_of(2)
    y_far_prev.wait_recv()
    y_far_next.wait_recv()
    a_send(2)
    x_far_prev.wait_recv()
    x_far_next.wait_recv()
    b_send(2)
    share(x, ys[2])
    share(xs[2], y)
    fa, fb = {}, {}
    for k in (3, 1, 2):
        a_prev[k].wait_recv()
        fa[k, 0] = same(cell(0, 0, xs[3], ys[k]), x_next)
        b_prev[k].wait_recv()
        fb[k, 0] = same(cell(0, 1, xs[k], ys[3]), y_next)
        a_next[k].wait_recv()
        fa[k, 1] = same(cell(1, 0, xs[1], ys[k]), x_prev)
        b_next[k].wait_recv()
        fb[k, 1] = same(cell(1, 1, xs[k], ys[1]), y_prev)
        if k == 1:
            for xx in (1, 3):
                for yy in (1, 3):
                    share(xs[xx], ys[yy])
            queries_of(3)
    for k in (3, 1, 2):
        for f in range(2):
            fa[k, f].wait_recv()
            fb[k, f].wait_recv()
    for xx, yy in ((1, 2), (3, 2), (2, 1), (2, 3), (2, 2)):
        share(xs[xx], ys[yy])
    for copy in siblings:
        copy.wait_recv()
    stay.wait()
    for own, copy, _ in a2a:
        pl.when(jnp.logical_not(own))(copy.wait_send)
    cp.finish()


def front(hidden, gain, w_query, w_key, w_value, doc_ids, positions, inverse):
    outside = pl.BlockSpec(memory_space=pltpu.HBM)
    inside = pl.BlockSpec(memory_space=pltpu.VMEM)
    return pl.pallas_call(
        front_kernel,
        out_shape=(
            jax.ShapeDtypeStruct((4, BLOCK, 2 * HEAD_SIZE), jnp.bfloat16),
            jax.ShapeDtypeStruct((2, 4, 2, 2, 4, BLOCK, HEAD_SIZE), jnp.bfloat16),
            jax.ShapeDtypeStruct((8, 128), jnp.int32),
        ),
        in_specs=[outside] * 8,
        out_specs=(inside, outside, inside),
        scratch_shapes=[
            pltpu.VMEM((48, 4096), jnp.bfloat16),
            pltpu.VMEM((1, 4096), jnp.float32),
            pltpu.VMEM((1, BLOCK), jnp.int32),
            pltpu.VMEM((1, BLOCK), jnp.int32),
            pltpu.VMEM((1, HEAD_SIZE), jnp.float32),
            pltpu.VMEM((8, 2, 48, 4096), jnp.bfloat16),
            pltpu.VMEM((4, 4, 4, 64, 384), jnp.bfloat16),
            pltpu.VMEM((4, 4, 4, 8, 128), jnp.int32),
            pltpu.VMEM((8, 128), jnp.int32),
            pltpu.VMEM((2, 4, BLOCK, HEAD_SIZE), jnp.float32),
            pltpu.VMEM((768, HEAD_SIZE), jnp.float32),
            pltpu.VMEM((2, 2, BLOCK, HEAD_SIZE), jnp.bfloat16),
            pltpu.VMEM((BLOCK, 2 * HEAD_SIZE), jnp.float32),
            pltpu.SemaphoreType.DMA((120,)),
            pltpu.SemaphoreType.DMA((120,)),
            pltpu.SemaphoreType.DMA((8,)),
            pltpu.SemaphoreType.DMA((8,)),
            pltpu.SemaphoreType.DMA((5,)),
        ],
        compiler_params=pltpu.CompilerParams(
            collective_id=0, has_side_effects=True, vmem_limit_bytes=55 << 20
        ),
        name="front",
    )(
        *(
            pltpu.with_memory_space_constraint(a, pltpu.HBM)
            for a in (hidden, gain, w_query, w_key, w_value, doc_ids, positions, inverse)
        )
    )


def attend_kernel(bounds, q_ref, both_in, first_ref, out_ref, even, odd, summed):
    both_ref = both_in.reshape(2, SEQUENCE, HEAD_SIZE)
    block = pl.program_id(0)
    t_low, t_clear, t_edge, t_high, row0 = (bounds[block, i] for i in range(5))
    scale = HEAD_SIZE ** (-0.5) * math.log2(math.e)
    width = 2 * BLOCK
    queries = jnp.concatenate([q_ref[0, :, :HEAD_SIZE], q_ref[0, :, HEAD_SIZE:]], axis=0)
    summed[...] = jnp.zeros_like(summed)

    half = KEY_TILE // 2

    def produce(store, begin, masked):
        peak = None
        for u in range(half // KEY_PIECE):
            first_key = begin + u * KEY_PIECE
            keys = both_ref[0, pl.ds(pl.multiple_of(first_key, KEY_PIECE), KEY_PIECE), :]
            piece = lax.dot_general(
                keys, queries, (((1,), (1,)), ((), ())), preferred_element_type=jnp.float32
            )
            if masked:
                key = first_key + lax.broadcasted_iota(jnp.int32, (KEY_PIECE, width), 0)
                lane = lax.broadcasted_iota(jnp.int32, (1, width), 1)
                query = row0 + jnp.where(lane < BLOCK, lane, lane - BLOCK)
                allowed = (key <= query) & (key >= first_ref[0])
                piece = jnp.where(allowed, piece, masked_score)
            store[u * KEY_PIECE : (u + 1) * KEY_PIECE, :] = piece
            top = jnp.max(piece.reshape(KEY_PIECE // 8, 8, width), axis=0)
            peak = top if peak is None else jnp.maximum(peak, top)
        return peak

    def consume(store, begin, peak, total, fresh):
        latest = jnp.maximum(peak, jnp.max(fresh, axis=0, keepdims=True))
        shrink = jnp.exp2((peak - latest) * scale)
        total = total * shrink
        offset = latest * scale
        gained = None
        for u in range(half // KEY_PIECE):
            weights = jnp.exp2(store[u * KEY_PIECE : (u + 1) * KEY_PIECE, :] * scale - offset)
            total = total + jnp.sum(weights.reshape(KEY_PIECE // 8, 8, width), axis=0)
            values = both_ref[1, pl.ds(pl.multiple_of(begin + u * KEY_PIECE, KEY_PIECE), KEY_PIECE), :]
            term = lax.dot_general(
                values, weights.astype(jnp.bfloat16), (((0,), (0,)), ((), ())),
                preferred_element_type=jnp.float32,
            )
            gained = term if gained is None else gained + term
        summed[...] = summed[...] * shrink + gained
        return latest, total

    def step(masked, t, carry):
        peak, total, fresh = carry
        begin = t * KEY_TILE
        following = produce(even, begin, masked)
        peak, total = consume(odd, begin - half, peak, total, fresh)
        fresh = produce(odd, begin + half, masked)
        peak, total = consume(even, begin, peak, total, following)
        return peak, total, fresh

    begin = t_low * KEY_TILE
    peak, total = jnp.full((1, width), masked_score, jnp.float32), jnp.zeros((8, width), jnp.float32)
    following = produce(even, begin, True)
    fresh = produce(odd, begin + half, True)
    peak, total = consume(even, begin, peak, total, following)
    carry = (peak, total, fresh)
    start = t_low + 1
    carry = lax.fori_loop(start, t_clear, functools.partial(step, True), carry)
    carry = lax.fori_loop(jnp.maximum(t_clear, start), t_edge, functools.partial(step, False), carry)
    carry = lax.fori_loop(jnp.maximum(t_edge, start), t_high, functools.partial(step, True), carry)
    peak, total = consume(odd, t_high * KEY_TILE - half, *carry)
    total = jnp.sum(total, axis=0, keepdims=True)
    result = (summed[...] / total).T
    out_ref[0, :, :HEAD_SIZE] = result[:BLOCK].astype(jnp.bfloat16)
    out_ref[0, :, HEAD_SIZE:] = result[BLOCK:].astype(jnp.bfloat16)


def attend(bounds, queries, both, first):
    return pl.pallas_call(
        attend_kernel,
        out_shape=jax.ShapeDtypeStruct((4, BLOCK, 2 * HEAD_SIZE), jnp.bfloat16),
        grid_spec=pltpu.PrefetchScalarGridSpec(
            num_scalar_prefetch=1,
            grid=(4,),
            in_specs=[
                pl.BlockSpec((1, BLOCK, 2 * HEAD_SIZE), lambda i, b: (i, 0, 0)),
                pl.BlockSpec(memory_space=pltpu.VMEM),
                pl.BlockSpec((1, 1, 2 * BLOCK), lambda i, b: (i, 0, 0)),
            ],
            out_specs=pl.BlockSpec((1, BLOCK, 2 * HEAD_SIZE), lambda i, b: (i, 0, 0)),
            scratch_shapes=[
                pltpu.VMEM((KEY_TILE // 2, 2 * BLOCK), jnp.float32),
                pltpu.VMEM((KEY_TILE // 2, 2 * BLOCK), jnp.float32),
                pltpu.VMEM((HEAD_SIZE, 2 * BLOCK), jnp.float32),
            ],
        ),
        compiler_params=pltpu.CompilerParams(vmem_limit_bytes=16 << 20),
        name="attend",
    )(bounds, queries, both, first)


def back_kernel(
    own, w_out, hidden, out,
    attended, mine, given, landed, joined, arrived,
    send_sems, recv_sems, local_sems, step_send, step_recv,
):
    x, y, zh, zl, c = place()
    cz = zh // 2
    sibling, across = device(x, y, zh, zl, 1 - c), device(x, y, zh, 1 - zl, c)
    partners = [device(x, y, (zh + k) % 4, zl, cc) for k in range(4) for cc in (c, 1 - c)][1:]
    partners.append(across)
    pieces = 4
    width = 4096 // pieces
    cut = lambda i: pl.ds(i * width, width)
    greet(partners)
    spot = lambda j, cc: attended.at[:, pl.ds(pl.multiple_of((2 * j + cc) * 256, 256), 256)]
    copies = []
    here = cz == c
    for k in (2, 1, 3, 0):
        zt = (zh + k) % 4
        copy = pltpu.make_async_remote_copy(
            src_ref=own.at[zt],
            dst_ref=spot(zh % 2, c),
            send_sem=send_sems.at[k],
            recv_sem=recv_sems.at[(zh % 2) * 2 + c],
            device_id=device(x, y, zt, zl, cz),
            device_id_type=MESH,
        )
        if k == 0:
            stay = pltpu.make_async_copy(own.at[zt], spot(zh % 2, c), local_sems.at[0])
            pl.when(here)(stay.start)
            pl.when(jnp.logical_not(here))(copy.start)
        else:
            copy.start()
        copies.append(copy)
    for j in range(2):
        for cc in range(2):
            arrives = pltpu.make_async_remote_copy(
                src_ref=own.at[0],
                dst_ref=spot(j, cc),
                send_sem=send_sems.at[0],
                recv_sem=recv_sems.at[2 * j + cc],
                device_id=sibling,
                device_id_type=MESH,
            )
            local = (zh == 2 * c + j) & (c == cc)
            pl.when(jnp.logical_not(local))(arrives.wait_recv)
    pl.when(here)(stay.wait)

    cp = Copies(step_send, step_recv)
    to_sibling, to_across = [], []

    def pass_on(i):
        to_sibling[i].wait_recv()
        joined[i] = (mine[i, 1 - zl] + landed[i, 1 - zl].astype(jnp.float32)).astype(jnp.bfloat16)
        to_across.append(cp.send(joined.at[i], arrived.at[i], across))

    for i in range(pieces):
        term = jnp.dot(attended[...], w_out[:, cut(i)], preferred_element_type=jnp.float32)
        term = term.reshape(2, 2, 48, width)
        mine[i] = jnp.where(c == 0, term[:, 0], term[:, 1])
        given[i] = jnp.where(c == 0, term[:, 1], term[:, 0]).astype(jnp.bfloat16)
        to_sibling.append(cp.send(given.at[i], landed.at[i], sibling))
        if i > 0:
            pass_on(i - 1)
    pass_on(pieces - 1)
    for i in range(pieces):
        total = mine[i, zl] + landed[i, zl].astype(jnp.float32)
        to_across[i].wait_recv()
        total = total + arrived[i].astype(jnp.float32)
        out[:, cut(i)] = (hidden[:, cut(i)].astype(jnp.float32) + total).astype(jnp.bfloat16)
    pl.when(jnp.logical_not(here))(copies[-1].wait_send)
    for copy in copies[:-1]:
        copy.wait_send()
    cp.finish()


def back(own, w_out, hidden):
    anywhere = pl.BlockSpec(memory_space=pl.ANY)
    inside = pl.BlockSpec(memory_space=pltpu.VMEM)
    return pl.pallas_call(
        back_kernel,
        out_shape=jax.ShapeDtypeStruct((48, 4096), jnp.bfloat16),
        in_specs=[anywhere, inside, inside],
        out_specs=inside,
        scratch_shapes=[
            pltpu.VMEM((BLOCK, 1024), jnp.bfloat16),
            pltpu.VMEM((4, 2, 48, 1024), jnp.float32),
            pltpu.VMEM((4, 2, 48, 1024), jnp.bfloat16),
            pltpu.VMEM((4, 2, 48, 1024), jnp.bfloat16),
            pltpu.VMEM((4, 48, 1024), jnp.bfloat16),
            pltpu.VMEM((4, 48, 1024), jnp.bfloat16),
            pltpu.SemaphoreType.DMA((4,)),
            pltpu.SemaphoreType.DMA((4,)),
            pltpu.SemaphoreType.DMA((1,)),
            pltpu.SemaphoreType.DMA((8,)),
            pltpu.SemaphoreType.DMA((8,)),
        ],
        compiler_params=pltpu.CompilerParams(
            collective_id=1, has_side_effects=True, vmem_limit_bytes=32 << 20
        ),
        name="back",
    )(own, w_out, hidden)


def body(hidden_in, norm_gain, w_query, w_key, value_weight, w_out, doc_ids, positions):
    x, y, zh, zl, c = place()
    inverse = yarn_inverse(HEAD_SIZE)
    queries, both, first = front(
        hidden_in,
        norm_gain.reshape(1, 4096),
        w_query,
        w_key,
        value_weight,
        doc_ids.reshape(1, BLOCK),
        positions.reshape(1, BLOCK),
        jnp.asarray([inverse + inverse], dtype=jnp.float32),
    )
    first = first.reshape(4, 256)[:, :BLOCK]
    row0 = (x * 16 + jnp.arange(4, dtype=jnp.int32) * 4 + y) * BLOCK
    t_low = first[:, 0] // KEY_TILE
    t_edge = jnp.maximum((row0 + 1) // KEY_TILE, t_low)
    t_clear = jnp.clip((first[:, -1] + KEY_TILE - 1) // KEY_TILE, t_low, t_edge)
    t_high = (row0 + BLOCK - 1) // KEY_TILE + 1
    bounds = jnp.stack([t_low, t_clear, t_edge, t_high, row0], axis=1)
    lanes = jnp.concatenate([first, first], axis=1).reshape(4, 1, 2 * BLOCK)
    both = pltpu.with_memory_space_constraint(both, pltpu.HBM)
    attended = attend(bounds, queries, both, lanes)
    return back(attended, w_out, hidden_in)


def solution(mesh):
    in_specs = (
        P(("outer", "inner", "tensor"), None),
        P(),
        P("inner", "tensor"),
        P("inner", "tensor"),
        P("inner", "tensor"),
        P("tensor", None),
        P(("outer", "inner")),
        P(("outer", "inner")),
    )
    out_specs = P(("outer", "inner", "tensor"), None)
    return jax.shard_map(body, mesh=mesh, in_specs=in_specs, out_specs=out_specs, check_vma=False)
```

```python
import functools
import math

import jax
import jax.numpy as jnp
from jax import lax
from jax.experimental import pallas as pl
from jax.experimental.pallas import tpu as pltpu
from jax.sharding import PartitionSpec as P

HEAD_SIZE = 128
BLOCK = 192
SEQUENCE = 12288
KEY_TILE = 1024
KEY_PIECE = 256
MESH = pl.DeviceIdType.MESH
FRONT_COPIES = 190


rope_base = 500000.0
yarn_factor = 8.0
trained_context = 8192.0
beta_fast = 32.0
beta_slow = 1.0
norm_epsilon = 1e-05
masked_score = -1e30


def yarn_inverse(head_dim):
    half_dim = head_dim // 2

    def correction(rotations):
        return (
            head_dim
            * math.log(trained_context / (rotations * 2.0 * math.pi))
            / (2.0 * math.log(rope_base))
        )

    lowest = max(math.floor(correction(beta_fast)), 0)
    highest = min(math.ceil(correction(beta_slow)), head_dim - 1)
    spread = max(highest - lowest, 0.001)
    values = []
    for column in range(half_dim):
        extrapolated = rope_base ** (-2.0 * column / head_dim)
        ramp = min(max((column - lowest) / spread, 0.0), 1.0)
        values.append(extrapolated / yarn_factor * ramp + extrapolated * (1.0 - ramp))
    return values


def place():
    outer, inner, tensor = (lax.axis_index(name) for name in ("outer", "inner", "tensor"))
    return outer, inner % 4, inner // 4, tensor // 2, tensor % 2


def device(x, y, zh, zl, c):
    return (x, zh * 4 + y, zl * 2 + c)


def greet(partners):
    barrier = pltpu.get_barrier_semaphore()
    for partner in partners:
        pl.semaphore_signal(barrier, inc=1, device_id=partner, device_id_type=MESH)
    pl.semaphore_wait(barrier, len(partners))


class Copies:
    def __init__(self, send_sems, recv_sems):
        self.send_sems, self.recv_sems, self.count, self.sent = send_sems, recv_sems, 0, []

    def send(self, src, dst, target):
        copy = pltpu.make_async_remote_copy(
            src_ref=src,
            dst_ref=dst,
            send_sem=self.send_sems.at[self.count],
            recv_sem=self.recv_sems.at[self.count],
            device_id=target,
            device_id_type=MESH,
        )
        self.count += 1
        copy.start()
        self.sent.append(copy)
        return copy

    def finish(self):
        for copy in self.sent:
            copy.wait_send()


def front_kernel(
    hidden_in, gain_in, w_query, w_key, w_value, doc_ids_in, positions_in, inverse_in,
    q_out, both, first_out,
    hidden, gain, doc_ids, positions, inverse, rows, weights_q, weights_kv,
    meta, meta_own, tables, product, kv, q_sum, q_own,
    send_sems, recv_sems, a2a_send, a2a_recv, local_sems,
):
    x, y, zh, zl, c = place()
    p = zh * 2 + zl
    near = lambda q: device(x, y, (q % 8) // 2, q % 2, c)
    right, left = near(p + 1), near(p + 7)
    sibling = device(x, y, zh, zl, 1 - c)
    xs = [(x + k) % 4 for k in range(4)]
    ys = [(y + k) % 4 for k in range(4)]
    y_next, y_far, y_prev = (device(x, ys[k], zh, zl, c) for k in (1, 2, 3))
    x_next, x_far, x_prev = (device(xs[k], y, zh, zl, c) for k in (1, 2, 3))
    columns = [device(x, y, (zh + k) % 4, zl, cc) for k in range(4) for cc in (c, 1 - c)][1:]
    partners = columns + [right, left, y_next, y_prev, y_far, x_next, x_prev, x_far]
    barrier = pltpu.get_barrier_semaphore()
    for partner in partners:
        pl.semaphore_signal(barrier, inc=1, device_id=partner, device_id_type=MESH)
    cp = Copies(send_sems, recv_sems)
    same = lambda ref, target: cp.send(ref, ref, target)
    fetches = [
        pltpu.make_async_copy(source, target, local_sems.at[i])
        for i, (source, target) in enumerate(
            (
                (doc_ids_in, doc_ids),
                (positions_in, positions),
                (hidden_in, hidden),
                (gain_in, gain),
                (inverse_in, inverse),
            )
        )
    ]
    for copy in fetches:
        copy.start()
    fetches[0].wait()
    fetches[1].wait()

    meta_own[...] = jnp.full((8, 128), 99, jnp.int32)
    meta_own[0:1, :] = doc_ids[:, :128]
    meta_own[1:2, :64] = doc_ids[:, 128:]
    meta_own[2:3, :] = positions[:, :128]
    meta_own[3:4, :64] = positions[:, 128:]
    meta[x, y, zh] = meta_own[...]
    for copy in fetches[2:]:
        copy.wait()
    widened = hidden[...].astype(jnp.float32)
    power = jnp.mean(widened * widened, axis=-1, keepdims=True)
    rows[p, c] = (widened * lax.rsqrt(power + norm_epsilon) * gain[...]).astype(jnp.bfloat16)
    pl.semaphore_wait(barrier, len(partners))

    a2a = {0: [], 1: []}
    stores = (weights_q, weights_kv)

    def scatter_weights(i):
        for j in range(2):
            for cc in range(2):
                zt = 2 * c + j
                own = (zt == zh) & (c == cc)
                taken = pl.ds(pl.multiple_of(x * 64, 64), 64)
                if i == 0:
                    source = w_query.at[taken, pl.ds(j * 512 + cc * 256, 256)]
                else:
                    source = (w_value if cc else w_key).at[taken, pl.ds(j * 128, 128)]
                spot = stores[i].at[zh, y, x]
                copy = pltpu.make_async_remote_copy(
                    src_ref=source,
                    dst_ref=spot,
                    send_sem=a2a_send.at[4 * i + 2 * j + cc],
                    recv_sem=a2a_recv.at[4 * i + zh],
                    device_id=device(x, y, zt, zl, cc),
                    device_id_type=MESH,
                )
                stay = pltpu.make_async_copy(source, spot, local_sems.at[i])
                pl.when(own)(stay.start)
                pl.when(jnp.logical_not(own))(copy.start)
                a2a[i].append((own, copy, stay))

    def collect_weights(i):
        for source in range(4):
            spot = stores[i].at[source, y, x]
            arrives = pltpu.make_async_remote_copy(
                src_ref=spot,
                dst_ref=spot,
                send_sem=a2a_send.at[0],
                recv_sem=a2a_recv.at[4 * i + source],
                device_id=sibling,
                device_id_type=MESH,
            )
            own = (zh == source) & (c == zh // 2)
            pl.when(jnp.logical_not(own))(arrives.wait_recv)
        for own, copy, stay in a2a[i]:
            pl.when(own)(stay.wait)

    wy, wy_far, wx, forwards = {}, {}, {0: {}, 1: {}}, {0: [], 1: []}

    def along_y(i):
        mine = stores[i].at[:, y, x]
        wy[i] = same(mine, y_next), same(mine, y_prev)

    def forward_y(i):
        wy[i][0].wait_recv()
        a = same(stores[i].at[pl.ds(0, 2), ys[3], x], y_next)
        wy[i][1].wait_recv()
        wy_far[i] = a, same(stores[i].at[pl.ds(2, 2), ys[1], x], y_prev)

    def along_x(i, k):
        piece = stores[i].at[:, ys[k], x]
        wx[i][k] = same(piece, x_next), same(piece, x_prev)

    def far_y(i):
        for copy in wy_far[i]:
            copy.wait_recv()
        along_x(i, 2)

    def forward_x(i, k):
        a, b = wx[i][k]
        a.wait_recv()
        forwards[i].append(same(stores[i].at[pl.ds(0, 2), ys[k], xs[3]], x_next))
        b.wait_recv()
        forwards[i].append(same(stores[i].at[pl.ds(2, 2), ys[k], xs[1]], x_prev))

    chunks_right = (pl.ds(0, 16), pl.ds(16, 32))
    chunks_left = (pl.ds(32, 16), pl.ds(0, 32))
    to_right, to_left, to_sibling = {}, {}, {}

    def far_spot(q, h, hop):
        if h == 0:
            return rows.at[q, c, pl.ds(0, 16) if hop == 7 else pl.ds(32, 16)]
        return rows.at[q, c, pl.ds(16, 16), pl.ds(0 if hop == 7 else 2048, 2048)]

    def ring(step):
        to_sibling[step] = []
        for h in range(2):
            for to, chunks, target, hop in (
                (to_right, chunks_right, right, 7),
                (to_left, chunks_left, left, 1),
            ):
                to[step, h].wait_recv()
                q = (p + hop * (step + 1)) % 8
                spot = rows.at[q, c, chunks[h]] if step < 3 else far_spot(q, h, hop)
                if step < 2:
                    to[step + 1, h] = same(spot, target)
                elif step == 2:
                    to[3, h] = same(far_spot(q, h, hop), target)
                to_sibling[step].append(same(spot, sibling))

    order = [zh, (zh + 3 + 2 * zl) % 4, (zh + 1 + 2 * zl) % 4, (zh + 2) % 4]

    def tables_of(zb):
        tile = meta[x, y, zb].astype(jnp.float32)
        upper = jnp.broadcast_to(tile[2:3], (128, 128)).T
        lower = jnp.broadcast_to(tile[3:4], (128, 128)).T
        angles = jnp.concatenate([upper, lower[:64]], axis=0) * inverse[...]
        attention_gain = 0.1 * math.log(yarn_factor) + 1.0
        lane = lax.broadcasted_iota(jnp.int32, (BLOCK, HEAD_SIZE), 1)
        sine = jnp.sin(angles) * attention_gain
        tables[0, zb] = jnp.cos(angles) * attention_gain
        tables[1, zb] = jnp.where(lane < HEAD_SIZE // 2, -sine, sine)

    def turn(head, cosine, sine):
        return head * cosine + pltpu.roll(head, HEAD_SIZE // 2, 1) * sine

    def multiply(zb, store, total):
        total[...] = jnp.zeros_like(total)

        @pl.loop(0, 4)
        def _(k):
            piece = store[k].reshape(1024, store.shape[-1])
            depth = pl.ds(pl.multiple_of(k * 1024, 1024), 1024)
            left_side = rows[pl.ds(2 * zb, 2), :, :, depth].reshape(BLOCK, 1024)
            total[...] += jnp.dot(left_side, piece, preferred_element_type=jnp.float32)

    q_stay = []

    def queries_of(s):
        zb = order[s]
        multiply(zb, weights_q, q_sum)
        for h in range(2):
            at = pl.ds(h * HEAD_SIZE, HEAD_SIZE)
            q_own[s, :, at] = turn(q_sum[:, at], tables[0, zb], tables[1, zb]).astype(jnp.bfloat16)
        q_stay.append(pltpu.make_async_copy(q_own.at[s], q_out.at[zb], local_sems.at[5 + s]))
        q_stay[-1].start()

    halves = (pl.ds(0, 96), pl.ds(96, 96))
    cell = lambda s, i, k: both.at[c, xs[i], order[s], ys[k]]
    side = lambda s, i, k, f: both.at[c, xs[i], order[s], ys[k], halves[f]]
    kx, kx_far, ky, ky_far, kv_stay, siblings = {}, {}, {}, {}, [], []
    is_key = c == 0

    def key_start(s):
        zb = order[s]
        for copy in to_sibling[s]:
            copy.wait_recv()
        multiply(zb, weights_kv, product)
        cosine = jnp.where(is_key, tables[0, zb], 1.0)
        sine = jnp.where(is_key, tables[1, zb], 0.0)
        kv[s] = turn(product[...], cosine, sine).astype(jnp.bfloat16)
        own, spot = kv.at[s], cell(s, 0, 0)
        kx[s] = cp.send(own, spot, x_next), cp.send(own, spot, x_prev)
        ky[s, 0] = cp.send(own, spot, y_next), cp.send(own, spot, y_prev)
        siblings.append(cp.send(own, spot, sibling))
        kv_stay.append(pltpu.make_async_copy(own, spot, local_sems.at[9 + s]))
        kv_stay[-1].start()

    def key_along_y(s, i):
        ky[s, i] = same(cell(s, i, 0), y_next), same(cell(s, i, 0), y_prev)
        siblings.append(same(cell(s, i, 0), sibling))

    def key_x(s):
        kx[s][0].wait_recv()
        a = same(side(s, 3, 0, 0), x_next)
        kx[s][1].wait_recv()
        kx_far[s] = a, same(side(s, 1, 0, 1), x_prev)
        key_along_y(s, 3)
        key_along_y(s, 1)

    def key_x_far(s):
        for copy in kx_far[s]:
            copy.wait_recv()
        key_along_y(s, 2)

    def key_y(s, i):
        ky[s, i][0].wait_recv()
        a = same(side(s, i, 3, 0), y_next)
        ky[s, i][1].wait_recv()
        ky_far[s, i] = a, same(side(s, i, 1, 1), y_prev)

    def share(s, k):
        siblings.append(same(both.at[c, :, order[s], ys[k]], sibling))

    def key_y_rest(s):
        key_y(s, 2)
        share(s, 3)
        share(s, 1)

    def key_end(s):
        for i in range(4):
            for copy in ky_far[s, i]:
                copy.wait_recv()
        share(s, 2)

    scatter_weights(1)
    meta_z = [
        cp.send(meta_own, meta.at[x, y, zh], device(x, y, (zh + k) % 4, zl, c)) for k in (1, 2, 3)
    ]
    for h in range(2):
        to_right[0, h] = same(rows.at[p, c, chunks_right[h]], right)
        to_left[0, h] = same(rows.at[p, c, chunks_left[h]], left)
    scatter_weights(0)
    own_to_sibling = same(rows.at[p, c], sibling)
    collect_weights(1)
    along_y(1)
    along_x(1, 0)
    forward_y(1)
    along_x(1, 3)
    along_x(1, 1)
    collect_weights(0)
    along_y(0)
    for copy in meta_z:
        copy.wait_recv()
    mine = meta.at[x, y]
    meta_y = [same(mine, target) for target in (y_next, y_far, y_prev)]
    forward_x(1, 0)
    far_y(1)
    tables_of(order[0])
    ring(0)
    forward_x(1, 3)
    forward_x(1, 1)
    along_x(0, 0)
    forward_y(0)
    along_x(0, 3)
    along_x(0, 1)
    forward_x(1, 2)
    far_y(0)
    tables_of(order[1])
    for copy in forwards[1]:
        copy.wait_recv()
    own_to_sibling.wait_recv()
    key_start(0)
    for copy in meta_y:
        copy.wait_recv()
    mine = meta.at[x]
    meta_x = [same(mine, target) for target in (x_next, x_far, x_prev)]
    tables_of(order[2])
    ring(1)
    key_x(0)
    forward_x(0, 0)
    key_start(1)
    key_y(0, 0)
    key_x_far(0)
    forward_x(0, 3)
    tables_of(order[3])
    key_x(1)
    key_y(0, 3)
    key_y(0, 1)
    forward_x(0, 1)
    ring(2)
    key_y(1, 0)
    key_x_far(1)
    key_y_rest(0)
    key_start(2)
    forward_x(0, 2)
    key_y(1, 3)
    key_y(1, 1)
    key_end(0)
    key_x(2)
    key_y_rest(1)
    key_y(2, 0)
    key_x_far(2)
    for copy in forwards[0]:
        copy.wait_recv()
    queries_of(0)
    ring(3)
    key_y(2, 3)
    key_y(2, 1)
    key_start(3)
    key_end(1)
    key_y_rest(2)
    queries_of(1)
    key_x(3)
    key_y(3, 0)
    key_end(2)
    queries_of(2)
    key_x_far(3)
    key_y(3, 3)
    key_y(3, 1)
    queries_of(3)
    key_y_rest(3)
    for copy in meta_x:
        copy.wait_recv()
    everything = meta[...].reshape(64, 8, 128)
    line = lax.broadcasted_iota(jnp.int32, (8, 128), 0)
    firsts = []
    for d in range(1, 6):
        hits = jnp.sum(jnp.where(everything < d, 1, 0), axis=0)
        hits = jnp.where(line < 2, hits, 0).astype(jnp.float32)
        firsts.append(jnp.sum(jnp.sum(hits, axis=0, keepdims=True), axis=1, keepdims=True))
    for zb in range(4):
        documents = meta[x, y, zb][0:2]
        first = jnp.zeros((2, 128), jnp.float32)
        for d in range(1, 6):
            first = jnp.where(documents == d, firsts[d - 1], first)
        first_out[2 * zb : 2 * zb + 2, :] = first.astype(jnp.int32)
    key_end(3)
    for copy in siblings:
        copy.wait_recv()
    for copy in q_stay + kv_stay:
        copy.wait()
    for i in range(2):
        for own, copy, _ in a2a[i]:
            pl.when(jnp.logical_not(own))(copy.wait_send)
    cp.finish()
    assert cp.count == FRONT_COPIES, cp.count


def front(hidden, gain, w_query, w_key, w_value, doc_ids, positions, inverse):
    outside = pl.BlockSpec(memory_space=pltpu.HBM)
    inside = pl.BlockSpec(memory_space=pltpu.VMEM)
    return pl.pallas_call(
        front_kernel,
        out_shape=(
            jax.ShapeDtypeStruct((4, BLOCK, 2 * HEAD_SIZE), jnp.bfloat16),
            jax.ShapeDtypeStruct((2, 4, 4, 4, BLOCK, HEAD_SIZE), jnp.bfloat16),
            jax.ShapeDtypeStruct((8, 128), jnp.int32),
        ),
        in_specs=[outside] * 8,
        out_specs=(outside, outside, inside),
        scratch_shapes=[
            pltpu.VMEM((48, 4096), jnp.bfloat16),
            pltpu.VMEM((1, 4096), jnp.float32),
            pltpu.VMEM((1, BLOCK), jnp.int32),
            pltpu.VMEM((1, BLOCK), jnp.int32),
            pltpu.VMEM((1, HEAD_SIZE), jnp.float32),
            pltpu.VMEM((8, 2, 48, 4096), jnp.bfloat16),
            pltpu.VMEM((4, 4, 4, 64, 256), jnp.bfloat16),
            pltpu.VMEM((4, 4, 4, 64, 128), jnp.bfloat16),
            pltpu.VMEM((4, 4, 4, 8, 128), jnp.int32),
            pltpu.VMEM((8, 128), jnp.int32),
            pltpu.VMEM((2, 4, BLOCK, HEAD_SIZE), jnp.float32),
            pltpu.VMEM((BLOCK, HEAD_SIZE), jnp.float32),
            pltpu.VMEM((4, BLOCK, HEAD_SIZE), jnp.bfloat16),
            pltpu.VMEM((BLOCK, 2 * HEAD_SIZE), jnp.float32),
            pltpu.VMEM((4, BLOCK, 2 * HEAD_SIZE), jnp.bfloat16),
            pltpu.SemaphoreType.DMA((FRONT_COPIES,)),
            pltpu.SemaphoreType.DMA((FRONT_COPIES,)),
            pltpu.SemaphoreType.DMA((8,)),
            pltpu.SemaphoreType.DMA((8,)),
            pltpu.SemaphoreType.DMA((13,)),
        ],
        compiler_params=pltpu.CompilerParams(
            collective_id=0, has_side_effects=True, vmem_limit_bytes=55 << 20
        ),
        name="front",
    )(
        *(
            pltpu.with_memory_space_constraint(a, pltpu.HBM)
            for a in (hidden, gain, w_query, w_key, w_value, doc_ids, positions, inverse)
        )
    )


def attend_kernel(bounds, q_ref, both_in, first_ref, out_ref, even, odd, summed):
    both_ref = both_in.reshape(2, SEQUENCE, HEAD_SIZE)
    block = pl.program_id(0)
    t_low, t_clear, t_edge, t_high, row0 = (bounds[block, i] for i in range(5))
    scale = HEAD_SIZE ** (-0.5) * math.log2(math.e)
    width = 2 * BLOCK
    queries = jnp.concatenate([q_ref[0, :, :HEAD_SIZE], q_ref[0, :, HEAD_SIZE:]], axis=0)
    summed[...] = jnp.zeros_like(summed)

    half = KEY_TILE // 2

    def produce(store, begin, masked):
        peak = None
        for u in range(half // KEY_PIECE):
            first_key = begin + u * KEY_PIECE
            keys = both_ref[0, pl.ds(pl.multiple_of(first_key, KEY_PIECE), KEY_PIECE), :]
            piece = lax.dot_general(
                keys, queries, (((1,), (1,)), ((), ())), preferred_element_type=jnp.float32
            )
            if masked:
                key = first_key + lax.broadcasted_iota(jnp.int32, (KEY_PIECE, width), 0)
                lane = lax.broadcasted_iota(jnp.int32, (1, width), 1)
                query = row0 + jnp.where(lane < BLOCK, lane, lane - BLOCK)
                allowed = (key <= query) & (key >= first_ref[0])
                piece = jnp.where(allowed, piece, masked_score)
            store[u * KEY_PIECE : (u + 1) * KEY_PIECE, :] = piece
            top = jnp.max(piece.reshape(KEY_PIECE // 8, 8, width), axis=0)
            peak = top if peak is None else jnp.maximum(peak, top)
        return peak

    def consume(store, begin, peak, total, fresh):
        latest = jnp.maximum(peak, jnp.max(fresh, axis=0, keepdims=True))
        shrink = jnp.exp2((peak - latest) * scale)
        total = total * shrink
        offset = latest * scale
        gained = None
        for u in range(half // KEY_PIECE):
            weights = jnp.exp2(store[u * KEY_PIECE : (u + 1) * KEY_PIECE, :] * scale - offset)
            total = total + jnp.sum(weights.reshape(KEY_PIECE // 8, 8, width), axis=0)
            values = both_ref[1, pl.ds(pl.multiple_of(begin + u * KEY_PIECE, KEY_PIECE), KEY_PIECE), :]
            term = lax.dot_general(
                values, weights.astype(jnp.bfloat16), (((0,), (0,)), ((), ())),
                preferred_element_type=jnp.float32,
            )
            gained = term if gained is None else gained + term
        summed[...] = summed[...] * shrink + gained
        return latest, total

    def step(masked, t, carry):
        peak, total, fresh = carry
        begin = t * KEY_TILE
        following = produce(even, begin, masked)
        peak, total = consume(odd, begin - half, peak, total, fresh)
        fresh = produce(odd, begin + half, masked)
        peak, total = consume(even, begin, peak, total, following)
        return peak, total, fresh

    begin = t_low * KEY_TILE
    peak, total = jnp.full((1, width), masked_score, jnp.float32), jnp.zeros((8, width), jnp.float32)
    following = produce(even, begin, True)
    fresh = produce(odd, begin + half, True)
    peak, total = consume(even, begin, peak, total, following)
    carry = (peak, total, fresh)
    start = t_low + 1
    carry = lax.fori_loop(start, t_clear, functools.partial(step, True), carry)
    carry = lax.fori_loop(jnp.maximum(t_clear, start), t_edge, functools.partial(step, False), carry)
    carry = lax.fori_loop(jnp.maximum(t_edge, start), t_high, functools.partial(step, True), carry)
    peak, total = consume(odd, t_high * KEY_TILE - half, *carry)
    total = jnp.sum(total, axis=0, keepdims=True)
    result = (summed[...] / total).T
    out_ref[0, :, :HEAD_SIZE] = result[:BLOCK].astype(jnp.bfloat16)
    out_ref[0, :, HEAD_SIZE:] = result[BLOCK:].astype(jnp.bfloat16)


def attend(bounds, queries, both, first):
    return pl.pallas_call(
        attend_kernel,
        out_shape=jax.ShapeDtypeStruct((4, BLOCK, 2 * HEAD_SIZE), jnp.bfloat16),
        grid_spec=pltpu.PrefetchScalarGridSpec(
            num_scalar_prefetch=1,
            grid=(4,),
            in_specs=[
                pl.BlockSpec((1, BLOCK, 2 * HEAD_SIZE), lambda i, b: (i, 0, 0)),
                pl.BlockSpec(memory_space=pltpu.VMEM),
                pl.BlockSpec((1, 1, 2 * BLOCK), lambda i, b: (i, 0, 0)),
            ],
            out_specs=pl.BlockSpec((1, BLOCK, 2 * HEAD_SIZE), lambda i, b: (i, 0, 0)),
            scratch_shapes=[
                pltpu.VMEM((KEY_TILE // 2, 2 * BLOCK), jnp.float32),
                pltpu.VMEM((KEY_TILE // 2, 2 * BLOCK), jnp.float32),
                pltpu.VMEM((HEAD_SIZE, 2 * BLOCK), jnp.float32),
            ],
        ),
        compiler_params=pltpu.CompilerParams(vmem_limit_bytes=16 << 20),
        name="attend",
    )(bounds, queries, both, first)


def back_kernel(
    own, w_out, hidden, out,
    attended, weights, mine, given, landed, joined, arrived,
    send_sems, recv_sems, local_sems, step_send, step_recv,
):
    x, y, zh, zl, c = place()
    cz = zh // 2
    sibling, across = device(x, y, zh, zl, 1 - c), device(x, y, zh, 1 - zl, c)
    partners = [device(x, y, (zh + k) % 4, zl, cc) for k in range(4) for cc in (c, 1 - c)][1:]
    partners.append(across)
    pieces = 4
    width = 4096 // pieces
    cut = lambda i: pl.ds(i * width, width)
    fetch = [
        pltpu.make_async_copy(w_out.at[:, cut(i)], weights.at[:, cut(i)], local_sems.at[1 + i])
        for i in range(pieces)
    ]
    for copy in fetch:
        copy.start()
    greet(partners)
    spot = lambda j, cc: attended.at[:, pl.ds(pl.multiple_of((2 * j + cc) * 256, 256), 256)]
    copies = []
    here = cz == c
    for k in (2, 1, 3, 0):
        zt = (zh + k) % 4
        copy = pltpu.make_async_remote_copy(
            src_ref=own.at[zt],
            dst_ref=spot(zh % 2, c),
            send_sem=send_sems.at[k],
            recv_sem=recv_sems.at[(zh % 2) * 2 + c],
            device_id=device(x, y, zt, zl, cz),
            device_id_type=MESH,
        )
        if k == 0:
            stay = pltpu.make_async_copy(own.at[zt], spot(zh % 2, c), local_sems.at[0])
            pl.when(here)(stay.start)
            pl.when(jnp.logical_not(here))(copy.start)
        else:
            copy.start()
        copies.append(copy)
    for j in range(2):
        for cc in range(2):
            arrives = pltpu.make_async_remote_copy(
                src_ref=own.at[0],
                dst_ref=spot(j, cc),
                send_sem=send_sems.at[0],
                recv_sem=recv_sems.at[2 * j + cc],
                device_id=sibling,
                device_id_type=MESH,
            )
            local = (zh == 2 * c + j) & (c == cc)
            pl.when(jnp.logical_not(local))(arrives.wait_recv)
    pl.when(here)(stay.wait)

    cp = Copies(step_send, step_recv)
    to_sibling, to_across = [], []

    def pass_on(i):
        to_sibling[i].wait_recv()
        joined[i] = (mine[i, 1 - zl] + landed[i, 1 - zl].astype(jnp.float32)).astype(jnp.bfloat16)
        to_across.append(cp.send(joined.at[i], arrived.at[i], across))

    for i in range(pieces):
        fetch[i].wait()
        term = jnp.dot(attended[...], weights[:, cut(i)], preferred_element_type=jnp.float32)
        term = term.reshape(2, 2, 48, width)
        mine[i] = jnp.where(c == 0, term[:, 0], term[:, 1])
        given[i] = jnp.where(c == 0, term[:, 1], term[:, 0]).astype(jnp.bfloat16)
        to_sibling.append(cp.send(given.at[i], landed.at[i], sibling))
        if i > 0:
            pass_on(i - 1)
    pass_on(pieces - 1)
    for i in range(pieces):
        total = mine[i, zl] + landed[i, zl].astype(jnp.float32)
        to_across[i].wait_recv()
        total = total + arrived[i].astype(jnp.float32)
        out[:, cut(i)] = (hidden[:, cut(i)].astype(jnp.float32) + total).astype(jnp.bfloat16)
    pl.when(jnp.logical_not(here))(copies[-1].wait_send)
    for copy in copies[:-1]:
        copy.wait_send()
    cp.finish()


def back(own, w_out, hidden):
    anywhere = pl.BlockSpec(memory_space=pl.ANY)
    inside = pl.BlockSpec(memory_space=pltpu.VMEM)
    return pl.pallas_call(
        back_kernel,
        out_shape=jax.ShapeDtypeStruct((48, 4096), jnp.bfloat16),
        in_specs=[anywhere, anywhere, inside],
        out_specs=inside,
        scratch_shapes=[
            pltpu.VMEM((BLOCK, 1024), jnp.bfloat16),
            pltpu.VMEM((1024, 4096), jnp.bfloat16),
            pltpu.VMEM((4, 2, 48, 1024), jnp.float32),
            pltpu.VMEM((4, 2, 48, 1024), jnp.bfloat16),
            pltpu.VMEM((4, 2, 48, 1024), jnp.bfloat16),
            pltpu.VMEM((4, 48, 1024), jnp.bfloat16),
            pltpu.VMEM((4, 48, 1024), jnp.bfloat16),
            pltpu.SemaphoreType.DMA((4,)),
            pltpu.SemaphoreType.DMA((4,)),
            pltpu.SemaphoreType.DMA((5,)),
            pltpu.SemaphoreType.DMA((8,)),
            pltpu.SemaphoreType.DMA((8,)),
        ],
        compiler_params=pltpu.CompilerParams(
            collective_id=1, has_side_effects=True, vmem_limit_bytes=32 << 20
        ),
        name="back",
    )(own, w_out, hidden)


def body(hidden_in, norm_gain, w_query, w_key, value_weight, w_out, doc_ids, positions):
    x, y, zh, zl, c = place()
    inverse = yarn_inverse(HEAD_SIZE)
    queries, both, first = front(
        hidden_in,
        norm_gain.reshape(1, 4096),
        w_query,
        w_key,
        value_weight,
        doc_ids.reshape(1, BLOCK),
        positions.reshape(1, BLOCK),
        jnp.asarray([inverse + inverse], dtype=jnp.float32),
    )
    first = first.reshape(4, 256)[:, :BLOCK]
    row0 = (x * 16 + jnp.arange(4, dtype=jnp.int32) * 4 + y) * BLOCK
    t_low = first[:, 0] // KEY_TILE
    t_edge = jnp.maximum((row0 + 1) // KEY_TILE, t_low)
    t_clear = jnp.clip((first[:, -1] + KEY_TILE - 1) // KEY_TILE, t_low, t_edge)
    t_high = (row0 + BLOCK - 1) // KEY_TILE + 1
    bounds = jnp.stack([t_low, t_clear, t_edge, t_high, row0], axis=1)
    lanes = jnp.concatenate([first, first], axis=1).reshape(4, 1, 2 * BLOCK)
    queries, both, w_out = (
        pltpu.with_memory_space_constraint(a, pltpu.HBM) for a in (queries, both, w_out)
    )
    attended = attend(bounds, queries, both, lanes)
    return back(attended, w_out, hidden_in)


def solution(mesh):
    in_specs = (
        P(("outer", "inner", "tensor"), None),
        P(),
        P("inner", "tensor"),
        P("inner", "tensor"),
        P("inner", "tensor"),
        P("tensor", None),
        P(("outer", "inner")),
        P(("outer", "inner")),
    )
    out_specs = P(("outer", "inner", "tensor"), None)
    return jax.shard_map(body, mesh=mesh, in_specs=in_specs, out_specs=out_specs, check_vma=False)
```

```python
import functools
import math

import jax
import jax.numpy as jnp
from jax import lax
from jax.experimental import pallas as pl
from jax.experimental.pallas import tpu as pltpu
from jax.sharding import PartitionSpec as P

HEAD_SIZE = 128
BLOCK = 192
SEQUENCE = 12288
KEY_TILE = 1024
KEY_PIECE = 256
MESH = pl.DeviceIdType.MESH
FRONT_COPIES = 190


rope_base = 500000.0
yarn_factor = 8.0
trained_context = 8192.0
beta_fast = 32.0
beta_slow = 1.0
norm_epsilon = 1e-05
masked_score = -1e30


def yarn_inverse(head_dim):
    half_dim = head_dim // 2

    def correction(rotations):
        return (
            head_dim
            * math.log(trained_context / (rotations * 2.0 * math.pi))
            / (2.0 * math.log(rope_base))
        )

    lowest = max(math.floor(correction(beta_fast)), 0)
    highest = min(math.ceil(correction(beta_slow)), head_dim - 1)
    spread = max(highest - lowest, 0.001)
    values = []
    for column in range(half_dim):
        extrapolated = rope_base ** (-2.0 * column / head_dim)
        ramp = min(max((column - lowest) / spread, 0.0), 1.0)
        values.append(extrapolated / yarn_factor * ramp + extrapolated * (1.0 - ramp))
    return values


def place():
    outer, inner, tensor = (lax.axis_index(name) for name in ("outer", "inner", "tensor"))
    return outer, inner % 4, inner // 4, tensor // 2, tensor % 2


def device(x, y, zh, zl, c):
    return (x, zh * 4 + y, zl * 2 + c)


def greet(partners):
    barrier = pltpu.get_barrier_semaphore()
    for partner in partners:
        pl.semaphore_signal(barrier, inc=1, device_id=partner, device_id_type=MESH)
    pl.semaphore_wait(barrier, len(partners))


class Copies:
    def __init__(self, send_sems, recv_sems):
        self.send_sems, self.recv_sems, self.count, self.sent = send_sems, recv_sems, 0, []

    def send(self, src, dst, target):
        copy = pltpu.make_async_remote_copy(
            src_ref=src,
            dst_ref=dst,
            send_sem=self.send_sems.at[self.count],
            recv_sem=self.recv_sems.at[self.count],
            device_id=target,
            device_id_type=MESH,
        )
        self.count += 1
        copy.start()
        self.sent.append(copy)
        return copy

    def finish(self):
        for copy in self.sent:
            copy.wait_send()


def front_kernel(
    hidden_in, gain_in, w_query, w_key, w_value, doc_ids_in, positions_in, inverse_in,
    q_out, both, first_out,
    hidden, gain, doc_ids, positions, inverse, rows, weights_q, weights_kv,
    meta, meta_own, tables, product, kv, q_sum, q_own,
    send_sems, recv_sems, a2a_send, a2a_recv, local_sems,
):
    x, y, zh, zl, c = place()
    p = zh * 2 + zl
    near = lambda q: device(x, y, (q % 8) // 2, q % 2, c)
    right, left = near(p + 1), near(p + 7)
    sibling = device(x, y, zh, zl, 1 - c)
    xs = [(x + k) % 4 for k in range(4)]
    ys = [(y + k) % 4 for k in range(4)]
    y_next, y_far, y_prev = (device(x, ys[k], zh, zl, c) for k in (1, 2, 3))
    x_next, x_far, x_prev = (device(xs[k], y, zh, zl, c) for k in (1, 2, 3))
    columns = [device(x, y, (zh + k) % 4, zl, cc) for k in range(4) for cc in (c, 1 - c)][1:]
    partners = columns + [right, left, y_next, y_prev, y_far, x_next, x_prev, x_far]
    barrier = pltpu.get_barrier_semaphore()
    for partner in partners:
        pl.semaphore_signal(barrier, inc=1, device_id=partner, device_id_type=MESH)
    cp = Copies(send_sems, recv_sems)
    same = lambda ref, target: cp.send(ref, ref, target)
    fetches = [
        pltpu.make_async_copy(source, target, local_sems.at[i])
        for i, (source, target) in enumerate(
            (
                (doc_ids_in, doc_ids),
                (positions_in, positions),
                (hidden_in, hidden),
                (gain_in, gain),
                (inverse_in, inverse),
            )
        )
    ]
    for copy in fetches:
        copy.start()
    fetches[0].wait()
    fetches[1].wait()

    meta_own[...] = jnp.full((8, 128), 99, jnp.int32)
    meta_own[0:1, :] = doc_ids[:, :128]
    meta_own[1:2, :64] = doc_ids[:, 128:]
    meta_own[2:3, :] = positions[:, :128]
    meta_own[3:4, :64] = positions[:, 128:]
    meta[x, y, zh] = meta_own[...]
    for copy in fetches[2:]:
        copy.wait()
    widened = hidden[...].astype(jnp.float32)
    power = jnp.mean(widened * widened, axis=-1, keepdims=True)
    rows[p, c] = (widened * lax.rsqrt(power + norm_epsilon) * gain[...]).astype(jnp.bfloat16)
    pl.semaphore_wait(barrier, len(partners))

    a2a = {0: [], 1: []}
    stores = (weights_q, weights_kv)

    def scatter_weights(i):
        for j in range(2):
            for cc in range(2):
                zt = 2 * c + j
                own = (zt == zh) & (c == cc)
                taken = pl.ds(pl.multiple_of(x * 64, 64), 64)
                if i == 0:
                    source = w_query.at[taken, pl.ds(j * 512 + cc * 256, 256)]
                else:
                    source = (w_value if cc else w_key).at[taken, pl.ds(j * 128, 128)]
                spot = stores[i].at[zh, y, x]
                copy = pltpu.make_async_remote_copy(
                    src_ref=source,
                    dst_ref=spot,
                    send_sem=a2a_send.at[4 * i + 2 * j + cc],
                    recv_sem=a2a_recv.at[4 * i + zh],
                    device_id=device(x, y, zt, zl, cc),
                    device_id_type=MESH,
                )
                stay = pltpu.make_async_copy(source, spot, local_sems.at[i])
                pl.when(own)(stay.start)
                pl.when(jnp.logical_not(own))(copy.start)
                a2a[i].append((own, copy, stay))

    def collect_weights(i):
        for source in range(4):
            spot = stores[i].at[source, y, x]
            arrives = pltpu.make_async_remote_copy(
                src_ref=spot,
                dst_ref=spot,
                send_sem=a2a_send.at[0],
                recv_sem=a2a_recv.at[4 * i + source],
                device_id=sibling,
                device_id_type=MESH,
            )
            own = (zh == source) & (c == zh // 2)
            pl.when(jnp.logical_not(own))(arrives.wait_recv)
        for own, copy, stay in a2a[i]:
            pl.when(own)(stay.wait)

    wy, wy_far, wx, forwards = {}, {}, {}, {0: [], 1: []}

    def along_y(i):
        mine = stores[i].at[:, y, x]
        wy[i] = same(mine, y_next), same(mine, y_prev)

    def forward_y(i, side):
        wy[i][side].wait_recv()
        spot = stores[i].at[pl.ds(2 * side, 2), ys[3 - 2 * side], x]
        wy_far[i, side] = same(spot, (y_next, y_prev)[side])

    def along_x(i, k):
        piece = stores[i].at[:, ys[k], x]
        wx[i, k] = same(piece, x_next), same(piece, x_prev)

    def far_y(i):
        wy_far[i, 0].wait_recv()
        wy_far[i, 1].wait_recv()
        along_x(i, 2)

    def forward_x(i, k, side):
        wx[i, k][side].wait_recv()
        spot = stores[i].at[pl.ds(2 * side, 2), ys[k], xs[3 - 2 * side]]
        forwards[i].append(same(spot, (x_next, x_prev)[side]))

    chunks_right = (pl.ds(0, 16), pl.ds(16, 32))
    chunks_left = (pl.ds(32, 16), pl.ds(0, 32))
    to_right, to_left, to_sibling, own_row = {}, {}, {k: [] for k in range(4)}, []

    def far_spot(q, h, hop):
        if h == 0:
            return rows.at[q, c, pl.ds(0, 16) if hop == 7 else pl.ds(32, 16)]
        return rows.at[q, c, pl.ds(16, 16), pl.ds(0 if hop == 7 else 2048, 2048)]

    def ring_start(h):
        to_right[0, h] = same(rows.at[p, c, chunks_right[h]], right)
        to_left[0, h] = same(rows.at[p, c, chunks_left[h]], left)

    def own_start():
        own_row.append(same(rows.at[p, c], sibling))

    def ring(step, h, side):
        to, chunks, target, hop = (
            (to_right, chunks_right, right, 7),
            (to_left, chunks_left, left, 1),
        )[side]
        to[step, h].wait_recv()
        q = (p + hop * (step + 1)) % 8
        spot = rows.at[q, c, chunks[h]] if step < 3 else far_spot(q, h, hop)
        if step < 2:
            to[step + 1, h] = same(spot, target)
        elif step == 2:
            to[3, h] = same(far_spot(q, h, hop), target)
        to_sibling[step].append(same(spot, sibling))

    metas = {}

    def meta_start():
        metas[0] = [
            cp.send(meta_own, meta.at[x, y, zh], device(x, y, (zh + k) % 4, zl, c))
            for k in (1, 2, 3)
        ]

    def meta_along_y():
        for copy in metas[0]:
            copy.wait_recv()
        mine = meta.at[x, y]
        metas[1] = [same(mine, target) for target in (y_next, y_far, y_prev)]

    def meta_along_x():
        for copy in metas[1]:
            copy.wait_recv()
        mine = meta.at[x]
        metas[2] = [same(mine, target) for target in (x_next, x_far, x_prev)]

    order = [zh, (zh + 3 + 2 * zl) % 4, (zh + 1 + 2 * zl) % 4, (zh + 2) % 4]

    def tables_of(zb):
        tile = meta[x, y, zb].astype(jnp.float32)
        upper = jnp.broadcast_to(tile[2:3], (128, 128)).T
        lower = jnp.broadcast_to(tile[3:4], (128, 128)).T
        angles = jnp.concatenate([upper, lower[:64]], axis=0) * inverse[...]
        attention_gain = 0.1 * math.log(yarn_factor) + 1.0
        lane = lax.broadcasted_iota(jnp.int32, (BLOCK, HEAD_SIZE), 1)
        sine = jnp.sin(angles) * attention_gain
        tables[0, zb] = jnp.cos(angles) * attention_gain
        tables[1, zb] = jnp.where(lane < HEAD_SIZE // 2, -sine, sine)

    def turn(head, cosine, sine):
        return head * cosine + pltpu.roll(head, HEAD_SIZE // 2, 1) * sine

    def multiply(zb, store, total):
        total[...] = jnp.zeros_like(total)

        @pl.loop(0, 4)
        def _(k):
            piece = store[k].reshape(1024, store.shape[-1])
            depth = pl.ds(pl.multiple_of(k * 1024, 1024), 1024)
            left_side = rows[pl.ds(2 * zb, 2), :, :, depth].reshape(BLOCK, 1024)
            total[...] += jnp.dot(left_side, piece, preferred_element_type=jnp.float32)

    q_stay = []

    def queries_of(s):
        zb = order[s]
        if not q_stay:
            for copy in forwards[0]:
                copy.wait_recv()
        multiply(zb, weights_q, q_sum)
        for h in range(2):
            at = pl.ds(h * HEAD_SIZE, HEAD_SIZE)
            q_own[s, :, at] = turn(q_sum[:, at], tables[0, zb], tables[1, zb]).astype(jnp.bfloat16)
        q_stay.append(pltpu.make_async_copy(q_own.at[s], q_out.at[zb], local_sems.at[5 + s]))
        q_stay[-1].start()

    halves = (pl.ds(0, 96), pl.ds(96, 96))
    cell = lambda s, i, k: both.at[c, xs[i], order[s], ys[k]]
    side_of = lambda s, i, k, f: both.at[c, xs[i], order[s], ys[k], halves[f]]
    kx, kx_far, ky, ky_far, kv_stay, siblings = {}, {}, {}, {}, [], []
    is_key = c == 0

    def key_start(s):
        zb = order[s]
        for copy in to_sibling[s] + (forwards[1] + own_row if s == 0 else []):
            copy.wait_recv()
        multiply(zb, weights_kv, product)
        cosine = jnp.where(is_key, tables[0, zb], 1.0)
        sine = jnp.where(is_key, tables[1, zb], 0.0)
        kv[s] = turn(product[...], cosine, sine).astype(jnp.bfloat16)
        own, spot = kv.at[s], cell(s, 0, 0)
        kx[s] = cp.send(own, spot, x_next), cp.send(own, spot, x_prev)
        ky[s, 0] = cp.send(own, spot, y_next), cp.send(own, spot, y_prev)
        siblings.append(cp.send(own, spot, sibling))
        kv_stay.append(pltpu.make_async_copy(own, spot, local_sems.at[9 + s]))
        kv_stay[-1].start()

    def key_along_y(s, i):
        ky[s, i] = same(cell(s, i, 0), y_next), same(cell(s, i, 0), y_prev)
        siblings.append(same(cell(s, i, 0), sibling))

    def key_x(s, side):
        kx[s][side].wait_recv()
        spot = side_of(s, 3 - 2 * side, 0, side)
        kx_far[s, side] = same(spot, (x_next, x_prev)[side])
        key_along_y(s, 3 - 2 * side)

    def key_x_far(s):
        kx_far[s, 0].wait_recv()
        kx_far[s, 1].wait_recv()
        key_along_y(s, 2)

    def key_y(s, i, side):
        ky[s, i][side].wait_recv()
        spot = side_of(s, i, 3 - 2 * side, side)
        ky_far[s, i, side] = same(spot, (y_next, y_prev)[side])

    def share(s, k):
        siblings.append(same(both.at[c, :, order[s], ys[k]], sibling))

    def key_end(s):
        for i in range(4):
            for side in range(2):
                ky_far[s, i, side].wait_recv()
        share(s, 2)

    scatter_weights(1)
    meta_start()
    scatter_weights(0)
    ring_start(0)
    ring_start(1)
    collect_weights(1)
    along_y(1)
    along_x(1, 0)
    forward_y(1, 0)
    own_start()
    along_x(1, 3)
    collect_weights(0)
    ring(0, 0, 0)
    forward_x(1, 0, 1)
    forward_y(1, 1)
    along_x(1, 1)
    forward_x(1, 0, 0)
    along_y(0)
    meta_along_y()
    ring(0, 0, 1)
    forward_x(1, 3, 1)
    far_y(1)
    ring(0, 1, 0)
    along_x(0, 0)
    forward_x(1, 2, 0)
    forward_x(1, 1, 0)
    forward_y(0, 1)
    forward_x(1, 3, 0)
    ring(1, 0, 0)
    ring(0, 1, 1)
    forward_x(1, 1, 1)
    forward_x(1, 2, 1)
    along_x(0, 1)
    tables_of(order[0])
    forward_y(0, 0)
    ring(1, 0, 1)
    tables_of(order[1])
    key_start(0)
    ring(1, 1, 0)
    far_y(0)
    along_x(0, 3)
    key_y(0, 0, 0)
    ring(2, 0, 0)
    ring(1, 1, 1)
    key_x(0, 0)
    key_x(0, 1)
    key_y(0, 0, 1)
    key_start(1)
    key_y(0, 3, 0)
    ring(2, 1, 0)
    forward_x(0, 3, 0)
    forward_x(0, 1, 1)
    ring(2, 0, 1)
    key_y(0, 1, 1)
    key_x_far(0)
    key_x(1, 0)
    key_x(1, 1)
    ring(2, 1, 1)
    key_y(0, 1, 0)
    key_y(0, 3, 1)
    key_y(1, 0, 1)
    ring(3, 0, 0)
    tables_of(order[2])
    forward_x(0, 2, 1)
    key_x_far(1)
    key_y(0, 2, 0)
    key_y(0, 2, 1)
    forward_x(0, 1, 0)
    key_y(1, 3, 0)
    key_start(2)
    forward_x(0, 0, 0)
    key_y(1, 1, 0)
    ring(3, 1, 0)
    key_y(1, 3, 1)
    ring(3, 1, 1)
    key_y(1, 2, 0)
    forward_x(0, 3, 1)
    key_y(1, 1, 1)
    ring(3, 0, 1)
    key_y(1, 2, 1)
    key_y(1, 0, 0)
    tables_of(order[3])
    share(0, 1)
    key_x(2, 0)
    key_x(2, 1)
    key_start(3)
    forward_x(0, 2, 0)
    key_x_far(2)
    key_y(2, 0, 1)
    forward_x(0, 0, 1)
    key_end(1)
    share(1, 1)
    key_x(3, 0)
    key_y(2, 1, 0)
    key_x(3, 1)
    share(1, 3)
    key_end(0)
    share(0, 3)
    key_y(2, 2, 1)
    key_x_far(3)
    key_y(2, 3, 1)
    key_y(2, 0, 0)
    key_y(2, 2, 0)
    key_y(2, 3, 0)
    key_y(2, 1, 1)
    share(2, 3)
    queries_of(2)
    key_y(3, 0, 0)
    key_y(3, 3, 1)
    queries_of(1)
    share(2, 1)
    key_y(3, 2, 0)
    meta_along_x()
    key_y(3, 1, 1)
    key_y(3, 2, 1)
    key_y(3, 0, 1)
    key_y(3, 1, 0)
    key_y(3, 3, 0)
    share(3, 3)
    share(3, 1)
    queries_of(0)
    key_end(2)
    queries_of(3)
    for copy in metas[2]:
        copy.wait_recv()
    everything = meta[...].reshape(64, 8, 128)
    line = lax.broadcasted_iota(jnp.int32, (8, 128), 0)
    firsts = []
    for d in range(1, 6):
        hits = jnp.sum(jnp.where(everything < d, 1, 0), axis=0)
        hits = jnp.where(line < 2, hits, 0).astype(jnp.float32)
        firsts.append(jnp.sum(jnp.sum(hits, axis=0, keepdims=True), axis=1, keepdims=True))
    for zb in range(4):
        documents = meta[x, y, zb][0:2]
        first = jnp.zeros((2, 128), jnp.float32)
        for d in range(1, 6):
            first = jnp.where(documents == d, firsts[d - 1], first)
        first_out[2 * zb : 2 * zb + 2, :] = first.astype(jnp.int32)
    key_end(3)
    for copy in siblings:
        copy.wait_recv()
    for copy in q_stay + kv_stay:
        copy.wait()
    for i in range(2):
        for own, copy, _ in a2a[i]:
            pl.when(jnp.logical_not(own))(copy.wait_send)
    cp.finish()
    assert cp.count == FRONT_COPIES, cp.count


def front(hidden, gain, w_query, w_key, w_value, doc_ids, positions, inverse):
    outside = pl.BlockSpec(memory_space=pltpu.HBM)
    inside = pl.BlockSpec(memory_space=pltpu.VMEM)
    return pl.pallas_call(
        front_kernel,
        out_shape=(
            jax.ShapeDtypeStruct((4, BLOCK, 2 * HEAD_SIZE), jnp.bfloat16),
            jax.ShapeDtypeStruct((2, 4, 4, 4, BLOCK, HEAD_SIZE), jnp.bfloat16),
            jax.ShapeDtypeStruct((8, 128), jnp.int32),
        ),
        in_specs=[outside] * 8,
        out_specs=(outside, outside, inside),
        scratch_shapes=[
            pltpu.VMEM((48, 4096), jnp.bfloat16),
            pltpu.VMEM((1, 4096), jnp.float32),
            pltpu.VMEM((1, BLOCK), jnp.int32),
            pltpu.VMEM((1, BLOCK), jnp.int32),
            pltpu.VMEM((1, HEAD_SIZE), jnp.float32),
            pltpu.VMEM((8, 2, 48, 4096), jnp.bfloat16),
            pltpu.VMEM((4, 4, 4, 64, 256), jnp.bfloat16),
            pltpu.VMEM((4, 4, 4, 64, 128), jnp.bfloat16),
            pltpu.VMEM((4, 4, 4, 8, 128), jnp.int32),
            pltpu.VMEM((8, 128), jnp.int32),
            pltpu.VMEM((2, 4, BLOCK, HEAD_SIZE), jnp.float32),
            pltpu.VMEM((BLOCK, HEAD_SIZE), jnp.float32),
            pltpu.VMEM((4, BLOCK, HEAD_SIZE), jnp.bfloat16),
            pltpu.VMEM((BLOCK, 2 * HEAD_SIZE), jnp.float32),
            pltpu.VMEM((4, BLOCK, 2 * HEAD_SIZE), jnp.bfloat16),
            pltpu.SemaphoreType.DMA((FRONT_COPIES,)),
            pltpu.SemaphoreType.DMA((FRONT_COPIES,)),
            pltpu.SemaphoreType.DMA((8,)),
            pltpu.SemaphoreType.DMA((8,)),
            pltpu.SemaphoreType.DMA((13,)),
        ],
        compiler_params=pltpu.CompilerParams(
            collective_id=0, has_side_effects=True, vmem_limit_bytes=55 << 20
        ),
        name="front",
    )(
        *(
            pltpu.with_memory_space_constraint(a, pltpu.HBM)
            for a in (hidden, gain, w_query, w_key, w_value, doc_ids, positions, inverse)
        )
    )


def attend_kernel(bounds, q_ref, both_in, first_ref, out_ref, even, odd, summed):
    both_ref = both_in.reshape(2, SEQUENCE, HEAD_SIZE)
    block = pl.program_id(0)
    t_low, t_clear, t_edge, t_high, row0 = (bounds[block, i] for i in range(5))
    scale = HEAD_SIZE ** (-0.5) * math.log2(math.e)
    width = 2 * BLOCK
    queries = jnp.concatenate([q_ref[0, :, :HEAD_SIZE], q_ref[0, :, HEAD_SIZE:]], axis=0)
    summed[...] = jnp.zeros_like(summed)

    half = KEY_TILE // 2

    def produce(store, begin, masked):
        peak = None
        for u in range(half // KEY_PIECE):
            first_key = begin + u * KEY_PIECE
            keys = both_ref[0, pl.ds(pl.multiple_of(first_key, KEY_PIECE), KEY_PIECE), :]
            piece = lax.dot_general(
                keys, queries, (((1,), (1,)), ((), ())), preferred_element_type=jnp.float32
            )
            if masked:
                key = first_key + lax.broadcasted_iota(jnp.int32, (KEY_PIECE, width), 0)
                lane = lax.broadcasted_iota(jnp.int32, (1, width), 1)
                query = row0 + jnp.where(lane < BLOCK, lane, lane - BLOCK)
                allowed = (key <= query) & (key >= first_ref[0])
                piece = jnp.where(allowed, piece, masked_score)
            store[u * KEY_PIECE : (u + 1) * KEY_PIECE, :] = piece
            top = jnp.max(piece.reshape(KEY_PIECE // 8, 8, width), axis=0)
            peak = top if peak is None else jnp.maximum(peak, top)
        return peak

    def consume(store, begin, peak, total, fresh):
        latest = jnp.maximum(peak, jnp.max(fresh, axis=0, keepdims=True))
        shrink = jnp.exp2((peak - latest) * scale)
        total = total * shrink
        offset = latest * scale
        gained = None
        for u in range(half // KEY_PIECE):
            weights = jnp.exp2(store[u * KEY_PIECE : (u + 1) * KEY_PIECE, :] * scale - offset)
            total = total + jnp.sum(weights.reshape(KEY_PIECE // 8, 8, width), axis=0)
            values = both_ref[1, pl.ds(pl.multiple_of(begin + u * KEY_PIECE, KEY_PIECE), KEY_PIECE), :]
            term = lax.dot_general(
                values, weights.astype(jnp.bfloat16), (((0,), (0,)), ((), ())),
                preferred_element_type=jnp.float32,
            )
            gained = term if gained is None else gained + term
        summed[...] = summed[...] * shrink + gained
        return latest, total

    def step(masked, t, carry):
        peak, total, fresh = carry
        begin = t * KEY_TILE
        following = produce(even, begin, masked)
        peak, total = consume(odd, begin - half, peak, total, fresh)
        fresh = produce(odd, begin + half, masked)
        peak, total = consume(even, begin, peak, total, following)
        return peak, total, fresh

    begin = t_low * KEY_TILE
    peak, total = jnp.full((1, width), masked_score, jnp.float32), jnp.zeros((8, width), jnp.float32)
    following = produce(even, begin, True)
    fresh = produce(odd, begin + half, True)
    peak, total = consume(even, begin, peak, total, following)
    carry = (peak, total, fresh)
    start = t_low + 1
    carry = lax.fori_loop(start, t_clear, functools.partial(step, True), carry)
    carry = lax.fori_loop(jnp.maximum(t_clear, start), t_edge, functools.partial(step, False), carry)
    carry = lax.fori_loop(jnp.maximum(t_edge, start), t_high, functools.partial(step, True), carry)
    peak, total = consume(odd, t_high * KEY_TILE - half, *carry)
    total = jnp.sum(total, axis=0, keepdims=True)
    result = (summed[...] / total).T
    out_ref[0, :, :HEAD_SIZE] = result[:BLOCK].astype(jnp.bfloat16)
    out_ref[0, :, HEAD_SIZE:] = result[BLOCK:].astype(jnp.bfloat16)


def attend(bounds, queries, both, first):
    return pl.pallas_call(
        attend_kernel,
        out_shape=jax.ShapeDtypeStruct((4, BLOCK, 2 * HEAD_SIZE), jnp.bfloat16),
        grid_spec=pltpu.PrefetchScalarGridSpec(
            num_scalar_prefetch=1,
            grid=(4,),
            in_specs=[
                pl.BlockSpec((1, BLOCK, 2 * HEAD_SIZE), lambda i, b: (i, 0, 0)),
                pl.BlockSpec(memory_space=pltpu.VMEM),
                pl.BlockSpec((1, 1, 2 * BLOCK), lambda i, b: (i, 0, 0)),
            ],
            out_specs=pl.BlockSpec((1, BLOCK, 2 * HEAD_SIZE), lambda i, b: (i, 0, 0)),
            scratch_shapes=[
                pltpu.VMEM((KEY_TILE // 2, 2 * BLOCK), jnp.float32),
                pltpu.VMEM((KEY_TILE // 2, 2 * BLOCK), jnp.float32),
                pltpu.VMEM((HEAD_SIZE, 2 * BLOCK), jnp.float32),
            ],
        ),
        compiler_params=pltpu.CompilerParams(vmem_limit_bytes=16 << 20),
        name="attend",
    )(bounds, queries, both, first)


def back_kernel(
    own, w_out, hidden, out,
    attended, weights, mine, given, landed, joined, arrived,
    send_sems, recv_sems, local_sems, step_send, step_recv,
):
    x, y, zh, zl, c = place()
    cz = zh // 2
    sibling, across = device(x, y, zh, zl, 1 - c), device(x, y, zh, 1 - zl, c)
    partners = [device(x, y, (zh + k) % 4, zl, cc) for k in range(4) for cc in (c, 1 - c)][1:]
    partners.append(across)
    pieces = 4
    width = 4096 // pieces
    cut = lambda i: pl.ds(i * width, width)
    fetch = [
        pltpu.make_async_copy(w_out.at[:, cut(i)], weights.at[:, cut(i)], local_sems.at[1 + i])
        for i in range(pieces)
    ]
    for copy in fetch:
        copy.start()
    greet(partners)
    spot = lambda j, cc: attended.at[:, pl.ds(pl.multiple_of((2 * j + cc) * 256, 256), 256)]
    copies = []
    here = cz == c
    for k in (2, 1, 3, 0):
        zt = (zh + k) % 4
        copy = pltpu.make_async_remote_copy(
            src_ref=own.at[zt],
            dst_ref=spot(zh % 2, c),
            send_sem=send_sems.at[k],
            recv_sem=recv_sems.at[(zh % 2) * 2 + c],
            device_id=device(x, y, zt, zl, cz),
            device_id_type=MESH,
        )
        if k == 0:
            stay = pltpu.make_async_copy(own.at[zt], spot(zh % 2, c), local_sems.at[0])
            pl.when(here)(stay.start)
            pl.when(jnp.logical_not(here))(copy.start)
        else:
            copy.start()
        copies.append(copy)
    for j in range(2):
        for cc in range(2):
            arrives = pltpu.make_async_remote_copy(
                src_ref=own.at[0],
                dst_ref=spot(j, cc),
                send_sem=send_sems.at[0],
                recv_sem=recv_sems.at[2 * j + cc],
                device_id=sibling,
                device_id_type=MESH,
            )
            local = (zh == 2 * c + j) & (c == cc)
            pl.when(jnp.logical_not(local))(arrives.wait_recv)
    pl.when(here)(stay.wait)

    cp = Copies(step_send, step_recv)
    to_sibling, to_across = [], []

    def pass_on(i):
        to_sibling[i].wait_recv()
        joined[i] = (mine[i, 1 - zl] + landed[i, 1 - zl].astype(jnp.float32)).astype(jnp.bfloat16)
        to_across.append(cp.send(joined.at[i], arrived.at[i], across))

    for i in range(pieces):
        fetch[i].wait()
        term = jnp.dot(attended[...], weights[:, cut(i)], preferred_element_type=jnp.float32)
        term = term.reshape(2, 2, 48, width)
        mine[i] = jnp.where(c == 0, term[:, 0], term[:, 1])
        given[i] = jnp.where(c == 0, term[:, 1], term[:, 0]).astype(jnp.bfloat16)
        to_sibling.append(cp.send(given.at[i], landed.at[i], sibling))
        if i > 0:
            pass_on(i - 1)
    pass_on(pieces - 1)
    for i in range(pieces):
        total = mine[i, zl] + landed[i, zl].astype(jnp.float32)
        to_across[i].wait_recv()
        total = total + arrived[i].astype(jnp.float32)
        out[:, cut(i)] = (hidden[:, cut(i)].astype(jnp.float32) + total).astype(jnp.bfloat16)
    pl.when(jnp.logical_not(here))(copies[-1].wait_send)
    for copy in copies[:-1]:
        copy.wait_send()
    cp.finish()


def back(own, w_out, hidden):
    anywhere = pl.BlockSpec(memory_space=pl.ANY)
    inside = pl.BlockSpec(memory_space=pltpu.VMEM)
    return pl.pallas_call(
        back_kernel,
        out_shape=jax.ShapeDtypeStruct((48, 4096), jnp.bfloat16),
        in_specs=[anywhere, anywhere, inside],
        out_specs=inside,
        scratch_shapes=[
            pltpu.VMEM((BLOCK, 1024), jnp.bfloat16),
            pltpu.VMEM((1024, 4096), jnp.bfloat16),
            pltpu.VMEM((4, 2, 48, 1024), jnp.float32),
            pltpu.VMEM((4, 2, 48, 1024), jnp.bfloat16),
            pltpu.VMEM((4, 2, 48, 1024), jnp.bfloat16),
            pltpu.VMEM((4, 48, 1024), jnp.bfloat16),
            pltpu.VMEM((4, 48, 1024), jnp.bfloat16),
            pltpu.SemaphoreType.DMA((4,)),
            pltpu.SemaphoreType.DMA((4,)),
            pltpu.SemaphoreType.DMA((5,)),
            pltpu.SemaphoreType.DMA((8,)),
            pltpu.SemaphoreType.DMA((8,)),
        ],
        compiler_params=pltpu.CompilerParams(
            collective_id=1, has_side_effects=True, vmem_limit_bytes=32 << 20
        ),
        name="back",
    )(own, w_out, hidden)


def body(hidden_in, norm_gain, w_query, w_key, value_weight, w_out, doc_ids, positions):
    x, y, zh, zl, c = place()
    inverse = yarn_inverse(HEAD_SIZE)
    queries, both, first = front(
        hidden_in,
        norm_gain.reshape(1, 4096),
        w_query,
        w_key,
        value_weight,
        doc_ids.reshape(1, BLOCK),
        positions.reshape(1, BLOCK),
        jnp.asarray([inverse + inverse], dtype=jnp.float32),
    )
    first = first.reshape(4, 256)[:, :BLOCK]
    row0 = (x * 16 + jnp.arange(4, dtype=jnp.int32) * 4 + y) * BLOCK
    t_low = first[:, 0] // KEY_TILE
    t_edge = jnp.maximum((row0 + 1) // KEY_TILE, t_low)
    t_clear = jnp.clip((first[:, -1] + KEY_TILE - 1) // KEY_TILE, t_low, t_edge)
    t_high = (row0 + BLOCK - 1) // KEY_TILE + 1
    bounds = jnp.stack([t_low, t_clear, t_edge, t_high, row0], axis=1)
    lanes = jnp.concatenate([first, first], axis=1).reshape(4, 1, 2 * BLOCK)
    queries, both, w_out = (
        pltpu.with_memory_space_constraint(a, pltpu.HBM) for a in (queries, both, w_out)
    )
    attended = attend(bounds, queries, both, lanes)
    return back(attended, w_out, hidden_in)


def solution(mesh):
    in_specs = (
        P(("outer", "inner", "tensor"), None),
        P(),
        P("inner", "tensor"),
        P("inner", "tensor"),
        P("inner", "tensor"),
        P("tensor", None),
        P(("outer", "inner")),
        P(("outer", "inner")),
    )
    out_specs = P(("outer", "inner", "tensor"), None)
    return jax.shard_map(body, mesh=mesh, in_specs=in_specs, out_specs=out_specs, check_vma=False)
```

```python
import functools
import math

import jax
import jax.numpy as jnp
from jax import lax
from jax.experimental import pallas as pl
from jax.experimental.pallas import tpu as pltpu
from jax.sharding import PartitionSpec as P

HEAD_SIZE = 128
BLOCK = 192
SEQUENCE = 12288
KEY_TILE = 1024
KEY_PIECE = 256
MESH = pl.DeviceIdType.MESH
FRONT_COPIES = 190


rope_base = 500000.0
yarn_factor = 8.0
trained_context = 8192.0
beta_fast = 32.0
beta_slow = 1.0
norm_epsilon = 1e-05
masked_score = -1e30


def yarn_inverse(head_dim):
    half_dim = head_dim // 2

    def correction(rotations):
        return (
            head_dim
            * math.log(trained_context / (rotations * 2.0 * math.pi))
            / (2.0 * math.log(rope_base))
        )

    lowest = max(math.floor(correction(beta_fast)), 0)
    highest = min(math.ceil(correction(beta_slow)), head_dim - 1)
    spread = max(highest - lowest, 0.001)
    values = []
    for column in range(half_dim):
        extrapolated = rope_base ** (-2.0 * column / head_dim)
        ramp = min(max((column - lowest) / spread, 0.0), 1.0)
        values.append(extrapolated / yarn_factor * ramp + extrapolated * (1.0 - ramp))
    return values


def place():
    outer, inner, tensor = (lax.axis_index(name) for name in ("outer", "inner", "tensor"))
    return outer, inner % 4, inner // 4, tensor // 2, tensor % 2


def device(x, y, zh, zl, c):
    return (x, zh * 4 + y, zl * 2 + c)


def greet(partners):
    barrier = pltpu.get_barrier_semaphore()
    for partner in partners:
        pl.semaphore_signal(barrier, inc=1, device_id=partner, device_id_type=MESH)
    pl.semaphore_wait(barrier, len(partners))


class Copies:
    def __init__(self, send_sems, recv_sems):
        self.send_sems, self.recv_sems, self.count, self.sent = send_sems, recv_sems, 0, []

    def send(self, src, dst, target):
        copy = pltpu.make_async_remote_copy(
            src_ref=src,
            dst_ref=dst,
            send_sem=self.send_sems.at[self.count],
            recv_sem=self.recv_sems.at[self.count],
            device_id=target,
            device_id_type=MESH,
        )
        self.count += 1
        copy.start()
        self.sent.append(copy)
        return copy

    def finish(self):
        for copy in self.sent:
            copy.wait_send()


def front_kernel(
    hidden_in, gain_in, w_query, w_key, w_value, doc_ids_in, positions_in, inverse_in,
    q_out, both, first_out,
    hidden, gain, doc_ids, positions, inverse, rows, weights_q, weights_kv,
    meta, meta_own, tables, product, kv, q_sum, q_own,
    send_sems, recv_sems, a2a_send, a2a_recv, local_sems,
):
    x, y, zh, zl, c = place()
    p = zh * 2 + zl
    near = lambda q: device(x, y, (q % 8) // 2, q % 2, c)
    right, left = near(p + 1), near(p + 7)
    sibling = device(x, y, zh, zl, 1 - c)
    xs = [(x + k) % 4 for k in range(4)]
    ys = [(y + k) % 4 for k in range(4)]
    y_next, y_far, y_prev = (device(x, ys[k], zh, zl, c) for k in (1, 2, 3))
    x_next, x_far, x_prev = (device(xs[k], y, zh, zl, c) for k in (1, 2, 3))
    columns = [device(x, y, (zh + k) % 4, zl, cc) for k in range(4) for cc in (c, 1 - c)][1:]
    partners = columns + [right, left, y_next, y_prev, y_far, x_next, x_prev, x_far]
    barrier = pltpu.get_barrier_semaphore()
    for partner in partners:
        pl.semaphore_signal(barrier, inc=1, device_id=partner, device_id_type=MESH)
    cp = Copies(send_sems, recv_sems)
    same = lambda ref, target: cp.send(ref, ref, target)
    fetches = [
        pltpu.make_async_copy(source, target, local_sems.at[i])
        for i, (source, target) in enumerate(
            (
                (doc_ids_in, doc_ids),
                (positions_in, positions),
                (hidden_in, hidden),
                (gain_in, gain),
                (inverse_in, inverse),
            )
        )
    ]
    for copy in fetches:
        copy.start()
    fetches[0].wait()
    fetches[1].wait()

    meta_own[...] = jnp.full((8, 128), 99, jnp.int32)
    meta_own[0:1, :] = doc_ids[:, :128]
    meta_own[1:2, :64] = doc_ids[:, 128:]
    meta_own[2:3, :] = positions[:, :128]
    meta_own[3:4, :64] = positions[:, 128:]
    meta[x, y, zh] = meta_own[...]
    for copy in fetches[2:]:
        copy.wait()
    widened = hidden[...].astype(jnp.float32)
    power = jnp.mean(widened * widened, axis=-1, keepdims=True)
    rows[p, c] = (widened * lax.rsqrt(power + norm_epsilon) * gain[...]).astype(jnp.bfloat16)
    pl.semaphore_wait(barrier, len(partners))

    a2a = {0: [], 1: []}
    stores = (weights_q, weights_kv)

    def scatter_weights(i):
        for j in range(2):
            for cc in range(2):
                zt = 2 * c + j
                own = (zt == zh) & (c == cc)
                taken = pl.ds(pl.multiple_of(x * 64, 64), 64)
                if i == 0:
                    source = w_query.at[taken, pl.ds(j * 512 + cc * 256, 256)]
                else:
                    source = (w_value if cc else w_key).at[taken, pl.ds(j * 128, 128)]
                spot = stores[i].at[zh, y, x]
                copy = pltpu.make_async_remote_copy(
                    src_ref=source,
                    dst_ref=spot,
                    send_sem=a2a_send.at[4 * i + 2 * j + cc],
                    recv_sem=a2a_recv.at[4 * i + zh],
                    device_id=device(x, y, zt, zl, cc),
                    device_id_type=MESH,
                )
                stay = pltpu.make_async_copy(source, spot, local_sems.at[i])
                pl.when(own)(stay.start)
                pl.when(jnp.logical_not(own))(copy.start)
                a2a[i].append((own, copy, stay))

    def collect_weights(i):
        for source in range(4):
            spot = stores[i].at[source, y, x]
            arrives = pltpu.make_async_remote_copy(
                src_ref=spot,
                dst_ref=spot,
                send_sem=a2a_send.at[0],
                recv_sem=a2a_recv.at[4 * i + source],
                device_id=sibling,
                device_id_type=MESH,
            )
            own = (zh == source) & (c == zh // 2)
            pl.when(jnp.logical_not(own))(arrives.wait_recv)
        for own, copy, stay in a2a[i]:
            pl.when(own)(stay.wait)

    wy, wy_far, wx, forwards = {}, {}, {}, {0: [], 1: []}

    def along_y(i):
        mine = stores[i].at[:, y, x]
        wy[i] = same(mine, y_next), same(mine, y_prev)

    def forward_y(i, side):
        wy[i][side].wait_recv()
        spot = stores[i].at[pl.ds(2 * side, 2), ys[3 - 2 * side], x]
        wy_far[i, side] = same(spot, (y_next, y_prev)[side])

    def along_x(i, k):
        piece = stores[i].at[:, ys[k], x]
        wx[i, k] = same(piece, x_next), same(piece, x_prev)

    def far_y(i):
        wy_far[i, 0].wait_recv()
        wy_far[i, 1].wait_recv()
        along_x(i, 2)

    def forward_x(i, k, side):
        wx[i, k][side].wait_recv()
        spot = stores[i].at[pl.ds(2 * side, 2), ys[k], xs[3 - 2 * side]]
        forwards[i].append(same(spot, (x_next, x_prev)[side]))

    chunks_right = (pl.ds(0, 16), pl.ds(16, 32))
    chunks_left = (pl.ds(32, 16), pl.ds(0, 32))
    to_right, to_left, to_sibling, own_row = {}, {}, {k: [] for k in range(4)}, []

    def far_spot(q, h, hop):
        if h == 0:
            return rows.at[q, c, pl.ds(0, 16) if hop == 7 else pl.ds(32, 16)]
        return rows.at[q, c, pl.ds(16, 16), pl.ds(0 if hop == 7 else 2048, 2048)]

    def ring_start(h):
        to_right[0, h] = same(rows.at[p, c, chunks_right[h]], right)
        to_left[0, h] = same(rows.at[p, c, chunks_left[h]], left)

    def own_start():
        own_row.append(same(rows.at[p, c], sibling))

    def ring(step, h, side):
        to, chunks, target, hop = (
            (to_right, chunks_right, right, 7),
            (to_left, chunks_left, left, 1),
        )[side]
        to[step, h].wait_recv()
        q = (p + hop * (step + 1)) % 8
        spot = rows.at[q, c, chunks[h]] if step < 3 else far_spot(q, h, hop)
        if step < 2:
            to[step + 1, h] = same(spot, target)
        elif step == 2:
            to[3, h] = same(far_spot(q, h, hop), target)
        to_sibling[step].append(same(spot, sibling))

    metas = {}

    def meta_start():
        metas[0] = [
            cp.send(meta_own, meta.at[x, y, zh], device(x, y, (zh + k) % 4, zl, c))
            for k in (1, 2, 3)
        ]

    def meta_along_y():
        for copy in metas[0]:
            copy.wait_recv()
        mine = meta.at[x, y]
        metas[1] = [same(mine, target) for target in (y_next, y_far, y_prev)]

    def meta_along_x():
        for copy in metas[1]:
            copy.wait_recv()
        mine = meta.at[x]
        metas[2] = [same(mine, target) for target in (x_next, x_far, x_prev)]

    order = [zh, (zh + 3 + 2 * zl) % 4, (zh + 1 + 2 * zl) % 4, (zh + 2) % 4]

    def tables_of(zb):
        tile = meta[x, y, zb].astype(jnp.float32)
        upper = jnp.broadcast_to(tile[2:3], (128, 128)).T
        lower = jnp.broadcast_to(tile[3:4], (128, 128)).T
        angles = jnp.concatenate([upper, lower[:64]], axis=0) * inverse[...]
        attention_gain = 0.1 * math.log(yarn_factor) + 1.0
        lane = lax.broadcasted_iota(jnp.int32, (BLOCK, HEAD_SIZE), 1)
        sine = jnp.sin(angles) * attention_gain
        tables[0, zb] = jnp.cos(angles) * attention_gain
        tables[1, zb] = jnp.where(lane < HEAD_SIZE // 2, -sine, sine)

    def turn(head, cosine, sine):
        return head * cosine + pltpu.roll(head, HEAD_SIZE // 2, 1) * sine

    def multiply(zb, store, total):
        total[...] = jnp.zeros_like(total)

        @pl.loop(0, 4)
        def _(k):
            piece = store[k].reshape(1024, store.shape[-1])
            depth = pl.ds(pl.multiple_of(k * 1024, 1024), 1024)
            left_side = rows[pl.ds(2 * zb, 2), :, :, depth].reshape(BLOCK, 1024)
            total[...] += jnp.dot(left_side, piece, preferred_element_type=jnp.float32)

    q_stay = []

    def queries_of(s):
        zb = order[s]
        if not q_stay:
            for copy in forwards[0]:
                copy.wait_recv()
        multiply(zb, weights_q, q_sum)
        for h in range(2):
            at = pl.ds(h * HEAD_SIZE, HEAD_SIZE)
            q_own[s, :, at] = turn(q_sum[:, at], tables[0, zb], tables[1, zb]).astype(jnp.bfloat16)
        q_stay.append(pltpu.make_async_copy(q_own.at[s], q_out.at[zb], local_sems.at[5 + s]))
        q_stay[-1].start()

    halves = (pl.ds(0, 96), pl.ds(96, 96))
    cell = lambda s, i, k: both.at[c, xs[i], order[s], ys[k]]
    side_of = lambda s, i, k, f: both.at[c, xs[i], order[s], ys[k], halves[f]]
    kx, kx_far, ky, ky_far, kv_stay, siblings = {}, {}, {}, {}, [], []
    is_key = c == 0

    def key_start(s):
        zb = order[s]
        for copy in to_sibling[s] + (forwards[1] + own_row if s == 0 else []):
            copy.wait_recv()
        multiply(zb, weights_kv, product)
        cosine = jnp.where(is_key, tables[0, zb], 1.0)
        sine = jnp.where(is_key, tables[1, zb], 0.0)
        kv[s] = turn(product[...], cosine, sine).astype(jnp.bfloat16)
        own, spot = kv.at[s], cell(s, 0, 0)
        kx[s] = cp.send(own, spot, x_next), cp.send(own, spot, x_prev)
        ky[s, 0] = cp.send(own, spot, y_next), cp.send(own, spot, y_prev)
        siblings.append(cp.send(own, spot, sibling))
        kv_stay.append(pltpu.make_async_copy(own, spot, local_sems.at[9 + s]))
        kv_stay[-1].start()

    def key_along_y(s, i):
        ky[s, i] = same(cell(s, i, 0), y_next), same(cell(s, i, 0), y_prev)
        siblings.append(same(cell(s, i, 0), sibling))

    def key_x(s, side):
        kx[s][side].wait_recv()
        spot = side_of(s, 3 - 2 * side, 0, side)
        kx_far[s, side] = same(spot, (x_next, x_prev)[side])
        key_along_y(s, 3 - 2 * side)

    def key_x_far(s):
        kx_far[s, 0].wait_recv()
        kx_far[s, 1].wait_recv()
        key_along_y(s, 2)

    def key_y(s, i, side):
        ky[s, i][side].wait_recv()
        spot = side_of(s, i, 3 - 2 * side, side)
        ky_far[s, i, side] = same(spot, (y_next, y_prev)[side])

    def share(s, k):
        siblings.append(same(both.at[c, :, order[s], ys[k]], sibling))

    def key_end(s):
        for i in range(4):
            for side in range(2):
                ky_far[s, i, side].wait_recv()
        share(s, 2)

    scatter_weights(1)
    meta_start()
    scatter_weights(0)
    ring_start(0)
    ring_start(1)
    collect_weights(1)
    along_y(1)
    along_x(1, 0)
    forward_y(1, 0)
    own_start()
    along_x(1, 3)
    collect_weights(0)
    ring(0, 0, 0)
    forward_x(1, 0, 1)
    forward_y(1, 1)
    along_x(1, 1)
    forward_x(1, 0, 0)
    along_y(0)
    meta_along_y()
    ring(0, 0, 1)
    forward_x(1, 3, 1)
    far_y(1)
    ring(0, 1, 0)
    along_x(0, 0)
    forward_x(1, 2, 0)
    forward_x(1, 1, 0)
    forward_y(0, 1)
    forward_x(1, 3, 0)
    ring(1, 0, 0)
    ring(0, 1, 1)
    forward_x(1, 1, 1)
    forward_x(1, 2, 1)
    along_x(0, 1)
    tables_of(order[0])
    forward_y(0, 0)
    ring(1, 0, 1)
    tables_of(order[1])
    key_start(0)
    ring(1, 1, 0)
    far_y(0)
    along_x(0, 3)
    key_y(0, 0, 0)
    ring(2, 0, 0)
    ring(1, 1, 1)
    key_x(0, 0)
    key_x(0, 1)
    key_y(0, 0, 1)
    key_start(1)
    key_y(0, 3, 0)
    ring(2, 1, 0)
    forward_x(0, 3, 0)
    forward_x(0, 1, 1)
    ring(2, 0, 1)
    key_y(0, 1, 1)
    key_x_far(0)
    key_x(1, 0)
    key_x(1, 1)
    ring(2, 1, 1)
    key_y(0, 1, 0)
    key_y(0, 3, 1)
    key_y(1, 0, 1)
    ring(3, 0, 0)
    tables_of(order[2])
    forward_x(0, 2, 1)
    key_x_far(1)
    key_y(0, 2, 0)
    key_y(0, 2, 1)
    forward_x(0, 1, 0)
    key_y(1, 3, 0)
    key_start(2)
    forward_x(0, 0, 0)
    key_y(1, 1, 0)
    ring(3, 1, 0)
    key_y(1, 3, 1)
    ring(3, 1, 1)
    key_y(1, 2, 0)
    forward_x(0, 3, 1)
    key_y(1, 1, 1)
    ring(3, 0, 1)
    key_y(1, 2, 1)
    key_y(1, 0, 0)
    tables_of(order[3])
    share(0, 1)
    key_x(2, 0)
    key_x(2, 1)
    key_start(3)
    forward_x(0, 2, 0)
    key_x_far(2)
    key_y(2, 0, 1)
    forward_x(0, 0, 1)
    key_end(1)
    share(1, 1)
    key_x(3, 0)
    key_y(2, 1, 0)
    key_x(3, 1)
    share(1, 3)
    key_end(0)
    share(0, 3)
    key_y(2, 2, 1)
    key_x_far(3)
    key_y(2, 3, 1)
    key_y(2, 0, 0)
    key_y(2, 2, 0)
    key_y(2, 3, 0)
    key_y(2, 1, 1)
    share(2, 3)
    queries_of(2)
    key_y(3, 0, 0)
    key_y(3, 3, 1)
    queries_of(1)
    share(2, 1)
    key_y(3, 2, 0)
    meta_along_x()
    key_y(3, 1, 1)
    key_y(3, 2, 1)
    key_y(3, 0, 1)
    key_y(3, 1, 0)
    key_y(3, 3, 0)
    share(3, 3)
    share(3, 1)
    queries_of(0)
    key_end(2)
    queries_of(3)
    for copy in metas[2]:
        copy.wait_recv()
    everything = meta[...].reshape(64, 8, 128)
    line = lax.broadcasted_iota(jnp.int32, (8, 128), 0)
    firsts = []
    for d in range(1, 6):
        hits = jnp.sum(jnp.where(everything < d, 1, 0), axis=0)
        hits = jnp.where(line < 2, hits, 0).astype(jnp.float32)
        firsts.append(jnp.sum(jnp.sum(hits, axis=0, keepdims=True), axis=1, keepdims=True))
    for zb in range(4):
        documents = meta[x, y, zb][0:2]
        first = jnp.zeros((2, 128), jnp.float32)
        for d in range(1, 6):
            first = jnp.where(documents == d, firsts[d - 1], first)
        first = first.astype(jnp.int32)
        first_out[zb] = jnp.concatenate([first[0:1], first[1:2, :64]] * 2, axis=1)
    key_end(3)
    for copy in siblings:
        copy.wait_recv()
    for copy in q_stay + kv_stay:
        copy.wait()
    for i in range(2):
        for own, copy, _ in a2a[i]:
            pl.when(jnp.logical_not(own))(copy.wait_send)
    cp.finish()
    assert cp.count == FRONT_COPIES, cp.count


def front(hidden, gain, w_query, w_key, w_value, doc_ids, positions, inverse):
    outside = pl.BlockSpec(memory_space=pltpu.HBM)
    inside = pl.BlockSpec(memory_space=pltpu.VMEM)
    return pl.pallas_call(
        front_kernel,
        out_shape=(
            jax.ShapeDtypeStruct((4, BLOCK, 2 * HEAD_SIZE), jnp.bfloat16),
            jax.ShapeDtypeStruct((2, 4, 4, 4, BLOCK, HEAD_SIZE), jnp.bfloat16),
            jax.ShapeDtypeStruct((4, 1, 2 * BLOCK), jnp.int32),
        ),
        in_specs=[outside] * 8,
        out_specs=(outside, outside, inside),
        scratch_shapes=[
            pltpu.VMEM((48, 4096), jnp.bfloat16),
            pltpu.VMEM((1, 4096), jnp.float32),
            pltpu.VMEM((1, BLOCK), jnp.int32),
            pltpu.VMEM((1, BLOCK), jnp.int32),
            pltpu.VMEM((1, HEAD_SIZE), jnp.float32),
            pltpu.VMEM((8, 2, 48, 4096), jnp.bfloat16),
            pltpu.VMEM((4, 4, 4, 64, 256), jnp.bfloat16),
            pltpu.VMEM((4, 4, 4, 64, 128), jnp.bfloat16),
            pltpu.VMEM((4, 4, 4, 8, 128), jnp.int32),
            pltpu.VMEM((8, 128), jnp.int32),
            pltpu.VMEM((2, 4, BLOCK, HEAD_SIZE), jnp.float32),
            pltpu.VMEM((BLOCK, HEAD_SIZE), jnp.float32),
            pltpu.VMEM((4, BLOCK, HEAD_SIZE), jnp.bfloat16),
            pltpu.VMEM((BLOCK, 2 * HEAD_SIZE), jnp.float32),
            pltpu.VMEM((4, BLOCK, 2 * HEAD_SIZE), jnp.bfloat16),
            pltpu.SemaphoreType.DMA((FRONT_COPIES,)),
            pltpu.SemaphoreType.DMA((FRONT_COPIES,)),
            pltpu.SemaphoreType.DMA((8,)),
            pltpu.SemaphoreType.DMA((8,)),
            pltpu.SemaphoreType.DMA((13,)),
        ],
        compiler_params=pltpu.CompilerParams(
            collective_id=0, has_side_effects=True, vmem_limit_bytes=55 << 20
        ),
        name="front",
    )(
        *(
            pltpu.with_memory_space_constraint(a, pltpu.HBM)
            for a in (hidden, gain, w_query, w_key, w_value, doc_ids, positions, inverse)
        )
    )


def attend_kernel(bounds, q_ref, both_in, first_ref, out_ref, even, odd, summed):
    both_ref = both_in.reshape(2, SEQUENCE, HEAD_SIZE)
    block = pl.program_id(0)
    t_low, t_clear, t_edge, t_high, row0 = (bounds[block, i] for i in range(5))
    scale = HEAD_SIZE ** (-0.5) * math.log2(math.e)
    width = 2 * BLOCK
    queries = jnp.concatenate([q_ref[0, :, :HEAD_SIZE], q_ref[0, :, HEAD_SIZE:]], axis=0)
    summed[...] = jnp.zeros_like(summed)

    half = KEY_TILE // 2

    def produce(store, begin, masked):
        peak = None
        for u in range(half // KEY_PIECE):
            first_key = begin + u * KEY_PIECE
            keys = both_ref[0, pl.ds(pl.multiple_of(first_key, KEY_PIECE), KEY_PIECE), :]
            piece = lax.dot_general(
                keys, queries, (((1,), (1,)), ((), ())), preferred_element_type=jnp.float32
            )
            if masked:
                key = first_key + lax.broadcasted_iota(jnp.int32, (KEY_PIECE, width), 0)
                lane = lax.broadcasted_iota(jnp.int32, (1, width), 1)
                query = row0 + jnp.where(lane < BLOCK, lane, lane - BLOCK)
                allowed = (key <= query) & (key >= first_ref[0])
                piece = jnp.where(allowed, piece, masked_score)
            store[u * KEY_PIECE : (u + 1) * KEY_PIECE, :] = piece
            top = jnp.max(piece.reshape(KEY_PIECE // 8, 8, width), axis=0)
            peak = top if peak is None else jnp.maximum(peak, top)
        return peak

    def consume(store, begin, peak, total, fresh):
        latest = jnp.maximum(peak, jnp.max(fresh, axis=0, keepdims=True))
        shrink = jnp.exp2((peak - latest) * scale)
        total = total * shrink
        offset = latest * scale
        gained = None
        for u in range(half // KEY_PIECE):
            weights = jnp.exp2(store[u * KEY_PIECE : (u + 1) * KEY_PIECE, :] * scale - offset)
            total = total + jnp.sum(weights.reshape(KEY_PIECE // 8, 8, width), axis=0)
            values = both_ref[1, pl.ds(pl.multiple_of(begin + u * KEY_PIECE, KEY_PIECE), KEY_PIECE), :]
            term = lax.dot_general(
                values, weights.astype(jnp.bfloat16), (((0,), (0,)), ((), ())),
                preferred_element_type=jnp.float32,
            )
            gained = term if gained is None else gained + term
        summed[...] = summed[...] * shrink + gained
        return latest, total

    def step(masked, t, carry):
        peak, total, fresh = carry
        begin = t * KEY_TILE
        following = produce(even, begin, masked)
        peak, total = consume(odd, begin - half, peak, total, fresh)
        fresh = produce(odd, begin + half, masked)
        peak, total = consume(even, begin, peak, total, following)
        return peak, total, fresh

    begin = t_low * KEY_TILE
    peak, total = jnp.full((1, width), masked_score, jnp.float32), jnp.zeros((8, width), jnp.float32)
    following = produce(even, begin, True)
    fresh = produce(odd, begin + half, True)
    peak, total = consume(even, begin, peak, total, following)
    carry = (peak, total, fresh)
    start = t_low + 1
    carry = lax.fori_loop(start, t_clear, functools.partial(step, True), carry)
    carry = lax.fori_loop(jnp.maximum(t_clear, start), t_edge, functools.partial(step, False), carry)
    carry = lax.fori_loop(jnp.maximum(t_edge, start), t_high, functools.partial(step, True), carry)
    peak, total = consume(odd, t_high * KEY_TILE - half, *carry)
    total = jnp.sum(total, axis=0, keepdims=True)
    result = (summed[...] / total).T
    out_ref[0, :, :HEAD_SIZE] = result[:BLOCK].astype(jnp.bfloat16)
    out_ref[0, :, HEAD_SIZE:] = result[BLOCK:].astype(jnp.bfloat16)


def attend(bounds, queries, both, first):
    return pl.pallas_call(
        attend_kernel,
        out_shape=jax.ShapeDtypeStruct((4, BLOCK, 2 * HEAD_SIZE), jnp.bfloat16),
        grid_spec=pltpu.PrefetchScalarGridSpec(
            num_scalar_prefetch=1,
            grid=(4,),
            in_specs=[
                pl.BlockSpec((1, BLOCK, 2 * HEAD_SIZE), lambda i, b: (i, 0, 0)),
                pl.BlockSpec(memory_space=pltpu.VMEM),
                pl.BlockSpec((1, 1, 2 * BLOCK), lambda i, b: (i, 0, 0)),
            ],
            out_specs=pl.BlockSpec((1, BLOCK, 2 * HEAD_SIZE), lambda i, b: (i, 0, 0)),
            scratch_shapes=[
                pltpu.VMEM((KEY_TILE // 2, 2 * BLOCK), jnp.float32),
                pltpu.VMEM((KEY_TILE // 2, 2 * BLOCK), jnp.float32),
                pltpu.VMEM((HEAD_SIZE, 2 * BLOCK), jnp.float32),
            ],
        ),
        compiler_params=pltpu.CompilerParams(vmem_limit_bytes=16 << 20),
        name="attend",
    )(bounds, queries, both, first)


def back_kernel(
    own, w_out, hidden, out,
    attended, weights, first, mine, given, landed, joined, arrived,
    send_sems, recv_sems, local_sems, step_send, step_recv,
):
    x, y, zh, zl, c = place()
    cz = zh // 2
    sibling, across = device(x, y, zh, zl, 1 - c), device(x, y, zh, 1 - zl, c)
    partners = [device(x, y, (zh + k) % 4, zl, cc) for k in range(4) for cc in (c, 1 - c)][1:]
    partners.append(across)
    pieces = 4
    width = 4096 // pieces
    cut = lambda i: pl.ds(i * width, width)
    fetch = [
        pltpu.make_async_copy(w_out.at[:, cut(i)], weights.at[:, cut(i)], local_sems.at[1 + i])
        for i in range(pieces)
    ]
    for copy in fetch:
        copy.start()
    greet(partners)
    spot = lambda j, cc: attended.at[:, pl.ds(pl.multiple_of((2 * j + cc) * 256, 256), 256)]
    copies = []
    here = cz == c
    for k in (2, 1, 3, 0):
        zt = (zh + k) % 4
        copy = pltpu.make_async_remote_copy(
            src_ref=own.at[zt],
            dst_ref=spot(zh % 2, c),
            send_sem=send_sems.at[k],
            recv_sem=recv_sems.at[(zh % 2) * 2 + c],
            device_id=device(x, y, zt, zl, cz),
            device_id_type=MESH,
        )
        if k == 0:
            stay = pltpu.make_async_copy(own.at[zt], spot(zh % 2, c), local_sems.at[0])
            pl.when(here)(stay.start)
            pl.when(jnp.logical_not(here))(copy.start)
        else:
            copy.start()
        copies.append(copy)
    near = jnp.where(here, zh % 2, 1 - zh % 2)

    def arrive(j):
        for cc in range(2):
            arrives = pltpu.make_async_remote_copy(
                src_ref=own.at[0],
                dst_ref=spot(j, cc),
                send_sem=send_sems.at[0],
                recv_sem=recv_sems.at[2 * j + cc],
                device_id=sibling,
                device_id_type=MESH,
            )
            local = (zh == 2 * c + j) & (c == cc)
            pl.when(jnp.logical_not(local))(arrives.wait_recv)

    def multiply(j, i):
        half = pl.ds(pl.multiple_of(j * 512, 512), 512)
        return jnp.dot(
            attended[:, half], weights[half, cut(i)], preferred_element_type=jnp.float32
        )

    arrive(near)
    pl.when(here)(stay.wait)
    for i in range(pieces):
        fetch[i].wait()
        first[i] = multiply(near, i)
    arrive(1 - near)

    cp = Copies(step_send, step_recv)
    to_sibling, to_across = [], []

    def pass_on(i):
        to_sibling[i].wait_recv()
        joined[i] = (mine[i, 1 - zl] + landed[i, 1 - zl].astype(jnp.float32)).astype(jnp.bfloat16)
        to_across.append(cp.send(joined.at[i], arrived.at[i], across))

    for i in range(pieces):
        term = (first[i] + multiply(1 - near, i)).reshape(2, 2, 48, width)
        mine[i] = jnp.where(c == 0, term[:, 0], term[:, 1])
        given[i] = jnp.where(c == 0, term[:, 1], term[:, 0]).astype(jnp.bfloat16)
        to_sibling.append(cp.send(given.at[i], landed.at[i], sibling))
        if i > 0:
            pass_on(i - 1)
    pass_on(pieces - 1)
    for i in range(pieces):
        total = mine[i, zl] + landed[i, zl].astype(jnp.float32)
        to_across[i].wait_recv()
        total = total + arrived[i].astype(jnp.float32)
        out[:, cut(i)] = (hidden[:, cut(i)].astype(jnp.float32) + total).astype(jnp.bfloat16)
    pl.when(jnp.logical_not(here))(copies[-1].wait_send)
    for copy in copies[:-1]:
        copy.wait_send()
    cp.finish()


def back(own, w_out, hidden):
    anywhere = pl.BlockSpec(memory_space=pl.ANY)
    inside = pl.BlockSpec(memory_space=pltpu.VMEM)
    return pl.pallas_call(
        back_kernel,
        out_shape=jax.ShapeDtypeStruct((48, 4096), jnp.bfloat16),
        in_specs=[anywhere, anywhere, inside],
        out_specs=inside,
        scratch_shapes=[
            pltpu.VMEM((BLOCK, 1024), jnp.bfloat16),
            pltpu.VMEM((1024, 4096), jnp.bfloat16),
            pltpu.VMEM((4, BLOCK, 1024), jnp.float32),
            pltpu.VMEM((4, 2, 48, 1024), jnp.float32),
            pltpu.VMEM((4, 2, 48, 1024), jnp.bfloat16),
            pltpu.VMEM((4, 2, 48, 1024), jnp.bfloat16),
            pltpu.VMEM((4, 48, 1024), jnp.bfloat16),
            pltpu.VMEM((4, 48, 1024), jnp.bfloat16),
            pltpu.SemaphoreType.DMA((4,)),
            pltpu.SemaphoreType.DMA((4,)),
            pltpu.SemaphoreType.DMA((5,)),
            pltpu.SemaphoreType.DMA((8,)),
            pltpu.SemaphoreType.DMA((8,)),
        ],
        compiler_params=pltpu.CompilerParams(
            collective_id=1, has_side_effects=True, vmem_limit_bytes=32 << 20
        ),
        name="back",
    )(own, w_out, hidden)


def body(hidden_in, norm_gain, w_query, w_key, value_weight, w_out, doc_ids, positions):
    x, y, zh, zl, c = place()
    inverse = yarn_inverse(HEAD_SIZE)
    queries, both, first = front(
        hidden_in,
        norm_gain.reshape(1, 4096),
        w_query,
        w_key,
        value_weight,
        doc_ids.reshape(1, BLOCK),
        positions.reshape(1, BLOCK),
        jnp.asarray([inverse + inverse], dtype=jnp.float32),
    )
    row0 = (x * 16 + jnp.arange(4, dtype=jnp.int32) * 4 + y) * BLOCK
    t_low = first[:, 0, 0] // KEY_TILE
    t_edge = jnp.maximum((row0 + 1) // KEY_TILE, t_low)
    t_clear = jnp.clip((first[:, 0, -1] + KEY_TILE - 1) // KEY_TILE, t_low, t_edge)
    t_high = (row0 + BLOCK - 1) // KEY_TILE + 1
    bounds = jnp.stack([t_low, t_clear, t_edge, t_high, row0], axis=1)
    queries, both, w_out = (
        pltpu.with_memory_space_constraint(a, pltpu.HBM) for a in (queries, both, w_out)
    )
    attended = attend(bounds, queries, both, first)
    return back(attended, w_out, hidden_in)


def solution(mesh):
    in_specs = (
        P(("outer", "inner", "tensor"), None),
        P(),
        P("inner", "tensor"),
        P("inner", "tensor"),
        P("inner", "tensor"),
        P("tensor", None),
        P(("outer", "inner")),
        P(("outer", "inner")),
    )
    out_specs = P(("outer", "inner", "tensor"), None)
    return jax.shard_map(body, mesh=mesh, in_specs=in_specs, out_specs=out_specs, check_vma=False)
```

```python
import functools
import math

import jax
import jax.numpy as jnp
from jax import lax
from jax.experimental import pallas as pl
from jax.experimental.pallas import tpu as pltpu
from jax.sharding import PartitionSpec as P

HEAD_SIZE = 128
BLOCK = 192
SEQUENCE = 12288
KEY_TILE = 1024
KEY_PIECE = 256
MESH = pl.DeviceIdType.MESH
FRONT_COPIES = 190


rope_base = 500000.0
yarn_factor = 8.0
trained_context = 8192.0
beta_fast = 32.0
beta_slow = 1.0
norm_epsilon = 1e-05
masked_score = -1e30


def yarn_inverse(head_dim):
    half_dim = head_dim // 2

    def correction(rotations):
        return (
            head_dim
            * math.log(trained_context / (rotations * 2.0 * math.pi))
            / (2.0 * math.log(rope_base))
        )

    lowest = max(math.floor(correction(beta_fast)), 0)
    highest = min(math.ceil(correction(beta_slow)), head_dim - 1)
    spread = max(highest - lowest, 0.001)
    values = []
    for column in range(half_dim):
        extrapolated = rope_base ** (-2.0 * column / head_dim)
        ramp = min(max((column - lowest) / spread, 0.0), 1.0)
        values.append(extrapolated / yarn_factor * ramp + extrapolated * (1.0 - ramp))
    return values


def place():
    outer, inner, tensor = (lax.axis_index(name) for name in ("outer", "inner", "tensor"))
    return outer, inner % 4, inner // 4, tensor // 2, tensor % 2


def device(x, y, zh, zl, c):
    return (x, zh * 4 + y, zl * 2 + c)


def greet(partners):
    barrier = pltpu.get_barrier_semaphore()
    for partner in partners:
        pl.semaphore_signal(barrier, inc=1, device_id=partner, device_id_type=MESH)
    pl.semaphore_wait(barrier, len(partners))


class Copies:
    def __init__(self, send_sems, recv_sems):
        self.send_sems, self.recv_sems, self.count, self.sent = send_sems, recv_sems, 0, []

    def send(self, src, dst, target):
        copy = pltpu.make_async_remote_copy(
            src_ref=src,
            dst_ref=dst,
            send_sem=self.send_sems.at[self.count],
            recv_sem=self.recv_sems.at[self.count],
            device_id=target,
            device_id_type=MESH,
        )
        self.count += 1
        copy.start()
        self.sent.append(copy)
        return copy

    def finish(self):
        for copy in self.sent:
            copy.wait_send()


def front_kernel(
    hidden_in, gain_in, w_query, w_key, w_value, doc_ids_in, positions_in, inverse_in,
    q_out, both, first_out,
    hidden, gain, doc_ids, positions, inverse, rows, weights_q, weights_kv,
    meta, meta_own, tables, product, kv, q_sum, q_own,
    send_sems, recv_sems, a2a_send, a2a_recv, local_sems,
):
    x, y, zh, zl, c = place()
    p = zh * 2 + zl
    near = lambda q: device(x, y, (q % 8) // 2, q % 2, c)
    right, left = near(p + 1), near(p + 7)
    sibling = device(x, y, zh, zl, 1 - c)
    xs = [(x + k) % 4 for k in range(4)]
    ys = [(y + k) % 4 for k in range(4)]
    y_next, y_far, y_prev = (device(x, ys[k], zh, zl, c) for k in (1, 2, 3))
    x_next, x_far, x_prev = (device(xs[k], y, zh, zl, c) for k in (1, 2, 3))
    columns = [device(x, y, (zh + k) % 4, zl, cc) for k in range(4) for cc in (c, 1 - c)][1:]
    partners = columns + [right, left, y_next, y_prev, y_far, x_next, x_prev, x_far]
    barrier = pltpu.get_barrier_semaphore()
    for partner in partners:
        pl.semaphore_signal(barrier, inc=1, device_id=partner, device_id_type=MESH)
    cp = Copies(send_sems, recv_sems)
    same = lambda ref, target: cp.send(ref, ref, target)
    fetches = [
        pltpu.make_async_copy(source, target, local_sems.at[i])
        for i, (source, target) in enumerate(
            (
                (doc_ids_in, doc_ids),
                (positions_in, positions),
                (hidden_in, hidden),
                (gain_in, gain),
                (inverse_in, inverse),
            )
        )
    ]
    for copy in fetches:
        copy.start()
    fetches[0].wait()
    fetches[1].wait()

    meta_own[...] = jnp.full((8, 128), 99, jnp.int32)
    meta_own[0:1, :] = doc_ids[:, :128]
    meta_own[1:2, :64] = doc_ids[:, 128:]
    meta_own[2:3, :] = positions[:, :128]
    meta_own[3:4, :64] = positions[:, 128:]
    meta[x, y, zh] = meta_own[...]
    for copy in fetches[2:]:
        copy.wait()
    widened = hidden[...].astype(jnp.float32)
    power = jnp.mean(widened * widened, axis=-1, keepdims=True)
    rows[p, c] = (widened * lax.rsqrt(power + norm_epsilon) * gain[...]).astype(jnp.bfloat16)
    pl.semaphore_wait(barrier, len(partners))

    a2a = {0: [], 1: []}
    stores = (weights_q, weights_kv)

    def scatter_weights(i):
        for j in range(2):
            for cc in range(2):
                zt = 2 * c + j
                own = (zt == zh) & (c == cc)
                taken = pl.ds(pl.multiple_of(x * 64, 64), 64)
                if i == 0:
                    source = w_query.at[taken, pl.ds(j * 512 + cc * 256, 256)]
                else:
                    source = (w_value if cc else w_key).at[taken, pl.ds(j * 128, 128)]
                spot = stores[i].at[zh, y, x]
                copy = pltpu.make_async_remote_copy(
                    src_ref=source,
                    dst_ref=spot,
                    send_sem=a2a_send.at[4 * i + 2 * j + cc],
                    recv_sem=a2a_recv.at[4 * i + zh],
                    device_id=device(x, y, zt, zl, cc),
                    device_id_type=MESH,
                )
                stay = pltpu.make_async_copy(source, spot, local_sems.at[i])
                pl.when(own)(stay.start)
                pl.when(jnp.logical_not(own))(copy.start)
                a2a[i].append((own, copy, stay))

    def collect_weights(i):
        for source in range(4):
            spot = stores[i].at[source, y, x]
            arrives = pltpu.make_async_remote_copy(
                src_ref=spot,
                dst_ref=spot,
                send_sem=a2a_send.at[0],
                recv_sem=a2a_recv.at[4 * i + source],
                device_id=sibling,
                device_id_type=MESH,
            )
            own = (zh == source) & (c == zh // 2)
            pl.when(jnp.logical_not(own))(arrives.wait_recv)
        for own, copy, stay in a2a[i]:
            pl.when(own)(stay.wait)

    wy, wy_far, wx, forwards = {}, {}, {}, {0: [], 1: []}

    def along_y(i):
        mine = stores[i].at[:, y, x]
        wy[i] = same(mine, y_next), same(mine, y_prev)

    def forward_y(i, side):
        wy[i][side].wait_recv()
        spot = stores[i].at[pl.ds(2 * side, 2), ys[3 - 2 * side], x]
        wy_far[i, side] = same(spot, (y_next, y_prev)[side])

    def along_x(i, k):
        piece = stores[i].at[:, ys[k], x]
        wx[i, k] = same(piece, x_next), same(piece, x_prev)

    def far_y(i):
        wy_far[i, 0].wait_recv()
        wy_far[i, 1].wait_recv()
        along_x(i, 2)

    def forward_x(i, k, side):
        wx[i, k][side].wait_recv()
        spot = stores[i].at[pl.ds(2 * side, 2), ys[k], xs[3 - 2 * side]]
        forwards[i].append(same(spot, (x_next, x_prev)[side]))

    chunks_right = (pl.ds(0, 16), pl.ds(16, 32))
    chunks_left = (pl.ds(32, 16), pl.ds(0, 32))
    to_right, to_left, to_sibling, own_row = {}, {}, {k: [] for k in range(4)}, []

    def far_spot(q, h, hop):
        if h == 0:
            return rows.at[q, c, pl.ds(0, 16) if hop == 7 else pl.ds(32, 16)]
        return rows.at[q, c, pl.ds(16, 16), pl.ds(0 if hop == 7 else 2048, 2048)]

    def ring_start(h):
        to_right[0, h] = same(rows.at[p, c, chunks_right[h]], right)
        to_left[0, h] = same(rows.at[p, c, chunks_left[h]], left)

    def own_start():
        own_row.append(same(rows.at[p, c], sibling))

    def ring(step, h, side):
        to, chunks, target, hop = (
            (to_right, chunks_right, right, 7),
            (to_left, chunks_left, left, 1),
        )[side]
        to[step, h].wait_recv()
        q = (p + hop * (step + 1)) % 8
        spot = rows.at[q, c, chunks[h]] if step < 3 else far_spot(q, h, hop)
        if step < 2:
            to[step + 1, h] = same(spot, target)
        elif step == 2:
            to[3, h] = same(far_spot(q, h, hop), target)
        to_sibling[step].append(same(spot, sibling))

    metas = {}

    def meta_start():
        metas[0] = [
            cp.send(meta_own, meta.at[x, y, zh], device(x, y, (zh + k) % 4, zl, c))
            for k in (1, 2, 3)
        ]

    def meta_along_y():
        for copy in metas[0]:
            copy.wait_recv()
        mine = meta.at[x, y]
        metas[1] = [same(mine, target) for target in (y_next, y_far, y_prev)]

    def meta_along_x():
        for copy in metas[1]:
            copy.wait_recv()
        mine = meta.at[x]
        metas[2] = [same(mine, target) for target in (x_next, x_far, x_prev)]

    order = [zh, (zh + 3 + 2 * zl) % 4, (zh + 1 + 2 * zl) % 4, (zh + 2) % 4]

    def tables_of(zb):
        tile = meta[x, y, zb].astype(jnp.float32)
        upper = jnp.broadcast_to(tile[2:3], (128, 128)).T
        lower = jnp.broadcast_to(tile[3:4], (128, 128)).T
        angles = jnp.concatenate([upper, lower[:64]], axis=0) * inverse[...]
        attention_gain = 0.1 * math.log(yarn_factor) + 1.0
        lane = lax.broadcasted_iota(jnp.int32, (BLOCK, HEAD_SIZE), 1)
        sine = jnp.sin(angles) * attention_gain
        tables[0, zb] = jnp.cos(angles) * attention_gain
        tables[1, zb] = jnp.where(lane < HEAD_SIZE // 2, -sine, sine)

    def turn(head, cosine, sine):
        return head * cosine + pltpu.roll(head, HEAD_SIZE // 2, 1) * sine

    def multiply(zb, store, total):
        total[...] = jnp.zeros_like(total)

        @pl.loop(0, 4)
        def _(k):
            piece = store[k].reshape(1024, store.shape[-1])
            depth = pl.ds(pl.multiple_of(k * 1024, 1024), 1024)
            left_side = rows[pl.ds(2 * zb, 2), :, :, depth].reshape(BLOCK, 1024)
            total[...] += jnp.dot(left_side, piece, preferred_element_type=jnp.float32)

    q_stay = []

    def queries_of(s):
        zb = order[s]
        if not q_stay:
            for copy in forwards[0]:
                copy.wait_recv()
        multiply(zb, weights_q, q_sum)
        for h in range(2):
            at = pl.ds(h * HEAD_SIZE, HEAD_SIZE)
            q_own[s, :, at] = turn(q_sum[:, at], tables[0, zb], tables[1, zb]).astype(jnp.bfloat16)
        q_stay.append(pltpu.make_async_copy(q_own.at[s], q_out.at[zb], local_sems.at[5 + s]))
        q_stay[-1].start()

    halves = (pl.ds(0, 96), pl.ds(96, 96))
    cell = lambda s, i, k: both.at[c, xs[i], order[s], ys[k]]
    side_of = lambda s, i, k, f: both.at[c, xs[i], order[s], ys[k], halves[f]]
    kx, kx_far, ky, ky_far, kv_stay, siblings = {}, {}, {}, {}, [], []
    is_key = c == 0

    def key_start(s):
        zb = order[s]
        for copy in to_sibling[s] + (forwards[1] + own_row if s == 0 else []):
            copy.wait_recv()
        multiply(zb, weights_kv, product)
        cosine = jnp.where(is_key, tables[0, zb], 1.0)
        sine = jnp.where(is_key, tables[1, zb], 0.0)
        kv[s] = turn(product[...], cosine, sine).astype(jnp.bfloat16)
        own, spot = kv.at[s], cell(s, 0, 0)
        kx[s] = cp.send(own, spot, x_next), cp.send(own, spot, x_prev)
        ky[s, 0] = cp.send(own, spot, y_next), cp.send(own, spot, y_prev)
        siblings.append(cp.send(own, spot, sibling))
        kv_stay.append(pltpu.make_async_copy(own, spot, local_sems.at[9 + s]))
        kv_stay[-1].start()

    def key_along_y(s, i):
        ky[s, i] = same(cell(s, i, 0), y_next), same(cell(s, i, 0), y_prev)
        siblings.append(same(cell(s, i, 0), sibling))

    def key_x(s, side):
        kx[s][side].wait_recv()
        spot = side_of(s, 3 - 2 * side, 0, side)
        kx_far[s, side] = same(spot, (x_next, x_prev)[side])
        key_along_y(s, 3 - 2 * side)

    def key_x_far(s):
        kx_far[s, 0].wait_recv()
        kx_far[s, 1].wait_recv()
        key_along_y(s, 2)

    def key_y(s, i, side):
        ky[s, i][side].wait_recv()
        spot = side_of(s, i, 3 - 2 * side, side)
        ky_far[s, i, side] = same(spot, (y_next, y_prev)[side])

    def share(s, k):
        siblings.append(same(both.at[c, :, order[s], ys[k]], sibling))

    def key_end(s):
        for i in range(4):
            for side in range(2):
                ky_far[s, i, side].wait_recv()
        share(s, 2)

    scatter_weights(1)
    ring_start(1)
    own_start()
    ring_start(0)
    scatter_weights(0)
    collect_weights(1)
    along_x(1, 0)
    meta_start()
    along_y(1)
    forward_y(1, 0)
    ring(0, 0, 0)
    forward_y(1, 1)
    along_x(1, 3)
    ring(0, 1, 0)
    collect_weights(0)
    along_x(1, 1)
    along_y(0)
    far_y(1)
    ring(0, 0, 1)
    forward_x(1, 3, 1)
    ring(0, 1, 1)
    forward_x(1, 3, 0)
    forward_x(1, 1, 1)
    forward_x(1, 1, 0)
    forward_x(1, 0, 0)
    forward_x(1, 0, 1)
    forward_x(1, 2, 1)
    meta_along_y()
    forward_y(0, 0)
    forward_x(1, 2, 0)
    ring(1, 0, 0)
    along_x(0, 0)
    forward_y(0, 1)
    tables_of(order[0])
    key_start(0)
    along_x(0, 3)
    ring(1, 0, 1)
    ring(1, 1, 0)
    ring(1, 1, 1)
    tables_of(order[1])
    key_x(0, 1)
    along_x(0, 1)
    key_y(0, 0, 0)
    key_x(0, 0)
    key_start(1)
    key_x_far(0)
    forward_x(0, 3, 0)
    ring(2, 0, 0)
    ring(2, 1, 0)
    forward_x(0, 0, 1)
    key_y(0, 3, 1)
    tables_of(order[3])
    ring(2, 0, 1)
    key_y(0, 3, 0)
    key_x(1, 0)
    key_x(1, 1)
    forward_x(0, 0, 0)
    forward_x(0, 1, 1)
    tables_of(order[2])
    key_y(0, 0, 1)
    ring(2, 1, 1)
    key_y(1, 0, 1)
    key_y(0, 1, 0)
    far_y(0)
    key_x_far(1)
    key_start(2)
    key_y(1, 3, 0)
    ring(3, 0, 1)
    ring(3, 1, 0)
    key_y(0, 2, 0)
    key_y(1, 0, 0)
    key_y(1, 1, 0)
    key_y(0, 1, 1)
    forward_x(0, 1, 0)
    key_y(0, 2, 1)
    forward_x(0, 3, 1)
    key_y(1, 2, 1)
    ring(3, 1, 1)
    key_y(1, 1, 1)
    ring(3, 0, 0)
    key_y(1, 3, 1)
    forward_x(0, 2, 0)
    forward_x(0, 2, 1)
    key_y(1, 2, 0)
    key_x(2, 0)
    share(1, 3)
    share(0, 3)
    key_x(2, 1)
    share(1, 1)
    key_start(3)
    key_y(2, 0, 0)
    key_x_far(2)
    key_y(2, 0, 1)
    key_x(3, 1)
    key_x(3, 0)
    key_end(0)
    key_y(2, 3, 1)
    share(0, 1)
    key_y(2, 3, 0)
    key_end(1)
    queries_of(1)
    key_x_far(3)
    queries_of(0)
    key_y(3, 0, 0)
    key_y(3, 0, 1)
    key_y(2, 2, 0)
    key_y(2, 1, 1)
    key_y(2, 1, 0)
    share(2, 3)
    key_y(2, 2, 1)
    share(2, 1)
    key_y(3, 3, 1)
    key_y(3, 1, 0)
    key_y(3, 2, 0)
    key_y(3, 1, 1)
    key_y(3, 2, 1)
    key_y(3, 3, 0)
    share(3, 3)
    share(3, 1)
    meta_along_x()
    queries_of(2)
    key_end(2)
    queries_of(3)
    for copy in metas[2]:
        copy.wait_recv()
    everything = meta[...].reshape(64, 8, 128)
    line = lax.broadcasted_iota(jnp.int32, (8, 128), 0)
    firsts = []
    for d in range(1, 6):
        hits = jnp.sum(jnp.where(everything < d, 1, 0), axis=0)
        hits = jnp.where(line < 2, hits, 0).astype(jnp.float32)
        firsts.append(jnp.sum(jnp.sum(hits, axis=0, keepdims=True), axis=1, keepdims=True))
    for zb in range(4):
        documents = meta[x, y, zb][0:2]
        first = jnp.zeros((2, 128), jnp.float32)
        for d in range(1, 6):
            first = jnp.where(documents == d, firsts[d - 1], first)
        first_out[2 * zb : 2 * zb + 2, :] = first.astype(jnp.int32)
    key_end(3)
    for copy in siblings:
        copy.wait_recv()
    for copy in q_stay + kv_stay:
        copy.wait()
    for i in range(2):
        for own, copy, _ in a2a[i]:
            pl.when(jnp.logical_not(own))(copy.wait_send)
    cp.finish()
    assert cp.count == FRONT_COPIES, cp.count


def front(hidden, gain, w_query, w_key, w_value, doc_ids, positions, inverse):
    outside = pl.BlockSpec(memory_space=pltpu.HBM)
    inside = pl.BlockSpec(memory_space=pltpu.VMEM)
    return pl.pallas_call(
        front_kernel,
        out_shape=(
            jax.ShapeDtypeStruct((4, BLOCK, 2 * HEAD_SIZE), jnp.bfloat16),
            jax.ShapeDtypeStruct((2, 4, 4, 4, BLOCK, HEAD_SIZE), jnp.bfloat16),
            jax.ShapeDtypeStruct((8, 128), jnp.int32),
        ),
        in_specs=[outside] * 8,
        out_specs=(outside, outside, inside),
        scratch_shapes=[
            pltpu.VMEM((48, 4096), jnp.bfloat16),
            pltpu.VMEM((1, 4096), jnp.float32),
            pltpu.VMEM((1, BLOCK), jnp.int32),
            pltpu.VMEM((1, BLOCK), jnp.int32),
            pltpu.VMEM((1, HEAD_SIZE), jnp.float32),
            pltpu.VMEM((8, 2, 48, 4096), jnp.bfloat16),
            pltpu.VMEM((4, 4, 4, 64, 256), jnp.bfloat16),
            pltpu.VMEM((4, 4, 4, 64, 128), jnp.bfloat16),
            pltpu.VMEM((4, 4, 4, 8, 128), jnp.int32),
            pltpu.VMEM((8, 128), jnp.int32),
            pltpu.VMEM((2, 4, BLOCK, HEAD_SIZE), jnp.float32),
            pltpu.VMEM((BLOCK, HEAD_SIZE), jnp.float32),
            pltpu.VMEM((4, BLOCK, HEAD_SIZE), jnp.bfloat16),
            pltpu.VMEM((BLOCK, 2 * HEAD_SIZE), jnp.float32),
            pltpu.VMEM((4, BLOCK, 2 * HEAD_SIZE), jnp.bfloat16),
            pltpu.SemaphoreType.DMA((FRONT_COPIES,)),
            pltpu.SemaphoreType.DMA((FRONT_COPIES,)),
            pltpu.SemaphoreType.DMA((8,)),
            pltpu.SemaphoreType.DMA((8,)),
            pltpu.SemaphoreType.DMA((13,)),
        ],
        compiler_params=pltpu.CompilerParams(
            collective_id=0, has_side_effects=True, vmem_limit_bytes=55 << 20
        ),
        name="front",
    )(
        *(
            pltpu.with_memory_space_constraint(a, pltpu.HBM)
            for a in (hidden, gain, w_query, w_key, w_value, doc_ids, positions, inverse)
        )
    )


def attend_kernel(bounds, q_ref, both_in, first_ref, out_ref, even, odd, summed):
    both_ref = both_in.reshape(2, SEQUENCE, HEAD_SIZE)
    block = pl.program_id(0)
    t_low, t_clear, t_edge, t_high, row0 = (bounds[block, i] for i in range(5))
    scale = HEAD_SIZE ** (-0.5) * math.log2(math.e)
    width = 2 * BLOCK
    queries = jnp.concatenate([q_ref[0, :, :HEAD_SIZE], q_ref[0, :, HEAD_SIZE:]], axis=0)
    summed[...] = jnp.zeros_like(summed)

    half = KEY_TILE // 2

    def produce(store, begin, masked):
        peak = None
        for u in range(half // KEY_PIECE):
            first_key = begin + u * KEY_PIECE
            keys = both_ref[0, pl.ds(pl.multiple_of(first_key, KEY_PIECE), KEY_PIECE), :]
            piece = lax.dot_general(
                keys, queries, (((1,), (1,)), ((), ())), preferred_element_type=jnp.float32
            )
            if masked:
                key = first_key + lax.broadcasted_iota(jnp.int32, (KEY_PIECE, width), 0)
                lane = lax.broadcasted_iota(jnp.int32, (1, width), 1)
                query = row0 + jnp.where(lane < BLOCK, lane, lane - BLOCK)
                allowed = (key <= query) & (key >= first_ref[0])
                piece = jnp.where(allowed, piece, masked_score)
            store[u * KEY_PIECE : (u + 1) * KEY_PIECE, :] = piece
            top = jnp.max(piece.reshape(KEY_PIECE // 8, 8, width), axis=0)
            peak = top if peak is None else jnp.maximum(peak, top)
        return peak

    def consume(store, begin, peak, total, fresh):
        latest = jnp.maximum(peak, jnp.max(fresh, axis=0, keepdims=True))
        shrink = jnp.exp2((peak - latest) * scale)
        total = total * shrink
        offset = latest * scale
        gained = None
        for u in range(half // KEY_PIECE):
            weights = jnp.exp2(store[u * KEY_PIECE : (u + 1) * KEY_PIECE, :] * scale - offset)
            total = total + jnp.sum(weights.reshape(KEY_PIECE // 8, 8, width), axis=0)
            values = both_ref[1, pl.ds(pl.multiple_of(begin + u * KEY_PIECE, KEY_PIECE), KEY_PIECE), :]
            term = lax.dot_general(
                values, weights.astype(jnp.bfloat16), (((0,), (0,)), ((), ())),
                preferred_element_type=jnp.float32,
            )
            gained = term if gained is None else gained + term
        summed[...] = summed[...] * shrink + gained
        return latest, total

    def step(masked, t, carry):
        peak, total, fresh = carry
        begin = t * KEY_TILE
        following = produce(even, begin, masked)
        peak, total = consume(odd, begin - half, peak, total, fresh)
        fresh = produce(odd, begin + half, masked)
        peak, total = consume(even, begin, peak, total, following)
        return peak, total, fresh

    begin = t_low * KEY_TILE
    peak, total = jnp.full((1, width), masked_score, jnp.float32), jnp.zeros((8, width), jnp.float32)
    following = produce(even, begin, True)
    fresh = produce(odd, begin + half, True)
    peak, total = consume(even, begin, peak, total, following)
    carry = (peak, total, fresh)
    start = t_low + 1
    carry = lax.fori_loop(start, t_clear, functools.partial(step, True), carry)
    carry = lax.fori_loop(jnp.maximum(t_clear, start), t_edge, functools.partial(step, False), carry)
    carry = lax.fori_loop(jnp.maximum(t_edge, start), t_high, functools.partial(step, True), carry)
    peak, total = consume(odd, t_high * KEY_TILE - half, *carry)
    total = jnp.sum(total, axis=0, keepdims=True)
    result = (summed[...] / total).T
    out_ref[0, :, :HEAD_SIZE] = result[:BLOCK].astype(jnp.bfloat16)
    out_ref[0, :, HEAD_SIZE:] = result[BLOCK:].astype(jnp.bfloat16)


def attend(bounds, queries, both, first):
    return pl.pallas_call(
        attend_kernel,
        out_shape=jax.ShapeDtypeStruct((4, BLOCK, 2 * HEAD_SIZE), jnp.bfloat16),
        grid_spec=pltpu.PrefetchScalarGridSpec(
            num_scalar_prefetch=1,
            grid=(4,),
            in_specs=[
                pl.BlockSpec((1, BLOCK, 2 * HEAD_SIZE), lambda i, b: (i, 0, 0)),
                pl.BlockSpec(memory_space=pltpu.VMEM),
                pl.BlockSpec((1, 1, 2 * BLOCK), lambda i, b: (i, 0, 0)),
            ],
            out_specs=pl.BlockSpec((1, BLOCK, 2 * HEAD_SIZE), lambda i, b: (i, 0, 0)),
            scratch_shapes=[
                pltpu.VMEM((KEY_TILE // 2, 2 * BLOCK), jnp.float32),
                pltpu.VMEM((KEY_TILE // 2, 2 * BLOCK), jnp.float32),
                pltpu.VMEM((HEAD_SIZE, 2 * BLOCK), jnp.float32),
            ],
        ),
        compiler_params=pltpu.CompilerParams(vmem_limit_bytes=16 << 20),
        name="attend",
    )(bounds, queries, both, first)


def back_kernel(
    own, w_out, hidden, out,
    attended, weights, mine, given, landed, joined, arrived,
    send_sems, recv_sems, local_sems, step_send, step_recv,
):
    x, y, zh, zl, c = place()
    cz = zh // 2
    sibling, across = device(x, y, zh, zl, 1 - c), device(x, y, zh, 1 - zl, c)
    partners = [device(x, y, (zh + k) % 4, zl, cc) for k in range(4) for cc in (c, 1 - c)][1:]
    partners.append(across)
    pieces = 8
    width = 4096 // pieces
    cut = lambda i: pl.ds(i * width, width)
    fetch = [
        pltpu.make_async_copy(w_out.at[:, cut(i)], weights.at[:, cut(i)], local_sems.at[1 + i])
        for i in range(pieces)
    ]
    for copy in fetch:
        copy.start()
    greet(partners)
    spot = lambda j, cc: attended.at[:, pl.ds(pl.multiple_of((2 * j + cc) * 256, 256), 256)]
    copies = []
    here = cz == c
    for k in (2, 1, 3, 0):
        zt = (zh + k) % 4
        copy = pltpu.make_async_remote_copy(
            src_ref=own.at[zt],
            dst_ref=spot(zh % 2, c),
            send_sem=send_sems.at[k],
            recv_sem=recv_sems.at[(zh % 2) * 2 + c],
            device_id=device(x, y, zt, zl, cz),
            device_id_type=MESH,
        )
        if k == 0:
            stay = pltpu.make_async_copy(own.at[zt], spot(zh % 2, c), local_sems.at[0])
            pl.when(here)(stay.start)
            pl.when(jnp.logical_not(here))(copy.start)
        else:
            copy.start()
        copies.append(copy)
    for j in range(2):
        for cc in range(2):
            arrives = pltpu.make_async_remote_copy(
                src_ref=own.at[0],
                dst_ref=spot(j, cc),
                send_sem=send_sems.at[0],
                recv_sem=recv_sems.at[2 * j + cc],
                device_id=sibling,
                device_id_type=MESH,
            )
            local = (zh == 2 * c + j) & (c == cc)
            pl.when(jnp.logical_not(local))(arrives.wait_recv)
    pl.when(here)(stay.wait)

    cp = Copies(step_send, step_recv)
    to_sibling, to_across = [], []

    def pass_on(i):
        to_sibling[i].wait_recv()
        joined[i] = (mine[i, 1 - zl] + landed[i, 1 - zl].astype(jnp.float32)).astype(jnp.bfloat16)
        to_across.append(cp.send(joined.at[i], arrived.at[i], across))

    for i in range(pieces):
        fetch[i].wait()
        term = jnp.dot(attended[...], weights[:, cut(i)], preferred_element_type=jnp.float32)
        term = term.reshape(2, 2, 48, width)
        mine[i] = jnp.where(c == 0, term[:, 0], term[:, 1])
        given[i] = jnp.where(c == 0, term[:, 1], term[:, 0]).astype(jnp.bfloat16)
        to_sibling.append(cp.send(given.at[i], landed.at[i], sibling))
        if i > 0:
            pass_on(i - 1)
    pass_on(pieces - 1)
    for i in range(pieces):
        total = mine[i, zl] + landed[i, zl].astype(jnp.float32)
        to_across[i].wait_recv()
        total = total + arrived[i].astype(jnp.float32)
        out[:, cut(i)] = (hidden[:, cut(i)].astype(jnp.float32) + total).astype(jnp.bfloat16)
    pl.when(jnp.logical_not(here))(copies[-1].wait_send)
    for copy in copies[:-1]:
        copy.wait_send()
    cp.finish()


def back(own, w_out, hidden):
    anywhere = pl.BlockSpec(memory_space=pl.ANY)
    inside = pl.BlockSpec(memory_space=pltpu.VMEM)
    return pl.pallas_call(
        back_kernel,
        out_shape=jax.ShapeDtypeStruct((48, 4096), jnp.bfloat16),
        in_specs=[anywhere, anywhere, inside],
        out_specs=inside,
        scratch_shapes=[
            pltpu.VMEM((BLOCK, 1024), jnp.bfloat16),
            pltpu.VMEM((1024, 4096), jnp.bfloat16),
            pltpu.VMEM((8, 2, 48, 512), jnp.float32),
            pltpu.VMEM((8, 2, 48, 512), jnp.bfloat16),
            pltpu.VMEM((8, 2, 48, 512), jnp.bfloat16),
            pltpu.VMEM((8, 48, 512), jnp.bfloat16),
            pltpu.VMEM((8, 48, 512), jnp.bfloat16),
            pltpu.SemaphoreType.DMA((4,)),
            pltpu.SemaphoreType.DMA((4,)),
            pltpu.SemaphoreType.DMA((9,)),
            pltpu.SemaphoreType.DMA((16,)),
            pltpu.SemaphoreType.DMA((16,)),
        ],
        compiler_params=pltpu.CompilerParams(
            collective_id=1, has_side_effects=True, vmem_limit_bytes=32 << 20
        ),
        name="back",
    )(own, w_out, hidden)


def body(hidden_in, norm_gain, w_query, w_key, value_weight, w_out, doc_ids, positions):
    x, y, zh, zl, c = place()
    inverse = yarn_inverse(HEAD_SIZE)
    queries, both, first = front(
        hidden_in,
        norm_gain.reshape(1, 4096),
        w_query,
        w_key,
        value_weight,
        doc_ids.reshape(1, BLOCK),
        positions.reshape(1, BLOCK),
        jnp.asarray([inverse + inverse], dtype=jnp.float32),
    )
    first = first.reshape(4, 256)[:, :BLOCK]
    row0 = (x * 16 + jnp.arange(4, dtype=jnp.int32) * 4 + y) * BLOCK
    t_low = first[:, 0] // KEY_TILE
    t_edge = jnp.maximum((row0 + 1) // KEY_TILE, t_low)
    t_clear = jnp.clip((first[:, -1] + KEY_TILE - 1) // KEY_TILE, t_low, t_edge)
    t_high = (row0 + BLOCK - 1) // KEY_TILE + 1
    bounds = jnp.stack([t_low, t_clear, t_edge, t_high, row0], axis=1)
    lanes = jnp.concatenate([first, first], axis=1).reshape(4, 1, 2 * BLOCK)
    queries, both, w_out = (
        pltpu.with_memory_space_constraint(a, pltpu.HBM) for a in (queries, both, w_out)
    )
    attended = attend(bounds, queries, both, lanes)
    return back(attended, w_out, hidden_in)


def solution(mesh):
    in_specs = (
        P(("outer", "inner", "tensor"), None),
        P(),
        P("inner", "tensor"),
        P("inner", "tensor"),
        P("inner", "tensor"),
        P("tensor", None),
        P(("outer", "inner")),
        P(("outer", "inner")),
    )
    out_specs = P(("outer", "inner", "tensor"), None)
    return jax.shard_map(body, mesh=mesh, in_specs=in_specs, out_specs=out_specs, check_vma=False)
```

```python
import functools
import math

import jax
import jax.numpy as jnp
from jax import lax
from jax.experimental import pallas as pl
from jax.experimental.pallas import tpu as pltpu
from jax.sharding import PartitionSpec as P

HEAD_SIZE = 128
BLOCK = 192
SEQUENCE = 12288
KEY_TILE = 1536
KEY_PIECE = 256
MESH = pl.DeviceIdType.MESH
FRONT_COPIES = 190


rope_base = 500000.0
yarn_factor = 8.0
trained_context = 8192.0
beta_fast = 32.0
beta_slow = 1.0
norm_epsilon = 1e-05
masked_score = -1e30


def yarn_inverse(head_dim):
    half_dim = head_dim // 2

    def correction(rotations):
        return (
            head_dim
            * math.log(trained_context / (rotations * 2.0 * math.pi))
            / (2.0 * math.log(rope_base))
        )

    lowest = max(math.floor(correction(beta_fast)), 0)
    highest = min(math.ceil(correction(beta_slow)), head_dim - 1)
    spread = max(highest - lowest, 0.001)
    values = []
    for column in range(half_dim):
        extrapolated = rope_base ** (-2.0 * column / head_dim)
        ramp = min(max((column - lowest) / spread, 0.0), 1.0)
        values.append(extrapolated / yarn_factor * ramp + extrapolated * (1.0 - ramp))
    return values


def place():
    outer, inner, tensor = (lax.axis_index(name) for name in ("outer", "inner", "tensor"))
    return outer, inner % 4, inner // 4, tensor // 2, tensor % 2


def device(x, y, zh, zl, c):
    return (x, zh * 4 + y, zl * 2 + c)


def greet(partners):
    barrier = pltpu.get_barrier_semaphore()
    for partner in partners:
        pl.semaphore_signal(barrier, inc=1, device_id=partner, device_id_type=MESH)
    pl.semaphore_wait(barrier, len(partners))


class Copies:
    def __init__(self, send_sems, recv_sems):
        self.send_sems, self.recv_sems, self.count, self.sent = send_sems, recv_sems, 0, []

    def send(self, src, dst, target):
        copy = pltpu.make_async_remote_copy(
            src_ref=src,
            dst_ref=dst,
            send_sem=self.send_sems.at[self.count],
            recv_sem=self.recv_sems.at[self.count],
            device_id=target,
            device_id_type=MESH,
        )
        self.count += 1
        copy.start()
        self.sent.append(copy)
        return copy

    def finish(self):
        for copy in self.sent:
            copy.wait_send()


def front_kernel(
    hidden_in, gain_in, w_query, w_key, w_value, doc_ids_in, positions_in, inverse_in,
    q_out, both, first_out,
    hidden, gain, doc_ids, positions, inverse, rows, weights_q, weights_kv,
    meta, meta_own, tables, product, kv, q_sum, q_own,
    send_sems, recv_sems, a2a_send, a2a_recv, local_sems,
):
    x, y, zh, zl, c = place()
    p = zh * 2 + zl
    near = lambda q: device(x, y, (q % 8) // 2, q % 2, c)
    right, left = near(p + 1), near(p + 7)
    sibling = device(x, y, zh, zl, 1 - c)
    xs = [(x + k) % 4 for k in range(4)]
    ys = [(y + k) % 4 for k in range(4)]
    y_next, y_far, y_prev = (device(x, ys[k], zh, zl, c) for k in (1, 2, 3))
    x_next, x_far, x_prev = (device(xs[k], y, zh, zl, c) for k in (1, 2, 3))
    columns = [device(x, y, (zh + k) % 4, zl, cc) for k in range(4) for cc in (c, 1 - c)][1:]
    partners = columns + [right, left, y_next, y_prev, y_far, x_next, x_prev, x_far]
    barrier = pltpu.get_barrier_semaphore()
    for partner in partners:
        pl.semaphore_signal(barrier, inc=1, device_id=partner, device_id_type=MESH)
    cp = Copies(send_sems, recv_sems)
    same = lambda ref, target: cp.send(ref, ref, target)
    fetches = [
        pltpu.make_async_copy(source, target, local_sems.at[i])
        for i, (source, target) in enumerate(
            (
                (doc_ids_in, doc_ids),
                (positions_in, positions),
                (hidden_in, hidden),
                (gain_in, gain),
                (inverse_in, inverse),
            )
        )
    ]
    for copy in fetches:
        copy.start()
    fetches[0].wait()
    fetches[1].wait()

    meta_own[...] = jnp.full((8, 128), 99, jnp.int32)
    meta_own[0:1, :] = doc_ids[:, :128]
    meta_own[1:2, :64] = doc_ids[:, 128:]
    meta_own[2:3, :] = positions[:, :128]
    meta_own[3:4, :64] = positions[:, 128:]
    meta[x, y, zh] = meta_own[...]
    for copy in fetches[2:]:
        copy.wait()
    widened = hidden[...].astype(jnp.float32)
    power = jnp.mean(widened * widened, axis=-1, keepdims=True)
    rows[p, c] = (widened * lax.rsqrt(power + norm_epsilon) * gain[...]).astype(jnp.bfloat16)
    pl.semaphore_wait(barrier, len(partners))

    a2a = {0: [], 1: []}
    stores = (weights_q, weights_kv)

    def scatter_weights(i):
        for j in range(2):
            for cc in range(2):
                zt = 2 * c + j
                own = (zt == zh) & (c == cc)
                taken = pl.ds(pl.multiple_of(x * 64, 64), 64)
                if i == 0:
                    source = w_query.at[taken, pl.ds(j * 512 + cc * 256, 256)]
                else:
                    source = (w_value if cc else w_key).at[taken, pl.ds(j * 128, 128)]
                spot = stores[i].at[zh, y, x]
                copy = pltpu.make_async_remote_copy(
                    src_ref=source,
                    dst_ref=spot,
                    send_sem=a2a_send.at[4 * i + 2 * j + cc],
                    recv_sem=a2a_recv.at[4 * i + zh],
                    device_id=device(x, y, zt, zl, cc),
                    device_id_type=MESH,
                )
                stay = pltpu.make_async_copy(source, spot, local_sems.at[i])
                pl.when(own)(stay.start)
                pl.when(jnp.logical_not(own))(copy.start)
                a2a[i].append((own, copy, stay))

    def collect_weights(i):
        for source in range(4):
            spot = stores[i].at[source, y, x]
            arrives = pltpu.make_async_remote_copy(
                src_ref=spot,
                dst_ref=spot,
                send_sem=a2a_send.at[0],
                recv_sem=a2a_recv.at[4 * i + source],
                device_id=sibling,
                device_id_type=MESH,
            )
            own = (zh == source) & (c == zh // 2)
            pl.when(jnp.logical_not(own))(arrives.wait_recv)
        for own, copy, stay in a2a[i]:
            pl.when(own)(stay.wait)

    wy, wy_far, wx, forwards = {}, {}, {}, {0: [], 1: []}

    def along_y(i):
        mine = stores[i].at[:, y, x]
        wy[i] = same(mine, y_next), same(mine, y_prev)

    def forward_y(i, side):
        wy[i][side].wait_recv()
        spot = stores[i].at[pl.ds(2 * side, 2), ys[3 - 2 * side], x]
        wy_far[i, side] = same(spot, (y_next, y_prev)[side])

    def along_x(i, k):
        piece = stores[i].at[:, ys[k], x]
        wx[i, k] = same(piece, x_next), same(piece, x_prev)

    def far_y(i):
        wy_far[i, 0].wait_recv()
        wy_far[i, 1].wait_recv()
        along_x(i, 2)

    def forward_x(i, k, side):
        wx[i, k][side].wait_recv()
        spot = stores[i].at[pl.ds(2 * side, 2), ys[k], xs[3 - 2 * side]]
        forwards[i].append(same(spot, (x_next, x_prev)[side]))

    chunks_right = (pl.ds(0, 16), pl.ds(16, 32))
    chunks_left = (pl.ds(32, 16), pl.ds(0, 32))
    to_right, to_left, to_sibling, own_row = {}, {}, {k: [] for k in range(4)}, []

    def far_spot(q, h, hop):
        if h == 0:
            return rows.at[q, c, pl.ds(0, 16) if hop == 7 else pl.ds(32, 16)]
        return rows.at[q, c, pl.ds(16, 16), pl.ds(0 if hop == 7 else 2048, 2048)]

    def ring_start(h):
        to_right[0, h] = same(rows.at[p, c, chunks_right[h]], right)
        to_left[0, h] = same(rows.at[p, c, chunks_left[h]], left)

    def own_start():
        own_row.append(same(rows.at[p, c], sibling))

    def ring(step, h, side):
        to, chunks, target, hop = (
            (to_right, chunks_right, right, 7),
            (to_left, chunks_left, left, 1),
        )[side]
        to[step, h].wait_recv()
        q = (p + hop * (step + 1)) % 8
        spot = rows.at[q, c, chunks[h]] if step < 3 else far_spot(q, h, hop)
        if step < 2:
            to[step + 1, h] = same(spot, target)
        elif step == 2:
            to[3, h] = same(far_spot(q, h, hop), target)
        to_sibling[step].append(same(spot, sibling))

    metas = {}

    def meta_start():
        metas[0] = [
            cp.send(meta_own, meta.at[x, y, zh], device(x, y, (zh + k) % 4, zl, c))
            for k in (1, 2, 3)
        ]

    def meta_along_y():
        for copy in metas[0]:
            copy.wait_recv()
        mine = meta.at[x, y]
        metas[1] = [same(mine, target) for target in (y_next, y_far, y_prev)]

    def meta_along_x():
        for copy in metas[1]:
            copy.wait_recv()
        mine = meta.at[x]
        metas[2] = [same(mine, target) for target in (x_next, x_far, x_prev)]

    order = [zh, (zh + 3 + 2 * zl) % 4, (zh + 1 + 2 * zl) % 4, (zh + 2) % 4]

    def tables_of(zb):
        tile = meta[x, y, zb].astype(jnp.float32)
        upper = jnp.broadcast_to(tile[2:3], (128, 128)).T
        lower = jnp.broadcast_to(tile[3:4], (128, 128)).T
        angles = jnp.concatenate([upper, lower[:64]], axis=0) * inverse[...]
        attention_gain = 0.1 * math.log(yarn_factor) + 1.0
        lane = lax.broadcasted_iota(jnp.int32, (BLOCK, HEAD_SIZE), 1)
        sine = jnp.sin(angles) * attention_gain
        tables[0, zb] = jnp.cos(angles) * attention_gain
        tables[1, zb] = jnp.where(lane < HEAD_SIZE // 2, -sine, sine)

    def turn(head, cosine, sine):
        return head * cosine + pltpu.roll(head, HEAD_SIZE // 2, 1) * sine

    def multiply(zb, store, total):
        total[...] = jnp.zeros_like(total)

        @pl.loop(0, 4)
        def _(k):
            piece = store[k].reshape(1024, store.shape[-1])
            depth = pl.ds(pl.multiple_of(k * 1024, 1024), 1024)
            left_side = rows[pl.ds(2 * zb, 2), :, :, depth].reshape(BLOCK, 1024)
            total[...] += jnp.dot(left_side, piece, preferred_element_type=jnp.float32)

    q_stay = []

    def queries_of(s):
        zb = order[s]
        if not q_stay:
            for copy in forwards[0]:
                copy.wait_recv()
        multiply(zb, weights_q, q_sum)
        for h in range(2):
            at = pl.ds(h * HEAD_SIZE, HEAD_SIZE)
            q_own[s, :, at] = turn(q_sum[:, at], tables[0, zb], tables[1, zb]).astype(jnp.bfloat16)
        q_stay.append(pltpu.make_async_copy(q_own.at[s], q_out.at[zb], local_sems.at[5 + s]))
        q_stay[-1].start()

    halves = (pl.ds(0, 96), pl.ds(96, 96))
    cell = lambda s, i, k: both.at[c, xs[i], order[s], ys[k]]
    side_of = lambda s, i, k, f: both.at[c, xs[i], order[s], ys[k], halves[f]]
    kx, kx_far, ky, ky_far, kv_stay, siblings = {}, {}, {}, {}, [], []
    is_key = c == 0

    def key_start(s):
        zb = order[s]
        for copy in to_sibling[s] + (forwards[1] + own_row if s == 0 else []):
            copy.wait_recv()
        multiply(zb, weights_kv, product)
        cosine = jnp.where(is_key, tables[0, zb], 1.0)
        sine = jnp.where(is_key, tables[1, zb], 0.0)
        kv[s] = turn(product[...], cosine, sine).astype(jnp.bfloat16)
        own, spot = kv.at[s], cell(s, 0, 0)
        kx[s] = cp.send(own, spot, x_next), cp.send(own, spot, x_prev)
        ky[s, 0] = cp.send(own, spot, y_next), cp.send(own, spot, y_prev)
        siblings.append(cp.send(own, spot, sibling))
        kv_stay.append(pltpu.make_async_copy(own, spot, local_sems.at[9 + s]))
        kv_stay[-1].start()

    def key_along_y(s, i):
        ky[s, i] = same(cell(s, i, 0), y_next), same(cell(s, i, 0), y_prev)
        siblings.append(same(cell(s, i, 0), sibling))

    def key_x(s, side):
        kx[s][side].wait_recv()
        spot = side_of(s, 3 - 2 * side, 0, side)
        kx_far[s, side] = same(spot, (x_next, x_prev)[side])
        key_along_y(s, 3 - 2 * side)

    def key_x_far(s):
        kx_far[s, 0].wait_recv()
        kx_far[s, 1].wait_recv()
        key_along_y(s, 2)

    def key_y(s, i, side):
        ky[s, i][side].wait_recv()
        spot = side_of(s, i, 3 - 2 * side, side)
        ky_far[s, i, side] = same(spot, (y_next, y_prev)[side])

    def share(s, k):
        siblings.append(same(both.at[c, :, order[s], ys[k]], sibling))

    def key_end(s):
        for i in range(4):
            for side in range(2):
                ky_far[s, i, side].wait_recv()
        share(s, 2)

    scatter_weights(1)
    meta_start()
    scatter_weights(0)
    ring_start(1)
    collect_weights(1)
    along_y(1)
    along_x(1, 0)
    ring_start(0)
    forward_y(1, 0)
    forward_y(1, 1)
    along_x(1, 3)
    collect_weights(0)
    ring(0, 1, 0)
    along_x(1, 1)
    along_y(0)
    far_y(1)
    own_start()
    along_x(0, 0)
    ring(0, 1, 1)
    forward_x(1, 1, 0)
    forward_x(1, 3, 1)
    ring(0, 0, 0)
    ring(0, 0, 1)
    forward_x(1, 3, 0)
    meta_along_y()
    forward_x(1, 0, 1)
    forward_x(1, 1, 1)
    forward_y(0, 1)
    forward_y(0, 0)
    forward_x(1, 2, 1)
    tables_of(order[0])
    forward_x(1, 2, 0)
    tables_of(order[1])
    forward_x(1, 0, 0)
    along_x(0, 1)
    ring(1, 1, 0)
    far_y(0)
    ring(1, 1, 1)
    key_start(0)
    tables_of(order[2])
    ring(1, 0, 0)
    ring(1, 0, 1)
    along_x(0, 3)
    key_x(0, 0)
    key_x(0, 1)
    tables_of(order[3])
    forward_x(0, 1, 1)
    ring(2, 1, 0)
    key_start(1)
    ring(2, 0, 0)
    key_y(0, 0, 1)
    ring(2, 1, 1)
    forward_x(0, 2, 1)
    key_y(0, 0, 0)
    key_x_far(0)
    ring(3, 1, 0)
    key_y(0, 1, 0)
    key_y(0, 3, 0)
    key_y(0, 3, 1)
    forward_x(0, 1, 0)
    forward_x(0, 2, 0)
    key_y(1, 0, 1)
    key_y(0, 1, 1)
    key_x(1, 0)
    ring(2, 0, 1)
    key_x(1, 1)
    key_y(1, 0, 0)
    ring(3, 0, 0)
    key_y(0, 2, 1)
    ring(3, 1, 1)
    key_start(2)
    forward_x(0, 0, 1)
    forward_x(0, 0, 0)
    forward_x(0, 3, 1)
    key_y(0, 2, 0)
    key_y(1, 1, 0)
    key_y(1, 3, 1)
    key_x_far(1)
    ring(3, 0, 1)
    key_x(2, 0)
    key_x(2, 1)
    share(0, 3)
    key_y(1, 3, 0)
    forward_x(0, 3, 0)
    share(0, 1)
    key_start(3)
    key_y(1, 2, 1)
    key_x_far(2)
    key_y(1, 1, 1)
    key_y(1, 2, 0)
    queries_of(3)
    key_x(3, 1)
    key_y(2, 3, 0)
    key_y(2, 1, 0)
    share(1, 3)
    key_end(0)
    key_x(3, 0)
    key_y(2, 2, 1)
    share(1, 1)
    key_x_far(3)
    key_y(2, 3, 1)
    key_y(2, 2, 0)
    key_y(2, 0, 1)
    key_y(2, 0, 0)
    key_end(1)
    key_y(3, 0, 1)
    key_y(2, 1, 1)
    queries_of(0)
    key_y(3, 0, 0)
    share(2, 3)
    share(2, 1)
    key_y(3, 3, 0)
    key_y(3, 3, 1)
    key_y(3, 1, 1)
    key_y(3, 1, 0)
    meta_along_x()
    key_y(3, 2, 0)
    share(3, 3)
    key_y(3, 2, 1)
    share(3, 1)
    queries_of(2)
    key_end(2)
    queries_of(1)
    for copy in metas[2]:
        copy.wait_recv()
    everything = meta[...].reshape(64, 8, 128)
    line = lax.broadcasted_iota(jnp.int32, (8, 128), 0)
    firsts = []
    for d in range(1, 6):
        hits = jnp.sum(jnp.where(everything < d, 1, 0), axis=0)
        hits = jnp.where(line < 2, hits, 0).astype(jnp.float32)
        firsts.append(jnp.sum(jnp.sum(hits, axis=0, keepdims=True), axis=1, keepdims=True))
    for zb in range(4):
        documents = meta[x, y, zb][0:2]
        first = jnp.zeros((2, 128), jnp.float32)
        for d in range(1, 6):
            first = jnp.where(documents == d, firsts[d - 1], first)
        first_out[2 * zb : 2 * zb + 2, :] = first.astype(jnp.int32)
    key_end(3)
    for copy in siblings:
        copy.wait_recv()
    for copy in q_stay + kv_stay:
        copy.wait()
    for i in range(2):
        for own, copy, _ in a2a[i]:
            pl.when(jnp.logical_not(own))(copy.wait_send)
    cp.finish()
    assert cp.count == FRONT_COPIES, cp.count


def front(hidden, gain, w_query, w_key, w_value, doc_ids, positions, inverse):
    outside = pl.BlockSpec(memory_space=pltpu.HBM)
    inside = pl.BlockSpec(memory_space=pltpu.VMEM)
    return pl.pallas_call(
        front_kernel,
        out_shape=(
            jax.ShapeDtypeStruct((4, BLOCK, 2 * HEAD_SIZE), jnp.bfloat16),
            jax.ShapeDtypeStruct((2, 4, 4, 4, BLOCK, HEAD_SIZE), jnp.bfloat16),
            jax.ShapeDtypeStruct((8, 128), jnp.int32),
        ),
        in_specs=[outside] * 8,
        out_specs=(outside, outside, inside),
        scratch_shapes=[
            pltpu.VMEM((48, 4096), jnp.bfloat16),
            pltpu.VMEM((1, 4096), jnp.float32),
            pltpu.VMEM((1, BLOCK), jnp.int32),
            pltpu.VMEM((1, BLOCK), jnp.int32),
            pltpu.VMEM((1, HEAD_SIZE), jnp.float32),
            pltpu.VMEM((8, 2, 48, 4096), jnp.bfloat16),
            pltpu.VMEM((4, 4, 4, 64, 256), jnp.bfloat16),
            pltpu.VMEM((4, 4, 4, 64, 128), jnp.bfloat16),
            pltpu.VMEM((4, 4, 4, 8, 128), jnp.int32),
            pltpu.VMEM((8, 128), jnp.int32),
            pltpu.VMEM((2, 4, BLOCK, HEAD_SIZE), jnp.float32),
            pltpu.VMEM((BLOCK, HEAD_SIZE), jnp.float32),
            pltpu.VMEM((4, BLOCK, HEAD_SIZE), jnp.bfloat16),
            pltpu.VMEM((BLOCK, 2 * HEAD_SIZE), jnp.float32),
            pltpu.VMEM((4, BLOCK, 2 * HEAD_SIZE), jnp.bfloat16),
            pltpu.SemaphoreType.DMA((FRONT_COPIES,)),
            pltpu.SemaphoreType.DMA((FRONT_COPIES,)),
            pltpu.SemaphoreType.DMA((8,)),
            pltpu.SemaphoreType.DMA((8,)),
            pltpu.SemaphoreType.DMA((13,)),
        ],
        compiler_params=pltpu.CompilerParams(
            collective_id=0, has_side_effects=True, vmem_limit_bytes=55 << 20
        ),
        name="front",
    )(
        *(
            pltpu.with_memory_space_constraint(a, pltpu.HBM)
            for a in (hidden, gain, w_query, w_key, w_value, doc_ids, positions, inverse)
        )
    )


def attend_kernel(bounds, q_ref, both_in, first_ref, out_ref, even, odd, summed):
    both_ref = both_in.reshape(2, SEQUENCE, HEAD_SIZE)
    block = pl.program_id(0)
    t_low, t_clear, t_edge, t_high, row0 = (bounds[block, i] for i in range(5))
    scale = HEAD_SIZE ** (-0.5) * math.log2(math.e)
    width = 2 * BLOCK
    queries = jnp.concatenate([q_ref[0, :, :HEAD_SIZE], q_ref[0, :, HEAD_SIZE:]], axis=0)
    summed[...] = jnp.zeros_like(summed)

    half = KEY_TILE // 2

    def produce(store, begin, masked):
        peak = None
        for u in range(half // KEY_PIECE):
            first_key = begin + u * KEY_PIECE
            keys = both_ref[0, pl.ds(pl.multiple_of(first_key, KEY_PIECE), KEY_PIECE), :]
            piece = lax.dot_general(
                keys, queries, (((1,), (1,)), ((), ())), preferred_element_type=jnp.float32
            )
            if masked:
                key = first_key + lax.broadcasted_iota(jnp.int32, (KEY_PIECE, width), 0)
                lane = lax.broadcasted_iota(jnp.int32, (1, width), 1)
                query = row0 + jnp.where(lane < BLOCK, lane, lane - BLOCK)
                allowed = (key <= query) & (key >= first_ref[0])
                piece = jnp.where(allowed, piece, masked_score)
            store[u * KEY_PIECE : (u + 1) * KEY_PIECE, :] = piece
            top = jnp.max(piece.reshape(KEY_PIECE // 8, 8, width), axis=0)
            peak = top if peak is None else jnp.maximum(peak, top)
        return peak

    def consume(store, begin, peak, total, fresh):
        latest = jnp.maximum(peak, jnp.max(fresh, axis=0, keepdims=True))
        shrink = jnp.exp2((peak - latest) * scale)
        total = total * shrink
        offset = latest * scale
        gained = None
        for u in range(half // KEY_PIECE):
            weights = jnp.exp2(store[u * KEY_PIECE : (u + 1) * KEY_PIECE, :] * scale - offset)
            total = total + jnp.sum(weights.reshape(KEY_PIECE // 8, 8, width), axis=0)
            values = both_ref[1, pl.ds(pl.multiple_of(begin + u * KEY_PIECE, KEY_PIECE), KEY_PIECE), :]
            term = lax.dot_general(
                values, weights.astype(jnp.bfloat16), (((0,), (0,)), ((), ())),
                preferred_element_type=jnp.float32,
            )
            gained = term if gained is None else gained + term
        summed[...] = summed[...] * shrink + gained
        return latest, total

    def step(masked, t, carry):
        peak, total, fresh = carry
        begin = t * KEY_TILE
        following = produce(even, begin, masked)
        peak, total = consume(odd, begin - half, peak, total, fresh)
        fresh = produce(odd, begin + half, masked)
        peak, total = consume(even, begin, peak, total, following)
        return peak, total, fresh

    begin = t_low * KEY_TILE
    peak, total = jnp.full((1, width), masked_score, jnp.float32), jnp.zeros((8, width), jnp.float32)
    following = produce(even, begin, True)
    fresh = produce(odd, begin + half, True)
    peak, total = consume(even, begin, peak, total, following)
    carry = (peak, total, fresh)
    start = t_low + 1
    carry = lax.fori_loop(start, t_clear, functools.partial(step, True), carry)
    carry = lax.fori_loop(jnp.maximum(t_clear, start), t_edge, functools.partial(step, False), carry)
    carry = lax.fori_loop(jnp.maximum(t_edge, start), t_high, functools.partial(step, True), carry)
    peak, total = consume(odd, t_high * KEY_TILE - half, *carry)
    total = jnp.sum(total, axis=0, keepdims=True)
    result = (summed[...] / total).T
    out_ref[0, :, :HEAD_SIZE] = result[:BLOCK].astype(jnp.bfloat16)
    out_ref[0, :, HEAD_SIZE:] = result[BLOCK:].astype(jnp.bfloat16)


def attend(bounds, queries, both, first):
    return pl.pallas_call(
        attend_kernel,
        out_shape=jax.ShapeDtypeStruct((4, BLOCK, 2 * HEAD_SIZE), jnp.bfloat16),
        grid_spec=pltpu.PrefetchScalarGridSpec(
            num_scalar_prefetch=1,
            grid=(4,),
            in_specs=[
                pl.BlockSpec((1, BLOCK, 2 * HEAD_SIZE), lambda i, b: (i, 0, 0)),
                pl.BlockSpec(memory_space=pltpu.VMEM),
                pl.BlockSpec((1, 1, 2 * BLOCK), lambda i, b: (i, 0, 0)),
            ],
            out_specs=pl.BlockSpec((1, BLOCK, 2 * HEAD_SIZE), lambda i, b: (i, 0, 0)),
            scratch_shapes=[
                pltpu.VMEM((KEY_TILE // 2, 2 * BLOCK), jnp.float32),
                pltpu.VMEM((KEY_TILE // 2, 2 * BLOCK), jnp.float32),
                pltpu.VMEM((HEAD_SIZE, 2 * BLOCK), jnp.float32),
            ],
        ),
        compiler_params=pltpu.CompilerParams(vmem_limit_bytes=16 << 20),
        name="attend",
    )(bounds, queries, both, first)


def back_kernel(
    own, w_out, hidden, out,
    attended, weights, mine, given, landed, joined, arrived,
    send_sems, recv_sems, local_sems, step_send, step_recv,
):
    x, y, zh, zl, c = place()
    cz = zh // 2
    sibling, across = device(x, y, zh, zl, 1 - c), device(x, y, zh, 1 - zl, c)
    partners = [device(x, y, (zh + k) % 4, zl, cc) for k in range(4) for cc in (c, 1 - c)][1:]
    partners.append(across)
    pieces = 4
    width = 4096 // pieces
    cut = lambda i: pl.ds(i * width, width)
    fetch = [
        pltpu.make_async_copy(w_out.at[:, cut(i)], weights.at[:, cut(i)], local_sems.at[1 + i])
        for i in range(pieces)
    ]
    for copy in fetch:
        copy.start()
    greet(partners)
    spot = lambda j, cc: attended.at[:, pl.ds(pl.multiple_of((2 * j + cc) * 256, 256), 256)]
    copies = []
    here = cz == c
    for k in (2, 1, 3, 0):
        zt = (zh + k) % 4
        copy = pltpu.make_async_remote_copy(
            src_ref=own.at[zt],
            dst_ref=spot(zh % 2, c),
            send_sem=send_sems.at[k],
            recv_sem=recv_sems.at[(zh % 2) * 2 + c],
            device_id=device(x, y, zt, zl, cz),
            device_id_type=MESH,
        )
        if k == 0:
            stay = pltpu.make_async_copy(own.at[zt], spot(zh % 2, c), local_sems.at[0])
            pl.when(here)(stay.start)
            pl.when(jnp.logical_not(here))(copy.start)
        else:
            copy.start()
        copies.append(copy)
    for j in range(2):
        for cc in range(2):
            arrives = pltpu.make_async_remote_copy(
                src_ref=own.at[0],
                dst_ref=spot(j, cc),
                send_sem=send_sems.at[0],
                recv_sem=recv_sems.at[2 * j + cc],
                device_id=sibling,
                device_id_type=MESH,
            )
            local = (zh == 2 * c + j) & (c == cc)
            pl.when(jnp.logical_not(local))(arrives.wait_recv)
    pl.when(here)(stay.wait)

    cp = Copies(step_send, step_recv)
    to_sibling, to_across = [], []

    def pass_on(i):
        to_sibling[i].wait_recv()
        joined[i] = (mine[i, 1 - zl] + landed[i, 1 - zl].astype(jnp.float32)).astype(jnp.bfloat16)
        to_across.append(cp.send(joined.at[i], arrived.at[i], across))

    for i in range(pieces):
        fetch[i].wait()
        term = jnp.dot(attended[...], weights[:, cut(i)], preferred_element_type=jnp.float32)
        term = term.reshape(2, 2, 48, width)
        mine[i] = jnp.where(c == 0, term[:, 0], term[:, 1])
        given[i] = jnp.where(c == 0, term[:, 1], term[:, 0]).astype(jnp.bfloat16)
        to_sibling.append(cp.send(given.at[i], landed.at[i], sibling))
        if i > 0:
            pass_on(i - 1)
    pass_on(pieces - 1)
    for i in range(pieces):
        total = mine[i, zl] + landed[i, zl].astype(jnp.float32)
        to_across[i].wait_recv()
        total = total + arrived[i].astype(jnp.float32)
        out[:, cut(i)] = (hidden[:, cut(i)].astype(jnp.float32) + total).astype(jnp.bfloat16)
    pl.when(jnp.logical_not(here))(copies[-1].wait_send)
    for copy in copies[:-1]:
        copy.wait_send()
    cp.finish()


def back(own, w_out, hidden):
    anywhere = pl.BlockSpec(memory_space=pl.ANY)
    inside = pl.BlockSpec(memory_space=pltpu.VMEM)
    return pl.pallas_call(
        back_kernel,
        out_shape=jax.ShapeDtypeStruct((48, 4096), jnp.bfloat16),
        in_specs=[anywhere, anywhere, inside],
        out_specs=inside,
        scratch_shapes=[
            pltpu.VMEM((BLOCK, 1024), jnp.bfloat16),
            pltpu.VMEM((1024, 4096), jnp.bfloat16),
            pltpu.VMEM((4, 2, 48, 1024), jnp.float32),
            pltpu.VMEM((4, 2, 48, 1024), jnp.bfloat16),
            pltpu.VMEM((4, 2, 48, 1024), jnp.bfloat16),
            pltpu.VMEM((4, 48, 1024), jnp.bfloat16),
            pltpu.VMEM((4, 48, 1024), jnp.bfloat16),
            pltpu.SemaphoreType.DMA((4,)),
            pltpu.SemaphoreType.DMA((4,)),
            pltpu.SemaphoreType.DMA((5,)),
            pltpu.SemaphoreType.DMA((8,)),
            pltpu.SemaphoreType.DMA((8,)),
        ],
        compiler_params=pltpu.CompilerParams(
            collective_id=1, has_side_effects=True, vmem_limit_bytes=32 << 20
        ),
        name="back",
    )(own, w_out, hidden)


def body(hidden_in, norm_gain, w_query, w_key, value_weight, w_out, doc_ids, positions):
    x, y, zh, zl, c = place()
    inverse = yarn_inverse(HEAD_SIZE)
    queries, both, first = front(
        hidden_in,
        norm_gain.reshape(1, 4096),
        w_query,
        w_key,
        value_weight,
        doc_ids.reshape(1, BLOCK),
        positions.reshape(1, BLOCK),
        jnp.asarray([inverse + inverse], dtype=jnp.float32),
    )
    first = first.reshape(4, 256)[:, :BLOCK]
    row0 = (x * 16 + jnp.arange(4, dtype=jnp.int32) * 4 + y) * BLOCK
    t_low = first[:, 0] // KEY_TILE
    t_edge = jnp.maximum((row0 + 1) // KEY_TILE, t_low)
    t_clear = jnp.clip((first[:, -1] + KEY_TILE - 1) // KEY_TILE, t_low, t_edge)
    t_high = (row0 + BLOCK - 1) // KEY_TILE + 1
    bounds = jnp.stack([t_low, t_clear, t_edge, t_high, row0], axis=1)
    lanes = jnp.concatenate([first, first], axis=1).reshape(4, 1, 2 * BLOCK)
    queries, both, w_out = (
        pltpu.with_memory_space_constraint(a, pltpu.HBM) for a in (queries, both, w_out)
    )
    attended = attend(bounds, queries, both, lanes)
    return back(attended, w_out, hidden_in)


def solution(mesh):
    in_specs = (
        P(("outer", "inner", "tensor"), None),
        P(),
        P("inner", "tensor"),
        P("inner", "tensor"),
        P("inner", "tensor"),
        P("tensor", None),
        P(("outer", "inner")),
        P(("outer", "inner")),
    )
    out_specs = P(("outer", "inner", "tensor"), None)
    return jax.shard_map(body, mesh=mesh, in_specs=in_specs, out_specs=out_specs, check_vma=False)
```
